32 devices in a mesh: dp: 8 (over y, x, core), tensor: 4 (over z).
Axes of the slice: x: 2, y: 2, z: 4, core: 2. Of those that a mesh axis runs over, the one named last changes fastest.
Arguments:
- block_input: bfloat16 [8, 3072, 768], P('dp', 'tensor'), may hold values from -6 to 6
- attention_gain: float32 [768], replicated, may hold values from 0.5 to 1.5
- qkv_weight: bfloat16 [3, 768, 768], P(None, None, 'tensor'), may hold values from -0.21875 to 0.21875
- proj_weight: bfloat16 [768, 768], P('tensor'), may hold values from -3.5 to 3.5
- moe_gain: float32 [768], replicated, may hold values from 0.5 to 1.5
- centroids: bfloat16 [4, 768], replicated, may hold values from -0.15625 to 0.15625
- expert_up: bfloat16 [4, 768, 3072], P(None, None, 'tensor'), may hold values from -0.21875 to 0.21875
- expert_down: bfloat16 [4, 3072, 768], P(None, 'tensor'), may hold values from -0.21875 to 0.21875
- out_grad: bfloat16 [8, 3072, 768], P('dp', 'tensor'), may hold values from -6 to 6
- routes: int32 [8, 3072, 1], P('dp'), may hold values from 0 to 3
- priority: int32 [8, 3072], P('dp'), may hold values from 0 to 3071, each once within a row
- segments: int32 [8, 3072], P('dp'), may hold values from 0 to 8, as said below
Outputs:
- block_output: bfloat16 [8, 3072, 768], P('dp', 'tensor')
- input_grad: bfloat16 [8, 3072, 768], P('dp', 'tensor')
- attention_gain_grad: float32 [768], P(('dp', 'tensor'))
- moe_gain_grad: float32 [768], P(('dp', 'tensor'))
- centroid_grad: float32 [4, 768], P(None, ('dp', 'tensor'))
- qkv_grad: float32 [3, 768, 768], P(None, 'dp', 'tensor')
- proj_grad: float32 [768, 768], P('tensor', 'dp')
- expert_up_grad: float32 [4, 768, 3072], P(None, 'dp', 'tensor')
- expert_down_grad: float32 [4, 3072, 768], P(None, 'tensor', 'dp')
The draws below stay inside these ranges and needn't reach their ends.
Inputs may be any that keep to these rules, and one draw needn't show every extreme that they name: `segments`: along each group's row the ids never fall and start at 0; the prompt (id 0) holds 1024 tokens or more, and every continuation id 1 to 8 holds at least one token.
All inputs are finite; a program needn't handle non-finite values.
Results may differ from the reference program's by a relative error of at most 0.023.
Values may be sent and summed in bfloat16 or wider, within the bound.
No kernel may reach another device: no remote copies, remote signals or barrier semaphores. Data moves between devices by JAX's collectives and lax.ppermute only.
A program may use at most 192 MiB of HBM per device.

```python
import jax
import jax.numpy as jnp
from jax import lax

D = 768
HEADS = 12
HEAD_DIM = 64
FF = 3072
EXPERTS = 4
PROMPT = 1024
CONT_LEN = 256
NCONT = 8
TOK_G = 3072
CAP = 864
GROUPS = 8


def draw_segments(key, part):

    def one_group(subkey):
        lengths = jax.random.randint(subkey, (NCONT,), CONT_LEN // 2, CONT_LEN + 1).astype(jnp.int32)
        prompt_length = TOK_G - jnp.sum(lengths)
        starts = prompt_length + jnp.cumsum(lengths) - lengths
        positions = jnp.arange(TOK_G, dtype=jnp.int32)
        return jnp.sum((positions[:, None] >= starts[None, :]).astype(jnp.int32), axis=1).astype(jnp.int32)
    return jax.vmap(one_group)(jax.random.split(key, GROUPS))


def with_spikes(values, rng, source, target, shards_of, factor):
    def block_of(position):
        return (jnp.arange(values.shape[position]) // (values.shape[position] // shards_of)).reshape((-1,) + (1,) * (values.ndim - 1 - position))

    first = jax.random.permutation(rng, shards_of)[block_of(target)]
    other_side = (block_of(target) + shards_of // 2) % shards_of
    return jnp.where((block_of(source) == first) | (block_of(source) == other_side), factor * values, values)


def block_scale(key, dims, cuts, smallest, high):
    level, own = 1.0, jax.random.fold_in(key, 6)
    for axis_at, blocks in cuts:
        steps = jnp.exp(jax.random.uniform(jax.random.fold_in(own, axis_at), (blocks,), jnp.float32, smallest / len(cuts), high / len(cuts)))
        level = level * jnp.repeat(steps, dims[axis_at] // blocks).reshape([-1 if axis == axis_at else 1 for axis in range(len(dims))])
    return level


def picks_of(rng, rows, number_of, top, lift):
    order = jax.random.permutation(jax.random.fold_in(rng, 1), number_of)
    pull = order
    for power in range(3):
        pull = pull * pull // number_of
    pull = pull * lift // number_of
    tickets = jax.random.randint(jax.random.fold_in(rng, 2), (rows, number_of), 0, 4096) + pull
    fixed_rows = jax.random.permutation(jax.random.fold_in(rng, 3), rows)[jnp.arange(number_of) % rows]
    tickets = jnp.where(jnp.arange(rows)[:, None] == fixed_rows[None, :], 1 << 14, tickets)
    score = tickets * number_of + jnp.arange(number_of)
    return lax.top_k(score.astype(jnp.int32), top)[1].astype(jnp.int32)


def centred(own_key, shape, scale, limit, cuts=(), kind=jnp.bfloat16):
    array = scale * jax.random.normal(own_key, shape, jnp.float32)
    if cuts:
        array = array * block_scale(own_key, shape, cuts, -0.22, 0.18)
    return jnp.clip(array, -limit, limit).astype(kind)


def heavy_noise(stream_key, dims, spread, reach, cuts, heavy, kind=jnp.bfloat16):
    values = spread * jax.random.normal(stream_key, dims, jnp.float32)
    if cuts:
        values = values * block_scale(stream_key, dims, cuts, -0.22, 0.18)
    return jnp.clip(with_spikes(values, jax.random.fold_in(stream_key, 3), *heavy), -reach, reach).astype(kind)


def setup_inputs(seed: int = 0) -> dict:
    arg_keys = jax.random.split(jax.random.key(seed), 13)
    block_input = heavy_noise(arg_keys[0], (GROUPS, TOK_G, D), 1.0, 6.0, ((0, 8), (1, 4)), (0, 2, 8, 2.0))
    attention_gain = jnp.clip(1.0 + 0.1 * jax.random.normal(arg_keys[1], (D,), jnp.float32), 0.5, 1.5)
    qkv_weight = centred(arg_keys[2], (3, D, D), D ** -0.5, 0.21875, ((2, 4),))
    proj_weight = centred(arg_keys[3], (D, D), (max(D * 4 // PROMPT, 1)) ** -0.5, 3.5, ((0, 4),))
    moe_gain = jnp.clip(1.0 + 0.1 * jax.random.normal(arg_keys[4], (D,), jnp.float32), 0.5, 1.5)
    centroids = centred(arg_keys[5], (EXPERTS, D), (2 * D) ** -0.5, 0.15625)
    expert_up = centred(arg_keys[6], (EXPERTS, D, FF), D ** -0.5, 0.21875, ((2, 4),))
    expert_down = centred(arg_keys[7], (EXPERTS, FF, D), (FF // 4) ** -0.5, 0.21875, ((1, 4),))
    out_grad = heavy_noise(arg_keys[8], (GROUPS, TOK_G, D), 1.0, 6.0, ((0, 8), (1, 4)), (0, 2, 8, 2.0))
    routes = picks_of(arg_keys[9], GROUPS * TOK_G, EXPERTS, 1, 2048).reshape((GROUPS, TOK_G, 1))
    priority = jax.vmap(lambda own: jax.random.permutation(own, TOK_G))(jax.random.split(arg_keys[10], GROUPS)).reshape((GROUPS, TOK_G)).astype(jnp.int32)
    segments = draw_segments(jax.random.fold_in(arg_keys[12], 71), 0)
    return dict(block_input=block_input, attention_gain=attention_gain, qkv_weight=qkv_weight, proj_weight=proj_weight, moe_gain=moe_gain, centroids=centroids, expert_up=expert_up, expert_down=expert_down, out_grad=out_grad, routes=routes, priority=priority, segments=segments)


@jax.custom_vjp
def low(v):
    return lax.optimization_barrier(v.astype(jnp.bfloat16)).astype(jnp.float32)

@jax.custom_vjp
def low_back(v):
    return v

def low_keep(v):
    return (low(v), None)

def low_pass(kept, grad):
    return (grad,)

def back_keep(v):
    return (v, None)

def back_low(kept, grad):
    return (low(grad),)
low.defvjp(low_keep, low_pass)
low_back.defvjp(back_keep, back_low)
epsilon = 1e-05
highest = lax.Precision.HIGHEST

def gelu_tanh(values):
    return 0.5 * values * (1.0 + jnp.tanh(0.7978845608028654 * (values + 0.044715 * values * values * values)))

def normalize_rows(values, gain_row):
    centered = values - lax.optimization_barrier(jnp.mean(values, axis=-1, keepdims=True))
    variance = lax.optimization_barrier(jnp.mean(centered * centered, axis=-1, keepdims=True))
    return centered * lax.rsqrt(variance + epsilon) * gain_row

def route_slots(route_col, priority_row, experts, capacity):
    token_count = route_col.shape[0]
    route_hot = (route_col[:, None] == jnp.arange(experts, dtype=jnp.int32)[None, :]).astype(jnp.int32)
    inverse = jnp.zeros((token_count,), jnp.int32).at[priority_row].set(jnp.arange(token_count, dtype=jnp.int32))
    ranked = route_hot[inverse]
    before = jnp.cumsum(ranked, axis=0) - ranked
    slot_rank = lax.optimization_barrier(jnp.sum(before * ranked, axis=1))[priority_row]
    kept_mask = slot_rank < capacity
    target = jnp.where(kept_mask, route_col * capacity + slot_rank, experts * capacity).astype(jnp.int32)
    slot_table = jnp.full((experts * capacity + 1,), token_count, jnp.int32).at[target].set(jnp.arange(token_count, dtype=jnp.int32))
    return (route_hot, kept_mask, target, slot_table[:experts * capacity])

def allowed_mask(segment, offset, block_rows):
    query_pos = offset + jnp.arange(block_rows, dtype=jnp.int32)
    key_pos = jnp.arange(segment.shape[0], dtype=jnp.int32)
    query_seg = lax.dynamic_slice_in_dim(segment, offset, block_rows, 0)
    causal = key_pos[None, :] <= query_pos[:, None]
    shared = (segment[None, :] == 0) | (segment[None, :] == query_seg[:, None])
    return causal & shared

def group_forward(params, inputs, segment, route_hot, kept_mask, target, slot_table):
    attention_gain, qkv_weight, proj_weight, moe_gain, centroids, expert_up, expert_down = params
    token_count = inputs.shape[0]
    model_width = inputs.shape[1]
    normed_one = low(normalize_rows(inputs, attention_gain))
    qkv_all = jnp.einsum('td,kdh->kth', normed_one, qkv_weight, precision=highest)
    qkv_all = low_back(low(qkv_all))
    queries = qkv_all[0].reshape(token_count, HEADS, HEAD_DIM)
    keys_all = qkv_all[1].reshape(token_count, HEADS, HEAD_DIM)
    values_all = qkv_all[2].reshape(token_count, HEADS, HEAD_DIM)
    block_rows = min(512, token_count)
    score_scale = HEAD_DIM ** (-0.5)

    def attend(offset):
        query_block = lax.dynamic_slice_in_dim(queries, offset, block_rows, 0)
        scores = jnp.einsum('qhd,khd->hqk', query_block, keys_all, precision=highest) * score_scale
        scores = low_back(scores)
        scores = jnp.where(allowed_mask(segment, offset, block_rows)[None], scores, -1e+30)
        top_score = lax.optimization_barrier(jnp.max(scores, axis=-1, keepdims=True))
        weights = jnp.exp(scores - top_score)
        prob_rows = low(weights / lax.optimization_barrier(jnp.sum(weights, axis=-1, keepdims=True)))
        return jnp.einsum('hqk,khd->qhd', prob_rows, values_all, precision=highest)
    offsets = jnp.arange(token_count // block_rows, dtype=jnp.int32) * block_rows
    context = lax.map(jax.checkpoint(attend), offsets).reshape(token_count, HEADS * HEAD_DIM)
    context = low_back(low(context))
    attended = low_back(jnp.dot(context, proj_weight, precision=highest))
    mixed_one = inputs + attended
    normed_two = low(normalize_rows(mixed_one, moe_gain))
    padded = jnp.concatenate([normed_two, jnp.zeros((1, model_width), normed_two.dtype)], axis=0)
    dispatched = padded[slot_table].reshape(EXPERTS, CAP, model_width)
    upward = low_back(jnp.einsum('ecd,edf->ecf', dispatched, expert_up, precision=highest))
    hidden = low(gelu_tanh(upward))
    returned = jnp.einsum('ecf,efd->ecd', hidden, expert_down, precision=highest).reshape(EXPERTS * CAP, model_width)
    returned = jnp.concatenate([returned, jnp.zeros((1, model_width), returned.dtype)], axis=0)[target]
    returned = low_back(returned)
    centroid_rows = jnp.dot(route_hot.astype(inputs.dtype), centroids, precision=highest)
    gate_used = jnp.where(kept_mask, jax.nn.sigmoid(lax.optimization_barrier(jnp.sum(normed_two * centroid_rows, axis=-1))), 0.0)
    return mixed_one + gate_used[:, None] * returned

def reference(block_input, attention_gain, qkv_weight, proj_weight, moe_gain, centroids, expert_up, expert_down, out_grad, routes, priority, segments):
    params = tuple((parameter.astype(jnp.float32) for parameter in (attention_gain, qkv_weight, proj_weight, moe_gain, centroids, expert_up, expert_down)))

    def group_step(summed, group_data):
        inputs, upstream, route_col, priority_row, segment = group_data
        route_hot, kept_mask, target, slot_table = route_slots(route_col[:, 0], priority_row, EXPERTS, CAP)

        def forward(weights, values):
            return group_forward(weights, values, segment, route_hot, kept_mask, target, slot_table)
        result, pullback = jax.vjp(forward, params, inputs.astype(jnp.float32))
        grad_params, grad_inputs = pullback(upstream.astype(jnp.float32))
        summed = tuple((total_now + partial_value for total_now, partial_value in zip(summed, grad_params)))
        return (summed, (result.astype(jnp.bfloat16), grad_inputs.astype(jnp.bfloat16)))
    initial = tuple((jnp.zeros_like(parameter) for parameter in params))
    summed, (outputs, input_grads) = lax.scan(group_step, initial, (block_input, out_grad, routes, priority, segments))
    return (outputs, input_grads, summed[0], summed[3], summed[4], summed[1], summed[2], summed[5], summed[6])
```

```python
import jax
import jax.numpy as jnp
from jax import lax
from jax.sharding import Mesh
from jax.sharding import PartitionSpec as P

HEAD_DIM = 64


epsilon = 1e-05
highest = lax.Precision.HIGHEST


def gelu_tanh(values):
    return (
        0.5
        * values
        * (1.0 + jnp.tanh(0.7978845608028654 * (values + 0.044715 * values * values * values)))
    )


def normalize_plain(values):
    centered = values - jnp.mean(values, axis=-1, keepdims=True)
    variance = jnp.mean(centered * centered, axis=-1, keepdims=True)
    inverse = lax.rsqrt(variance + epsilon)
    return (centered * inverse, inverse)


def normalize_back(upstream, unit_rows, inverse, gain_row):
    scaled = upstream * gain_row
    centered = scaled - jnp.mean(scaled, axis=-1, keepdims=True)
    return inverse * (centered - unit_rows * jnp.mean(scaled * unit_rows, axis=-1, keepdims=True))


def route_slots(route_col, priority_row, experts, capacity):
    token_count = route_col.shape[0]
    route_hot = (route_col[:, None] == jnp.arange(experts, dtype=jnp.int32)[None, :]).astype(
        jnp.int32
    )
    inverse = (
        jnp.zeros((token_count,), jnp.int32)
        .at[priority_row]
        .set(jnp.arange(token_count, dtype=jnp.int32))
    )
    ranked = route_hot[inverse]
    before = jnp.cumsum(ranked, axis=0) - ranked
    slot_rank = jnp.sum(before * ranked, axis=1)[priority_row]
    kept_mask = slot_rank < capacity
    target = jnp.where(kept_mask, route_col * capacity + slot_rank, experts * capacity)
    slot_table = (
        jnp.full((experts * capacity + 1,), token_count, jnp.int32)
        .at[target]
        .set(jnp.arange(token_count, dtype=jnp.int32))
    )
    return (route_hot, kept_mask, target, slot_table[: experts * capacity])


def allowed_mask(segment, offset, block_rows):
    query_pos = offset + jnp.arange(block_rows, dtype=jnp.int32)
    key_pos = jnp.arange(segment.shape[0], dtype=jnp.int32)
    query_seg = lax.dynamic_slice_in_dim(segment, offset, block_rows, 0)
    causal = key_pos[None, :] <= query_pos[:, None]
    shared = (segment[None, :] == 0) | (segment[None, :] == query_seg[:, None])
    return causal & shared


def swap_roles(value):
    moves = [(2 * c + h, 2 * h + c) for c in range(2) for h in range(2)]
    return lax.ppermute(value, ("c", "zh"), moves)


def flip(value, axis):
    return lax.ppermute(value, axis, [(0, 1), (1, 0)])


def gather_rows(rows):
    count, width = rows.shape
    core, near = lax.axis_index("c"), lax.axis_index("zl")
    across = flip(rows, "zl")
    beside = flip(rows, "c")
    corner = flip(across, "c")
    whole = jnp.zeros((4 * count, width), rows.dtype)
    for block, c, z in (
        (rows, core, near),
        (beside, 1 - core, near),
        (across, core, 1 - near),
        (corner, 1 - core, 1 - near),
    ):
        whole = lax.dynamic_update_slice_in_dim(whole, block, (2 * c + z) * count, 0)
    return whole


def scatter_rows(partial):
    count = partial.shape[0] // 4
    core, near = lax.axis_index("c"), lax.axis_index("zl")

    def block(c, z):
        return lax.dynamic_slice_in_dim(partial, (2 * c + z) * count, count, 0)

    far = flip(block(1 - core, 1 - near), "c").astype(jnp.float32)
    far = (far + block(core, 1 - near).astype(jnp.float32)).astype(partial.dtype)
    far = flip(far, "zl").astype(jnp.float32)
    beside = flip(block(1 - core, near), "c").astype(jnp.float32)
    return block(core, near).astype(jnp.float32) + beside + far


def other_quarter(weight, after=None):
    users = lax.axis_size("u") * lax.axis_size("c")
    flat = weight.reshape(-1, weight.shape[-1])
    part = flat.shape[0] // users
    mine = lax.axis_index("u") * 2 + lax.axis_index("c")
    piece = lax.dynamic_slice_in_dim(flat, mine * part, part, 0)
    if after is not None:
        piece, after = lax.optimization_barrier((piece, after))
    piece = flip(piece, "zh")
    return lax.all_gather(piece, ("u", "c"), axis=0, tiled=True).reshape(weight.shape)


def pick_quarter(weight, after=None):
    keep = lax.axis_index("c") == lax.axis_index("zh")
    return jnp.where(keep, weight, other_quarter(weight, after))


def body(
    block_input,
    attention_gain,
    qkv_weight,
    proj_weight,
    moe_gain,
    centroids,
    expert_up,
    expert_down,
    out_grad,
    routes,
    priority,
    segments,
):
    row_count = block_input.shape[1]
    model_width = block_input.shape[2]
    experts = expert_up.shape[0]
    token_count = segments.shape[1]
    capacity = 9 * token_count // (8 * experts)
    local_width = qkv_weight.shape[2]
    head_count = local_width // HEAD_DIM
    block_rows = min(512, token_count)
    score_scale = HEAD_DIM ** (-0.5)
    own_start = (2 * lax.axis_index("c") + lax.axis_index("zl")) * row_count
    held = swap_roles(block_input[0])
    indices = swap_roles(jnp.stack([routes[0, :, 0], priority[0], segments[0]]))
    segment = indices[2]
    qkv_weight = pick_quarter(qkv_weight)
    proj_weight = pick_quarter(proj_weight)
    out_grad = swap_roles(out_grad[0])
    expert_up = pick_quarter(expert_up, held)
    expert_down = pick_quarter(expert_down, held)
    inputs = held.astype(jnp.float32)
    unit_one, inverse_one = normalize_plain(inputs)
    normed_one_rows = (unit_one * attention_gain).astype(jnp.bfloat16)
    normed_one = gather_rows(normed_one_rows)
    qkv_all = jnp.einsum(
        "td,kdh->kth", normed_one, qkv_weight, preferred_element_type=jnp.float32
    ).astype(jnp.bfloat16)
    queries = qkv_all[0].reshape(token_count, head_count, HEAD_DIM)
    keys_all = qkv_all[1].reshape(token_count, head_count, HEAD_DIM)
    values_all = qkv_all[2].reshape(token_count, head_count, HEAD_DIM)

    def masked_scores(offset):
        query_block = lax.dynamic_slice_in_dim(queries, offset, block_rows, 0)
        scores = (
            jnp.einsum("qhd,khd->hqk", query_block, keys_all, preferred_element_type=jnp.float32)
            * score_scale
        )
        return (
            jnp.where(allowed_mask(segment, offset, block_rows)[None], scores, -1e30),
            query_block,
        )

    def attend(offset):
        scores = masked_scores(offset)[0]
        top_score = jnp.max(scores, axis=-1, keepdims=True)
        weights = jnp.exp(scores - top_score)
        totals = jnp.sum(weights, axis=-1, keepdims=True)
        prob_rows = (weights / totals).astype(jnp.bfloat16)
        context_block = jnp.einsum(
            "hqk,khd->qhd", prob_rows, values_all, preferred_element_type=jnp.float32
        )
        return (context_block.astype(jnp.bfloat16), (top_score + jnp.log(totals))[:, :, 0])

    offsets = jnp.arange(token_count // block_rows, dtype=jnp.int32) * block_rows
    context_blocks, log_totals = lax.map(attend, offsets)
    context = context_blocks.reshape(token_count, local_width)
    attended = scatter_rows(jnp.dot(context, proj_weight, preferred_element_type=jnp.float32).astype(jnp.bfloat16))
    mixed_one = inputs + attended
    unit_two, inverse_two = normalize_plain(mixed_one)
    normed_two_rows = (unit_two * moe_gain).astype(jnp.bfloat16)
    normed_two = gather_rows(normed_two_rows)
    route_hot, kept_mask, target, slot_table = route_slots(
        indices[0], indices[1], experts, capacity
    )
    zero_row = jnp.zeros((1, model_width), jnp.bfloat16)
    zero_float = jnp.zeros((1, model_width), jnp.float32)
    dispatched = jnp.concatenate([normed_two, zero_row], axis=0)[slot_table].reshape(
        experts, capacity, model_width
    )
    upward = jnp.einsum("ecd,edf->ecf", dispatched, expert_up, preferred_element_type=jnp.float32)
    hidden = gelu_tanh(upward).astype(jnp.bfloat16)
    returned = jnp.einsum(
        "ecf,efd->ecd", hidden, expert_down, preferred_element_type=jnp.float32
    ).reshape(experts * capacity, model_width)
    returned = jnp.concatenate([returned, zero_float], axis=0)
    expert_out = scatter_rows(returned[target].astype(jnp.bfloat16))
    hot_rows = lax.dynamic_slice_in_dim(route_hot, own_start, row_count, 0)
    kept_rows = lax.dynamic_slice_in_dim(kept_mask, own_start, row_count, 0)
    centroid_rows = jnp.dot(
        hot_rows.astype(jnp.bfloat16), centroids, preferred_element_type=jnp.float32
    )
    normed_two_float = normed_two_rows.astype(jnp.float32)
    gate_prob = jax.nn.sigmoid(jnp.sum(normed_two_float * centroid_rows, axis=-1))
    gate_used = jnp.where(kept_rows, gate_prob, 0.0)
    mixed_two = mixed_one + gate_used[:, None] * expert_out
    block_output = swap_roles(mixed_two.astype(jnp.bfloat16))[None]
    upstream = out_grad.astype(jnp.float32)
    grad_eo_rows = (gate_used[:, None] * upstream).astype(jnp.bfloat16)
    grad_gate = jnp.where(kept_rows, jnp.sum(upstream * expert_out, axis=-1), 0.0)
    grad_score = grad_gate * gate_prob * (1.0 - gate_prob)
    grad_eo = gather_rows(grad_eo_rows)
    grad_dispatched = jnp.concatenate([grad_eo, zero_row], axis=0)[slot_table].reshape(
        experts, capacity, model_width
    )
    grad_hidden = jnp.einsum(
        "ecd,efd->ecf", grad_dispatched, expert_down, preferred_element_type=jnp.float32
    )
    down_part = jnp.einsum(
        "ecf,ecd->efd", hidden, grad_dispatched, preferred_element_type=jnp.float32
    )
    gelu_value, gelu_pull = jax.vjp(gelu_tanh, upward)
    grad_upward = gelu_pull(grad_hidden)[0].astype(jnp.bfloat16)
    up_part = jnp.einsum(
        "ecd,ecf->edf", dispatched, grad_upward, preferred_element_type=jnp.float32
    )
    back_moe = jnp.einsum(
        "ecf,edf->ecd", grad_upward, expert_up, preferred_element_type=jnp.float32
    ).reshape(experts * capacity, model_width)
    back_moe = jnp.concatenate([back_moe, zero_float], axis=0)
    grad_two = (
        scatter_rows(back_moe[target].astype(jnp.bfloat16))
        + grad_score[:, None] * centroid_rows
    )
    centroid_part = jnp.einsum(
        "te,td->ed",
        hot_rows.astype(jnp.float32),
        grad_score[:, None] * normed_two_float,
        precision=highest,
    )
    moe_gain_part = jnp.sum(grad_two * unit_two, axis=0)
    grad_mixed = upstream + normalize_back(grad_two, unit_two, inverse_two, moe_gain)
    grad_att_rows = grad_mixed.astype(jnp.bfloat16)
    grad_att = gather_rows(grad_att_rows)
    proj_part = jnp.einsum("tc,td->cd", context, grad_att, preferred_element_type=jnp.float32)
    grad_context = jnp.einsum(
        "td,cd->tc", grad_att, proj_weight, preferred_element_type=jnp.float32
    ).astype(jnp.bfloat16)
    grad_context = grad_context.reshape(token_count, head_count, HEAD_DIM)

    def back_block(carried, offset_and_log):
        offset, log_block = offset_and_log
        key_grad, value_grad = carried
        scores, query_block = masked_scores(offset)
        prob_rows = jnp.exp(scores - log_block[:, :, None])
        prob_low = prob_rows.astype(jnp.bfloat16)
        grad_block = lax.dynamic_slice_in_dim(grad_context, offset, block_rows, 0)
        grad_probs = jnp.einsum(
            "qhd,khd->hqk", grad_block, values_all, preferred_element_type=jnp.float32
        )
        row_inner = jnp.sum(prob_rows * grad_probs, axis=-1, keepdims=True)
        grad_scores = (prob_rows * (grad_probs - row_inner)).astype(jnp.bfloat16)
        query_grad = (
            jnp.einsum("hqk,khd->qhd", grad_scores, keys_all, preferred_element_type=jnp.float32)
            * score_scale
        ).astype(jnp.bfloat16)
        key_grad = (
            key_grad
            + jnp.einsum(
                "hqk,qhd->khd", grad_scores, query_block, preferred_element_type=jnp.float32
            )
            * score_scale
        )
        value_grad = value_grad + jnp.einsum(
            "hqk,qhd->khd", prob_low, grad_block, preferred_element_type=jnp.float32
        )
        return ((key_grad, value_grad), query_grad)

    zero_keys = jnp.zeros((token_count, head_count, HEAD_DIM), jnp.float32)
    (key_grad, value_grad), query_blocks = lax.scan(
        back_block, (zero_keys, zero_keys), (offsets, log_totals)
    )
    grad_qkv = jnp.stack(
        [
            query_blocks.reshape(token_count, local_width),
            key_grad.astype(jnp.bfloat16).reshape(token_count, local_width),
            value_grad.astype(jnp.bfloat16).reshape(token_count, local_width),
        ]
    )
    qkv_part = jnp.einsum("td,kth->kdh", normed_one, grad_qkv, preferred_element_type=jnp.float32)
    grad_one = scatter_rows(jnp.einsum("kth,kdh->td", grad_qkv, qkv_weight, preferred_element_type=jnp.float32).astype(
            jnp.bfloat16
        ))
    attention_gain_part = jnp.sum(grad_one * unit_one, axis=0)
    input_grad = swap_roles(
        (grad_mixed + normalize_back(grad_one, unit_one, inverse_one, attention_gain)).astype(
            jnp.bfloat16
        )
    )[None]
    everyone = ("u", "c", "zh", "zl")
    gain_one_sum, gain_two_sum, centroid_sum = (
        lax.psum_scatter(attention_gain_part, everyone, scatter_dimension=0, tiled=True),
        lax.psum_scatter(moe_gain_part, everyone, scatter_dimension=0, tiled=True),
        lax.psum_scatter(centroid_part, everyone, scatter_dimension=1, tiled=True),
    )

    def summed(part, dimension):
        part = lax.psum_scatter(
            part.astype(jnp.bfloat16), ("u", "zh"), scatter_dimension=dimension, tiled=True
        )
        return swap_roles(part).astype(jnp.float32)

    qkv_summed, proj_summed, up_summed, down_summed = (
        summed(qkv_part, 1),
        summed(proj_part, 1),
        summed(up_part, 1),
        summed(down_part, 2),
    )
    return (
        block_output,
        input_grad,
        gain_one_sum,
        gain_two_sum,
        centroid_sum,
        qkv_summed,
        proj_summed,
        up_summed,
        down_summed,
    )


def solution(mesh):
    shape = mesh.devices.shape
    bits = (shape[0] // 2, 2, shape[1] // 2, 2)
    dp, tensor = ("u", "c"), ("zh", "zl")
    mesh = Mesh(mesh.devices.reshape(bits), dp + tensor)
    return jax.shard_map(
        body,
        mesh=mesh,
        in_specs=(
            P(dp, tensor, None),
            P(),
            P(None, None, tensor),
            P(tensor, None),
            P(),
            P(),
            P(None, None, tensor),
            P(None, tensor, None),
            P(dp, tensor, None),
            P(dp, None, None),
            P(dp, None),
            P(dp, None),
        ),
        out_specs=(
            P(dp, tensor, None),
            P(dp, tensor, None),
            P(dp + tensor),
            P(dp + tensor),
            P(None, dp + tensor),
            P(None, dp, tensor),
            P(tensor, dp),
            P(None, dp, tensor),
            P(None, tensor, dp),
        ),
        check_vma=False,
    )
```

```python
import jax
import jax.numpy as jnp
from jax import lax
from jax.experimental import pallas as pl
from jax.experimental.pallas import tpu as pltpu
from jax.sharding import Mesh
from jax.sharding import PartitionSpec as P

HEAD_DIM = 64
QUERY_BLOCK = 512
BLOCK = 256
LOG2E = 1.4426950408889634
NEGATIVE = -1e30
TILE = 256
ALIGN = 16
HBM = pl.BlockSpec(memory_space=pl.ANY)

epsilon = 1e-05
highest = lax.Precision.HIGHEST


def normalize_plain(values):
    centered = values - jnp.mean(values, axis=-1, keepdims=True)
    variance = jnp.mean(centered * centered, axis=-1, keepdims=True)
    inverse = lax.rsqrt(variance + epsilon)
    return (centered * inverse, inverse)


def normalize_back(upstream, unit_rows, inverse, gain_row):
    scaled = upstream * gain_row
    centered = scaled - jnp.mean(scaled, axis=-1, keepdims=True)
    return inverse * (centered - unit_rows * jnp.mean(scaled * unit_rows, axis=-1, keepdims=True))


def matmul(a, b, dims=((1,), (0,))):
    return lax.dot_general(a, b, (dims, ((), ())), preferred_element_type=jnp.float32)


def key_ranges(segment, block):
    token_count = segment.shape[0]
    position = jnp.arange(token_count, dtype=jnp.int32)
    prompt = jnp.sum((segment == 0).astype(jnp.int32))
    fresh = jnp.concatenate([jnp.ones((1,), jnp.bool_), segment[1:] != segment[:-1]])
    start = lax.cummax(jnp.where(fresh, position, 0), axis=0)
    first = jnp.arange(token_count // block, dtype=jnp.int32) * block
    whole = jnp.minimum(prompt, first) // block
    shared = (jnp.minimum(prompt, first + block) + block - 1) // block
    own = jnp.maximum(shared, start[first] // block)
    last = first // block + 1
    return (jnp.stack([whole, shared, own, last, jnp.full_like(whole, prompt)]), start[None, :])


def copies(pairs, semaphores):
    moved = [
        pltpu.make_async_copy(source, target, semaphores.at[place])
        for place, (source, target) in enumerate(pairs)
    ]
    for copy in moved:
        copy.start()
    for copy in moved:
        copy.wait()


def rank_rows(ref, rank, like):
    count = like.shape[0]
    return ref.at[pl.ds(pl.multiple_of(rank * count, count), count)]


def send_ranks(ref, targets, ranks, semaphores, edge, block, down):
    count = targets[0].shape[0]
    for rank in range(4):
        if down:
            first = rank * count
            due = (edge <= first) & (edge + block > first)
        else:
            last = (rank + 1) * count
            due = (edge >= last) & (edge - block < last)

        @pl.when(due)
        def _(rank=rank):
            for b, target in enumerate(targets):

                @pl.when(ranks[b] == rank)
                def _(b=b, target=target):
                    source = ref.at[rank * count : (rank + 1) * count]
                    pltpu.make_async_copy(source, target, semaphores.at[b]).start()


def await_ranks(ref, targets, ranks, semaphores):
    for b, target in enumerate(targets):
        pltpu.make_async_copy(rank_rows(ref, ranks[b], target), target, semaphores.at[b]).wait()


def forward_kernel(
    ranges, ranks, x0, x1, x2, x3, w_ref, proj_ref, start_ref,
    p0, p1, p2, p3, q_ref, qt_ref, k_ref, kt_ref, v_ref, ctx_ref, lse_ref,
    x_ref, part_ref, vt_ref, score_ref, top_ref, sum_ref, arrived, left,
):
    step = pl.program_id(0)
    heads = q_ref.shape[0]
    block = q_ref.shape[1]
    rows = pl.ds(pl.multiple_of(step * block, block), block)

    @pl.when(step == 0)
    def _():
        copies(
            [(x, rank_rows(x_ref, ranks[b], x)) for b, x in enumerate((x0, x1, x2, x3))], arrived
        )

    x = x_ref[rows, :]
    kinds = []
    for kind in range(3):
        made = matmul(x, w_ref[kind])
        kinds.append((made.astype(jnp.bfloat16), made.T.astype(jnp.bfloat16)))
    for head in range(heads):
        part = slice(head * HEAD_DIM, (head + 1) * HEAD_DIM)
        q_ref[head] = kinds[0][0][:, part]
        k_ref[head, rows, :] = kinds[1][0][:, part]
        v_ref[head, rows, :] = kinds[2][0][:, part]
        qt_ref[head] = kinds[0][1][part]
        for piece in range(kt_ref.shape[0]):
            columns = slice(piece * kt_ref.shape[3], (piece + 1) * kt_ref.shape[3])
            kt_ref[piece, head] = kinds[1][1][part, columns]
        vt_ref[step, head, :HEAD_DIM] = kinds[2][1][part]
        vt_ref[step, head, HEAD_DIM:] = jnp.ones((16, block), jnp.bfloat16)
    top_ref[...] = jnp.full_like(top_ref, NEGATIVE)
    sum_ref[...] = jnp.zeros_like(sum_ref)
    prompt = ranges[4, step]
    scale = LOG2E * HEAD_DIM ** (-0.5)

    def visit(key, masked):
        place = pl.ds(pl.multiple_of(key * block, block), block)
        if masked:
            key_at = key * block + lax.broadcasted_iota(jnp.int32, (block, block), 0)
            query_at = step * block + lax.broadcasted_iota(jnp.int32, (block, block), 1)
            seen = (key_at <= query_at) & ((key_at < prompt) | (key_at >= start_ref[...]))
        for head in range(heads):
            scores = matmul(k_ref[head, place, :], qt_ref[head])
            if masked:
                scores = jnp.where(seen, scores, NEGATIVE)
            score_ref[key, head] = scores
            top_ref[head] = jnp.maximum(
                top_ref[head], jnp.max(scores.reshape(block // 8, 8, block), axis=0)
            )

    def plain(key, carry):
        visit(key, False)
        return carry

    def edge(key, carry):
        visit(key, True)
        return carry

    lax.fori_loop(0, ranges[0, step], plain, 0)
    lax.fori_loop(ranges[0, step], ranges[1, step], edge, 0)
    lax.fori_loop(ranges[2, step], ranges[3, step], edge, 0)
    for head in range(heads):
        top_ref[head, :1] = jnp.max(top_ref[head], axis=0, keepdims=True) * scale

    def add(key, carry):
        for head in range(heads):
            weights = jnp.exp2(score_ref[key, head] * scale - top_ref[head, :1])
            sum_ref[head] += matmul(vt_ref[key, head], weights.astype(jnp.bfloat16))
        return carry

    lax.fori_loop(0, ranges[1, step], add, 0)
    lax.fori_loop(ranges[2, step], ranges[3, step], add, 0)
    for head in range(heads):
        total = sum_ref[head, HEAD_DIM : HEAD_DIM + 1]
        context = sum_ref[head, :HEAD_DIM] / total
        ctx_ref[head * HEAD_DIM : (head + 1) * HEAD_DIM] = context.astype(jnp.bfloat16)
        lse_ref[head] = top_ref[head, :1] + jnp.log(total) * LOG2E
    part_ref[rows, :] = matmul(ctx_ref[...], proj_ref[...], ((0,), (0,))).astype(jnp.bfloat16)
    send_ranks(part_ref, (p0, p1, p2, p3), ranks, left, (step + 1) * block, block, False)

    @pl.when(step == pl.num_programs(0) - 1)
    def _():
        await_ranks(part_ref, (p0, p1, p2, p3), ranks, left)


def attention_forward(ranges, start, ranks, x, w, proj):
    tokens, width = start.shape[1], x[0].shape[1]
    local = w.shape[2]
    heads = local // HEAD_DIM
    block = QUERY_BLOCK
    fine = BLOCK
    count = tokens // block
    low = jnp.bfloat16
    head_rows = pl.BlockSpec((heads, tokens, HEAD_DIM), lambda i, r, n: (0, 0, 0))
    flops = 2 * tokens * width * local * 4 + tokens * tokens * local * 2
    return pl.pallas_call(
        forward_kernel,
        grid_spec=pltpu.PrefetchScalarGridSpec(
            num_scalar_prefetch=2,
            grid=(count,),
            in_specs=[
                *[HBM] * 4,
                pl.BlockSpec((3, width, local), lambda i, r, n: (0, 0, 0)),
                pl.BlockSpec((local, width), lambda i, r, n: (0, 0)),
                pl.BlockSpec((1, block), lambda i, r, n: (0, i)),
            ],
            out_specs=[
                *[HBM] * 4,
                pl.BlockSpec((heads, block, HEAD_DIM), lambda i, r, n: (0, i, 0)),
                pl.BlockSpec((heads, HEAD_DIM, block), lambda i, r, n: (0, 0, i)),
                head_rows,
                pl.BlockSpec((block // fine, heads, HEAD_DIM, fine), lambda i, r, n: (i, 0, 0, 0)),
                head_rows,
                pl.BlockSpec((local, block), lambda i, r, n: (0, i)),
                pl.BlockSpec((heads, 1, block), lambda i, r, n: (0, 0, i)),
            ],
            scratch_shapes=[
                pltpu.VMEM((tokens, width), low),
                pltpu.VMEM((tokens, width), low),
                pltpu.VMEM((count, heads, HEAD_DIM + 16, block), low),
                pltpu.VMEM((count, heads, block, block), jnp.float32),
                pltpu.VMEM((heads, 8, block), jnp.float32),
                pltpu.VMEM((heads, HEAD_DIM + 16, block), jnp.float32),
                pltpu.SemaphoreType.DMA((4,)),
                pltpu.SemaphoreType.DMA((4,)),
            ],
        ),
        out_shape=[
            *[jax.ShapeDtypeStruct(x[0].shape, low)] * 4,
            jax.ShapeDtypeStruct((heads, tokens, HEAD_DIM), low),
            jax.ShapeDtypeStruct((heads, HEAD_DIM, tokens), low),
            jax.ShapeDtypeStruct((heads, tokens, HEAD_DIM), low),
            jax.ShapeDtypeStruct((tokens // fine, heads, HEAD_DIM, fine), low),
            jax.ShapeDtypeStruct((heads, tokens, HEAD_DIM), low),
            jax.ShapeDtypeStruct((local, tokens), low),
            jax.ShapeDtypeStruct((heads, 1, tokens), jnp.float32),
        ],
        compiler_params=pltpu.CompilerParams(vmem_limit_bytes=56 << 20),
        cost_estimate=pl.CostEstimate(
            flops=4 * flops, transcendentals=tokens * tokens * heads // 2, bytes_accessed=40 << 20
        ),
        name="attention_forward",
    )(ranges, ranks, *x, w, proj, start)


def backward_kernel(
    ranges, ranks, g0, g1, g2, g3, x0, x1, x2, x3,
    ctx_ref, lse_ref, q_ref, qt_ref, start_ref, k_ref, kt_ref, v_ref, w_ref, proj_ref,
    p0, p1, p2, p3, weights_ref,
    g_ref, x_ref, part_ref, wgrad_ref, pgrad_ref,
    dk_ref, dv_ref, dqt_ref, out_ref, outt_ref, inner_ref, arrived, left,
):
    number = pl.program_id(0)
    step = pl.num_programs(0) - 1 - number
    heads = q_ref.shape[0]
    block = q_ref.shape[1]
    rows = pl.ds(pl.multiple_of(step * block, block), block)

    @pl.when(number == 0)
    def _():
        copies(
            [(g, rank_rows(g_ref, ranks[b], g)) for b, g in enumerate((g0, g1, g2, g3))]
            + [(x, rank_rows(x_ref, ranks[b], x)) for b, x in enumerate((x0, x1, x2, x3))],
            arrived,
        )
        dk_ref[...] = jnp.zeros_like(dk_ref)
        dv_ref[...] = jnp.zeros_like(dv_ref)
        wgrad_ref[...] = jnp.zeros_like(wgrad_ref)
        pgrad_ref[...] = jnp.zeros_like(pgrad_ref)

    upstream = g_ref[rows, :]
    outer = matmul(upstream, proj_ref[...], ((1,), (1,)))
    low = outer.astype(jnp.bfloat16)
    turned = outer.T.astype(jnp.bfloat16)
    for head in range(heads):
        part = slice(head * HEAD_DIM, (head + 1) * HEAD_DIM)
        out_ref[head] = low[:, part]
        outt_ref[head] = turned[part]
        inner_ref[head] = jnp.sum(
            turned[part].astype(jnp.float32) * ctx_ref[part].astype(jnp.float32),
            axis=0,
            keepdims=True,
        )
    pgrad_ref[...] += matmul(ctx_ref[...], upstream)
    dqt_ref[...] = jnp.zeros_like(dqt_ref)
    prompt = ranges[4, step]
    scale = LOG2E * HEAD_DIM ** (-0.5)

    def visit(key, masked):
        place = pl.ds(pl.multiple_of(key * block, block), block)
        if masked:
            key_at = key * block + lax.broadcasted_iota(jnp.int32, (block, block), 0)
            query_at = step * block + lax.broadcasted_iota(jnp.int32, (block, block), 1)
            seen = (key_at <= query_at) & ((key_at < prompt) | (key_at >= start_ref[...]))
        made = [
            (
                matmul(k_ref[head, place, :], qt_ref[head]),
                matmul(v_ref[head, place, :], outt_ref[head]),
            )
            for head in range(heads)
        ]
        for head in range(heads):
            scores, dprob = made[head]
            scores = scores * scale
            if masked:
                scores = jnp.where(seen, scores, NEGATIVE)
            prob = jnp.exp2(scores - lse_ref[head])
            dscore = (prob * (dprob - inner_ref[head])).astype(jnp.bfloat16)
            made[head] = prob.astype(jnp.bfloat16), dscore
        for head in range(heads):
            prob, dscore = made[head]
            dv_ref[head, place, :] += matmul(prob, out_ref[head])
            dk_ref[head, place, :] += matmul(dscore, q_ref[head])
            dqt_ref[head] += matmul(kt_ref[key, head], dscore)

    def plain(key, carry):
        visit(key, False)
        return carry

    def edge(key, carry):
        visit(key, True)
        return carry

    lax.fori_loop(0, ranges[0, step], plain, 0)
    lax.fori_loop(ranges[0, step], ranges[1, step], edge, 0)
    lax.fori_loop(ranges[2, step], ranges[3, step], edge, 0)
    small = HEAD_DIM ** (-0.5)
    x = x_ref[rows, :]
    total = None
    for kind in range(3):
        if kind == 0:
            grad = jnp.concatenate([dqt_ref[head] for head in range(heads)], axis=0).T * small
        elif kind == 1:
            grad = jnp.concatenate([dk_ref[head, rows, :] for head in range(heads)], axis=1) * small
        else:
            grad = jnp.concatenate([dv_ref[head, rows, :] for head in range(heads)], axis=1)
        grad = grad.astype(jnp.bfloat16)
        wgrad_ref[kind] += matmul(x, grad, ((0,), (0,)))
        term = matmul(grad, w_ref[kind], ((1,), (1,)))
        total = term if total is None else total + term
    part_ref[rows, :] = total.astype(jnp.bfloat16)
    send_ranks(part_ref, (p0, p1, p2, p3), ranks, left, step * block, block, True)

    @pl.when(step == 0)
    def _():
        weights_ref[:3] = wgrad_ref[...].astype(jnp.bfloat16)
        weights_ref[3] = pgrad_ref[...].T.astype(jnp.bfloat16)
        await_ranks(part_ref, (p0, p1, p2, p3), ranks, left)


def attention_backward(ranges, start, ranks, upstream, x, saved, w, proj):
    q, qt, k, kt, v, ctx, lse = saved
    tokens, width = start.shape[1], x[0].shape[1]
    local = w.shape[2]
    heads = local // HEAD_DIM
    block = BLOCK
    count = tokens // block
    low = jnp.bfloat16

    def at(i):
        return count - 1 - i

    head_rows = pl.BlockSpec((heads, tokens, HEAD_DIM), lambda i, r, n: (0, 0, 0))
    flops = 2 * tokens * width * local * 8 + tokens * tokens * local * 5
    return pl.pallas_call(
        backward_kernel,
        grid_spec=pltpu.PrefetchScalarGridSpec(
            num_scalar_prefetch=2,
            grid=(count,),
            in_specs=[
                *[HBM] * 8,
                pl.BlockSpec((local, block), lambda i, r, n: (0, at(i))),
                pl.BlockSpec((heads, 1, block), lambda i, r, n: (0, 0, at(i))),
                pl.BlockSpec((heads, block, HEAD_DIM), lambda i, r, n: (0, at(i), 0)),
                pl.BlockSpec((heads, HEAD_DIM, block), lambda i, r, n: (0, 0, at(i))),
                pl.BlockSpec((1, block), lambda i, r, n: (0, at(i))),
                head_rows,
                pl.BlockSpec((count, heads, HEAD_DIM, block), lambda i, r, n: (0, 0, 0, 0)),
                head_rows,
                pl.BlockSpec((3, width, local), lambda i, r, n: (0, 0, 0)),
                pl.BlockSpec((local, width), lambda i, r, n: (0, 0)),
            ],
            out_specs=[
                *[HBM] * 4,
                pl.BlockSpec((4, width, local), lambda i, r, n: (0, 0, 0)),
            ],
            scratch_shapes=[
                pltpu.VMEM((tokens, width), low),
                pltpu.VMEM((tokens, width), low),
                pltpu.VMEM((tokens, width), low),
                pltpu.VMEM((3, width, local), jnp.float32),
                pltpu.VMEM((local, width), jnp.float32),
                pltpu.VMEM((heads, tokens, HEAD_DIM), jnp.float32),
                pltpu.VMEM((heads, tokens, HEAD_DIM), jnp.float32),
                pltpu.VMEM((heads, HEAD_DIM, block), jnp.float32),
                pltpu.VMEM((heads, block, HEAD_DIM), low),
                pltpu.VMEM((heads, HEAD_DIM, block), low),
                pltpu.VMEM((heads, 1, block), jnp.float32),
                pltpu.SemaphoreType.DMA((8,)),
                pltpu.SemaphoreType.DMA((4,)),
            ],
        ),
        out_shape=[
            *[jax.ShapeDtypeStruct(x[0].shape, low)] * 4,
            jax.ShapeDtypeStruct((4, width, local), low),
        ],
        compiler_params=pltpu.CompilerParams(vmem_limit_bytes=56 << 20),
        cost_estimate=pl.CostEstimate(
            flops=4 * flops, transcendentals=tokens * tokens * heads // 2, bytes_accessed=40 << 20
        ),
        name="attention_backward",
    )(ranges, ranks, *upstream, *x, ctx, lse, q, qt, start, k, kt, v, w, proj)


def route_rows(route, priority, experts, capacity, row_count, ranks):
    own_start = ranks[0] * row_count
    own_route = lax.dynamic_slice_in_dim(route, own_start, row_count, 0)
    own_priority = lax.dynamic_slice_in_dim(priority, own_start, row_count, 0)
    ahead = (route[None, :] == own_route[:, None]) & (priority[None, :] < own_priority[:, None])
    kept = jnp.sum(ahead.astype(jnp.int32), axis=1) < capacity
    kinds = jnp.arange(experts, dtype=jnp.int32)
    block_hot = (route.reshape(-1, row_count)[:, :, None] == kinds).astype(jnp.int32)
    lengths = (jnp.sum(block_hot, axis=1) + ALIGN - 1) // ALIGN * ALIGN
    starts = jnp.cumsum(lengths, axis=1) - lengths
    own_hot = (own_route[:, None] == kinds).astype(jnp.int32)
    index = jnp.arange(row_count, dtype=jnp.int32)
    before = (own_route[None, :] == own_route[:, None]) & (index[None, :] < index[:, None])
    own_starts = lax.dynamic_slice_in_dim(starts, ranks[0], 1, 0)
    place = jnp.sum(before.astype(jnp.int32), axis=1) + jnp.sum(own_hot * own_starts, axis=1)
    slots = jnp.arange(row_count + experts * ALIGN, dtype=jnp.int32)
    order = (slots[:, None] == place[None, :]).astype(jnp.bfloat16)
    picked = [
        lax.dynamic_slice_in_dim(array, ranks[b], 1, 0)[0]
        for array in (starts, lengths)
        for b in range(4)
    ]
    home = at_home().astype(jnp.int32)[None]
    return (kept, order, jnp.concatenate([*picked, home]), own_hot)


def sort_rows(order, rows):
    return jnp.dot(order, rows, preferred_element_type=jnp.float32).astype(jnp.bfloat16)


def unsort_rows(order, rows):
    return matmul(order, rows.astype(jnp.bfloat16), ((0,), (0,)))


def each_tile(table, expert, experts, visit):
    for block in range(4):
        start = table[block * experts + expert]
        length = table[(4 + block) * experts + expert]

        def tile(number, carry, block=block, start=start, length=length):
            place = pl.ds(pl.multiple_of(start + number * TILE, ALIGN), TILE)
            visit(block, place, length - number * TILE)
            return carry

        lax.fori_loop(0, (length + TILE - 1) // TILE, tile, 0)


def fetch_weights(choice, kept, given, targets, semaphores):
    for place, target in enumerate(targets):
        for expert in range(target.shape[0]):
            ready = semaphores.at[place, expert]

            @pl.when(choice == 1)
            def _(place=place, target=target, expert=expert, ready=ready):
                pltpu.make_async_copy(kept[place].at[expert], target.at[expert], ready).start()

            @pl.when(choice == 0)
            def _(place=place, target=target, expert=expert, ready=ready):
                pltpu.make_async_copy(given[place].at[expert], target.at[expert], ready).start()


def await_weights(kept, targets, expert, semaphores):
    for place, target in enumerate(targets):
        pltpu.make_async_copy(
            kept[place].at[expert], target.at[expert], semaphores.at[place, expert]
        ).wait()


def within(rows, left):
    return jnp.where(lax.broadcasted_iota(jnp.int32, rows.shape, 0) < left, rows, 0)


def moe_forward_kernel(
    table, x0, x1, x2, x3, own_up, own_down, new_up, new_down,
    y0, y1, y2, y3, hidden_out, slope_out,
    x_ref, y_ref, hidden_ref, slope_ref, up_ref, down_ref, semaphores, ready,
):
    expert = pl.program_id(0)
    experts = pl.num_programs(0)
    count = x0.shape[0]
    kept, given, held = (own_up, own_down), (new_up, new_down), (up_ref, down_ref)

    @pl.when(expert == 0)
    def _():
        fetch_weights(table[8 * experts], kept, given, held, ready)
        for ref in (hidden_ref, slope_ref, y_ref):
            ref[...] = jnp.zeros_like(ref)
        x_ref[:, count:, :] = jnp.zeros((4, TILE, x_ref.shape[2]), jnp.bfloat16)
        copies([(x, x_ref.at[b, :count]) for b, x in enumerate((x0, x1, x2, x3))], semaphores)

    await_weights(kept, held, expert, ready)

    def visit(block, place, left):
        u = matmul(x_ref[block, place, :], up_ref[expert])
        bend = jnp.tanh(0.7978845608028654 * (u + 0.044715 * u * u * u))
        hidden = (0.5 * u * (1.0 + bend)).astype(jnp.bfloat16)
        slope = 0.5 * (1.0 + bend) + 0.5 * u * (1.0 - bend * bend) * (
            0.7978845608028654 * (1.0 + 3.0 * 0.044715 * u * u)
        )
        hidden_ref[block, place, :] = hidden
        slope_ref[block, place, :] = slope.astype(jnp.bfloat16)
        y_ref[block, place, :] = matmul(hidden, down_ref[expert]).astype(jnp.bfloat16)

    each_tile(table, expert, experts, visit)

    @pl.when(expert == experts - 1)
    def _():
        copies(
            [(y_ref.at[b, :count], y) for b, y in enumerate((y0, y1, y2, y3))]
            + [(hidden_ref, hidden_out), (slope_ref, slope_out)],
            semaphores,
        )


def moe_backward_kernel(
    table, d0, d1, d2, d3, slope_in, own_up, own_down, new_up, new_down,
    y0, y1, y2, y3, grad_out,
    d_ref, slope_ref, y_ref, grad_ref, up_ref, down_ref, semaphores, ready,
):
    expert = pl.program_id(0)
    experts = pl.num_programs(0)
    count = d0.shape[0]
    kept, given, held = (own_up, own_down), (new_up, new_down), (up_ref, down_ref)

    @pl.when(expert == 0)
    def _():
        fetch_weights(table[8 * experts], kept, given, held, ready)
        for ref in (grad_ref, y_ref):
            ref[...] = jnp.zeros_like(ref)
        d_ref[:, count:, :] = jnp.zeros((4, TILE, d_ref.shape[2]), jnp.bfloat16)
        copies(
            [(d, d_ref.at[b, :count]) for b, d in enumerate((d0, d1, d2, d3))]
            + [(slope_in, slope_ref)],
            semaphores,
        )

    await_weights(kept, held, expert, ready)

    def visit(block, place, left):
        upstream = within(d_ref[block, place, :], left)
        slope = slope_ref[block, place, :].astype(jnp.float32)
        grad = (matmul(upstream, down_ref[expert], ((1,), (1,))) * slope).astype(jnp.bfloat16)
        grad_ref[block, place, :] = grad
        y_ref[block, place, :] = matmul(grad, up_ref[expert], ((1,), (1,))).astype(jnp.bfloat16)

    each_tile(table, expert, experts, visit)

    @pl.when(expert == experts - 1)
    def _():
        copies(
            [(y_ref.at[b, :count], y) for b, y in enumerate((y0, y1, y2, y3))]
            + [(grad_ref, grad_out)],
            semaphores,
        )


def moe_weights_kernel(
    table, x0, x1, x2, x3, d0, d1, d2, d3, hidden_in, grad_in,
    out_ref,
    x_ref, d_ref, hidden_ref, grad_ref, up_sum, down_sum, semaphores,
):
    expert = pl.program_id(0)
    experts = pl.num_programs(0)
    count = x0.shape[0]

    @pl.when(expert == 0)
    def _():
        for ref in (x_ref, d_ref):
            ref[:, count:, :] = jnp.zeros((4, TILE, ref.shape[2]), jnp.bfloat16)
        copies(
            [(x, x_ref.at[b, :count]) for b, x in enumerate((x0, x1, x2, x3))]
            + [(d, d_ref.at[b, :count]) for b, d in enumerate((d0, d1, d2, d3))]
            + [(hidden_in, hidden_ref), (grad_in, grad_ref)],
            semaphores,
        )

    up_sum[...] = jnp.zeros_like(up_sum)
    down_sum[...] = jnp.zeros_like(down_sum)

    def visit(block, place, left):
        up_sum[...] += matmul(
            x_ref[block, place, :], within(grad_ref[block, place, :], left), ((0,), (0,))
        )
        down_sum[...] += matmul(
            within(d_ref[block, place, :], left), hidden_ref[block, place, :], ((0,), (0,))
        )

    each_tile(table, expert, experts, visit)
    out_ref[0, 0] = up_sum[...].astype(jnp.bfloat16)
    out_ref[1, 0] = down_sum[...].astype(jnp.bfloat16)


def moe_call(kernel, name, table, arrays, outs, scratch, sums, experts, cost):
    low = jnp.bfloat16
    specs = [HBM] * len(outs)
    ready = [pltpu.SemaphoreType.DMA((2, experts))]
    if sums:
        specs = [pl.BlockSpec((2, 1) + outs[0][2:], lambda e, t: (0, e, 0, 0))]
        ready = []
    return pl.pallas_call(
        kernel,
        grid_spec=pltpu.PrefetchScalarGridSpec(
            num_scalar_prefetch=1,
            grid=(experts,),
            in_specs=[HBM] * len(arrays),
            out_specs=specs,
            scratch_shapes=[
                *[pltpu.VMEM(shape, low) for shape in scratch],
                *[pltpu.VMEM(shape, jnp.float32) for shape in sums],
                pltpu.SemaphoreType.DMA((10,)),
                *ready,
            ],
        ),
        out_shape=[jax.ShapeDtypeStruct(shape, low) for shape in outs],
        compiler_params=pltpu.CompilerParams(vmem_limit_bytes=58 << 20),
        cost_estimate=pl.CostEstimate(flops=cost, transcendentals=0, bytes_accessed=40 << 20),
        name=name,
    )(table, *arrays)


def moe_forward(table, x, own, new):
    count, width = x[0].shape
    experts, _, hidden = own[0].shape
    wide, tall = (4, count + TILE, width), (4, count + TILE, hidden)
    *y, hid, slope = moe_call(
        moe_forward_kernel, "moe_forward", table, [*x, *own, *new],
        [(count, width)] * 4 + [tall, tall],
        [wide, wide, tall, tall, own[0].shape, own[1].shape], [], experts,
        20 * count * width * hidden,
    )
    return (y, hid, slope)


def moe_backward(table, d, slope, own, new):
    count, width = d[0].shape
    experts, _, hidden = own[0].shape
    wide, tall = (4, count + TILE, width), (4, count + TILE, hidden)
    *y, grad = moe_call(
        moe_backward_kernel, "moe_backward", table, [*d, slope, *own, *new],
        [(count, width)] * 4 + [tall],
        [wide, tall, wide, tall, own[0].shape, own[1].shape], [], experts,
        20 * count * width * hidden,
    )
    return (y, grad)


def moe_weights(table, x, d, hid, grad, experts):
    count, width = x[0].shape
    hidden = hid.shape[2]
    wide, tall = (4, count + TILE, width), (4, count + TILE, hidden)
    return moe_call(
        moe_weights_kernel, "moe_weights", table, [*x, *d, hid, grad],
        [(2, experts, width, hidden)], [wide, wide, tall, tall], [(width, hidden)] * 2, experts,
        20 * count * width * hidden,
    )[0]


def at_home():
    return lax.axis_index("c") == lax.axis_index("zh")


def swap_roles(value):
    moved = lax.ppermute(value, ("c", "zh"), [(1, 2), (2, 1)])
    return jnp.where(at_home(), value, moved)


def flip(value, axis):
    return lax.ppermute(value, axis, [(0, 1), (1, 0)])


def gather_blocks(rows):
    across = flip(rows, "zl")
    return [rows, flip(rows, "c"), across, flip(across, "c")]


def scatter_blocks(blocks):
    own, beside, across, corner = blocks
    far = flip(corner, "c").astype(jnp.float32)
    far = flip((far + across.astype(jnp.float32)).astype(own.dtype), "zl").astype(jnp.float32)
    return own.astype(jnp.float32) + flip(beside, "c").astype(jnp.float32) + far


def halve(value, axis, dimension):
    count = value.shape[dimension] // 2
    side = lax.axis_index(axis)
    kept = lax.dynamic_slice_in_dim(value, side * count, count, dimension)
    sent = lax.dynamic_slice_in_dim(value, (1 - side) * count, count, dimension)
    total = kept.astype(jnp.float32) + flip(sent, axis).astype(jnp.float32)
    return total.astype(value.dtype)


def sum_home(value, dimension):
    count = value.shape[dimension] // 2
    high = lax.axis_index("zh")
    straight = lax.dynamic_slice_in_dim(value, high * count, count, dimension)
    turned = lax.dynamic_slice_in_dim(value, (1 - high) * count, count, dimension)
    turned = lax.ppermute(turned, ("c", "zh"), [(0, 2), (1, 0), (2, 3), (3, 1)])
    return swap_roles(straight).astype(jnp.float32) + turned.astype(jnp.float32)


def other_quarter(weight, users):
    flat = weight.reshape(-1, weight.shape[-1])
    part = flat.shape[0] // lax.axis_size(users)
    piece = lax.dynamic_slice_in_dim(flat, lax.axis_index(users) * part, part, 0)
    piece = flip(piece, "zh")
    return lax.all_gather(piece, users, axis=0, tiled=True).reshape(weight.shape)


def body(
    high_bits,
    block_input,
    attention_gain,
    qkv_weight,
    proj_weight,
    moe_gain,
    centroids,
    expert_up,
    expert_down,
    out_grad,
    routes,
    priority,
    segments,
):
    row_count = block_input.shape[1]
    model_width = block_input.shape[2]
    experts = expert_up.shape[0]
    token_count = segments.shape[1]
    capacity = 9 * token_count // (8 * experts)
    local_width = qkv_weight.shape[2]
    users = (*high_bits, "c")
    core, near = lax.axis_index("c"), lax.axis_index("zl")
    ranks = jnp.stack(
        [2 * core + near, 2 * (1 - core) + near, 2 * core + 1 - near, 3 - 2 * core - near]
    )
    indices = jnp.stack([routes[0, :, 0], priority[0], segments[0]])
    indices = jnp.where(at_home(), indices, flip(indices, "c"))
    segment = indices[2]
    held = swap_roles(block_input[0])
    small = jnp.concatenate([qkv_weight, proj_weight.reshape(1, model_width, local_width)], axis=0)
    small = jnp.where(at_home(), small, other_quarter(small, users))
    qkv_used, proj_used = small[:3], small[3].reshape(local_width, model_width)
    own_experts = (expert_up, expert_down)
    expert_up, expert_down, held = lax.optimization_barrier((expert_up, expert_down, held))
    new_experts = [other_quarter(weight, users) for weight in (expert_up, expert_down)]
    inputs = held.astype(jnp.float32)
    unit_one, inverse_one = normalize_plain(inputs)
    normed_one_rows = (unit_one * attention_gain).astype(jnp.bfloat16)
    normed_one = gather_blocks(normed_one_rows)
    *attended, q, qt, k, kt, v, ctx, lse = attention_forward(
        *key_ranges(segment, QUERY_BLOCK), ranks, normed_one, qkv_used, proj_used
    )
    saved = (q, qt, k, kt, v, ctx, lse)
    upstream = swap_roles(out_grad[0]).astype(jnp.float32)
    kept_rows, order, table, hot_rows = route_rows(
        indices[0], indices[1], experts, capacity, row_count, ranks
    )
    attended = scatter_blocks(attended)
    mixed_one = inputs + attended
    unit_two, inverse_two = normalize_plain(mixed_one)
    normed_two_rows = (unit_two * moe_gain).astype(jnp.bfloat16)
    centroid_rows = jnp.dot(
        hot_rows.astype(jnp.bfloat16), centroids, preferred_element_type=jnp.float32
    )
    normed_two_float = normed_two_rows.astype(jnp.float32)
    gate_prob = jax.nn.sigmoid(jnp.sum(normed_two_float * centroid_rows, axis=-1))
    gate_used = jnp.where(kept_rows, gate_prob, 0.0)
    grad_eo_rows = (gate_used[:, None] * upstream).astype(jnp.bfloat16)
    dispatched = gather_blocks(sort_rows(order, normed_two_rows))
    grad_sorted = sort_rows(order, grad_eo_rows)
    grad_sorted, *dispatched = lax.optimization_barrier((grad_sorted, *dispatched))
    grad_dispatched = gather_blocks(grad_sorted)
    returned, hidden, slope = moe_forward(table, dispatched, own_experts, new_experts)
    expert_out = unsort_rows(order, scatter_blocks(returned))
    mixed_two = mixed_one + gate_used[:, None] * expert_out
    block_output = swap_roles(mixed_two.astype(jnp.bfloat16))[None]
    grad_gate = jnp.where(kept_rows, jnp.sum(upstream * expert_out, axis=-1), 0.0)
    grad_score = grad_gate * gate_prob * (1.0 - gate_prob)
    back_moe, grad_upward = moe_backward(table, grad_dispatched, slope, own_experts, new_experts)
    expert_part = moe_weights(table, dispatched, grad_dispatched, hidden, grad_upward, experts)
    grad_two = unsort_rows(order, scatter_blocks(back_moe)) + grad_score[:, None] * centroid_rows
    centroid_part = jnp.einsum(
        "te,td->ed",
        hot_rows.astype(jnp.float32),
        grad_score[:, None] * normed_two_float,
        precision=highest,
    )
    moe_gain_part = jnp.sum(grad_two * unit_two, axis=0)
    grad_mixed = upstream + normalize_back(grad_two, unit_two, inverse_two, moe_gain)
    grad_att = gather_blocks(grad_mixed.astype(jnp.bfloat16))
    *grad_one, weights_part = attention_backward(
        *key_ranges(segment, BLOCK), ranks, grad_att, normed_one, saved, qkv_used, proj_used
    )
    grad_one = scatter_blocks(grad_one)
    input_grad = swap_roles(
        (grad_mixed + normalize_back(grad_one, unit_one, inverse_one, attention_gain)).astype(
            jnp.bfloat16
        )
    )[None]

    expert_part = lax.psum_scatter(expert_part, high_bits, scatter_dimension=2, tiled=True)
    expert_summed = sum_home(expert_part, 2)
    up_summed, down_summed = expert_summed[0], jnp.swapaxes(expert_summed[1], 1, 2)
    for bit in high_bits:
        weights_part = halve(weights_part, bit, 1)
    weights_part = sum_home(weights_part, 1)
    qkv_summed, proj_summed = weights_part[:3], weights_part[3].T
    early = jnp.concatenate([moe_gain_part[None], centroid_part], axis=0)
    for bit in (*users, "zh", "zl"):
        early = halve(early, bit, 1)
    gain_two_sum, centroid_sum = early[0], early[1:]
    slice_rows = qkv_summed.shape[1]
    own_rows = lax.dynamic_slice_in_dim(
        qkv_weight, lax.axis_index(users) * slice_rows, slice_rows, 1
    )
    gain_one = jnp.sum(own_rows.astype(jnp.float32) * qkv_summed, axis=(0, 2))
    for bit in ("zh", "zl"):
        gain_one = halve(gain_one, bit, 0)
    share = gain_one.shape[0]
    own_gain = lax.axis_index((*users, "zh", "zl")) * share
    gain_one_sum = gain_one / lax.dynamic_slice_in_dim(attention_gain, own_gain, share, 0)
    return (
        block_output,
        input_grad,
        gain_one_sum,
        gain_two_sum,
        centroid_sum,
        qkv_summed,
        proj_summed,
        up_summed,
        down_summed,
    )


def solution(mesh):
    shape = mesh.devices.shape
    high_bits = tuple(f"u{place}" for place in range((shape[0] // 2).bit_length() - 1))
    dp, tensor = (*high_bits, "c"), ("zh", "zl")
    mesh = Mesh(mesh.devices.reshape((2,) * len(dp + tensor)), dp + tensor)

    def program(*arguments):
        return body(high_bits, *arguments)

    return jax.shard_map(
        program,
        mesh=mesh,
        in_specs=(
            P(dp, tensor, None),
            P(),
            P(None, None, tensor),
            P(tensor, None),
            P(),
            P(),
            P(None, None, tensor),
            P(None, tensor, None),
            P(dp, tensor, None),
            P(dp, None, None),
            P(dp, None),
            P(dp, None),
        ),
        out_specs=(
            P(dp, tensor, None),
            P(dp, tensor, None),
            P(dp + tensor),
            P(dp + tensor),
            P(None, dp + tensor),
            P(None, dp, tensor),
            P(tensor, dp),
            P(None, dp, tensor),
            P(None, tensor, dp),
        ),
        check_vma=False,
    )
```

```python
import jax
import jax.numpy as jnp
from jax import lax
from jax.experimental import pallas as pl
from jax.experimental.pallas import tpu as pltpu
from jax.sharding import Mesh
from jax.sharding import PartitionSpec as P

HEAD_DIM = 64
QUERY_BLOCK = 512
BLOCK = 256
LOG2E = 1.4426950408889634
NEGATIVE = -1e30
TILE = 256
ALIGN = 16
CONTINUATIONS = 8
HBM = pl.BlockSpec(memory_space=pl.ANY)

epsilon = 1e-05
highest = lax.Precision.HIGHEST


def normalize_plain(values):
    centered = values - jnp.mean(values, axis=-1, keepdims=True)
    variance = jnp.mean(centered * centered, axis=-1, keepdims=True)
    inverse = lax.rsqrt(variance + epsilon)
    return (centered * inverse, inverse)


def normalize_back(upstream, unit_rows, inverse, gain_row):
    scaled = upstream * gain_row
    centered = scaled - jnp.mean(scaled, axis=-1, keepdims=True)
    return inverse * (centered - unit_rows * jnp.mean(scaled * unit_rows, axis=-1, keepdims=True))


def matmul(a, b, dims=((1,), (0,))):
    return lax.dot_general(a, b, (dims, ((), ())), preferred_element_type=jnp.float32)


def key_ranges(segment, block):
    token_count = segment.shape[0]
    numbers = jnp.arange(1, CONTINUATIONS + 1, dtype=jnp.int32)[:, None]
    earlier = jnp.sum((segment[None, :] < numbers).astype(jnp.int32), axis=1, keepdims=True)
    prompt = earlier[0, 0]
    start = jnp.sum(jnp.where(segment[None, :] == numbers, earlier, 0), axis=0)
    first = jnp.arange(token_count // block, dtype=jnp.int32) * block
    whole = jnp.minimum(prompt, first) // block
    shared = (jnp.minimum(prompt, first + block) + block - 1) // block
    own = jnp.maximum(shared, start.reshape(-1, block)[:, 0] // block)
    last = first // block + 1
    return (jnp.stack([whole, shared, own, last, jnp.full_like(whole, prompt)]), start[None, :])


def copies(pairs, semaphores):
    moved = [
        pltpu.make_async_copy(source, target, semaphores.at[place])
        for place, (source, target) in enumerate(pairs)
    ]
    for copy in moved:
        copy.start()
    for copy in moved:
        copy.wait()


def rank_rows(ref, rank, like):
    count = like.shape[0]
    return ref.at[pl.ds(pl.multiple_of(rank * count, count), count)]


def send_ranks(ref, targets, ranks, semaphores, edge, block, down):
    count = targets[0].shape[0]
    for rank in range(4):
        if down:
            first = rank * count
            due = (edge <= first) & (edge + block > first)
        else:
            last = (rank + 1) * count
            due = (edge >= last) & (edge - block < last)

        @pl.when(due)
        def _(rank=rank):
            for b, target in enumerate(targets):

                @pl.when(ranks[b] == rank)
                def _(b=b, target=target):
                    source = ref.at[rank * count : (rank + 1) * count]
                    pltpu.make_async_copy(source, target, semaphores.at[b]).start()


def await_ranks(ref, targets, ranks, semaphores):
    for b, target in enumerate(targets):
        pltpu.make_async_copy(rank_rows(ref, ranks[b], target), target, semaphores.at[b]).wait()


def forward_kernel(
    ranges, ranks, x0, x1, x2, x3, w_ref, proj_ref, start_ref,
    p0, p1, p2, p3, q_ref, qt_ref, k_ref, kt_ref, v_ref, ctx_ref, lse_ref,
    x_ref, part_ref, vt_ref, score_ref, top_ref, sum_ref, arrived, left,
):
    step = pl.program_id(0)
    heads = q_ref.shape[0]
    block = q_ref.shape[1]
    rows = pl.ds(pl.multiple_of(step * block, block), block)

    @pl.when(step == 0)
    def _():
        copies(
            [(x, rank_rows(x_ref, ranks[b], x)) for b, x in enumerate((x0, x1, x2, x3))], arrived
        )

    x = x_ref[rows, :]
    kinds = []
    for kind in range(3):
        made = matmul(x, w_ref[kind])
        kinds.append((made.astype(jnp.bfloat16), made.T.astype(jnp.bfloat16)))
    for head in range(heads):
        part = slice(head * HEAD_DIM, (head + 1) * HEAD_DIM)
        q_ref[head] = kinds[0][0][:, part]
        k_ref[head, rows, :] = kinds[1][0][:, part]
        v_ref[head, rows, :] = kinds[2][0][:, part]
        qt_ref[head] = kinds[0][1][part]
        for piece in range(kt_ref.shape[0]):
            columns = slice(piece * kt_ref.shape[3], (piece + 1) * kt_ref.shape[3])
            kt_ref[piece, head] = kinds[1][1][part, columns]
        vt_ref[step, head, :HEAD_DIM] = kinds[2][1][part]
        vt_ref[step, head, HEAD_DIM:] = jnp.ones((16, block), jnp.bfloat16)
    top_ref[...] = jnp.full_like(top_ref, NEGATIVE)
    sum_ref[...] = jnp.zeros_like(sum_ref)
    prompt = ranges[4, step]
    scale = LOG2E * HEAD_DIM ** (-0.5)

    def visit(key, masked):
        place = pl.ds(pl.multiple_of(key * block, block), block)
        if masked:
            key_at = key * block + lax.broadcasted_iota(jnp.int32, (block, block), 0)
            query_at = step * block + lax.broadcasted_iota(jnp.int32, (block, block), 1)
            seen = (key_at <= query_at) & ((key_at < prompt) | (key_at >= start_ref[...]))
        for head in range(heads):
            scores = matmul(k_ref[head, place, :], qt_ref[head])
            if masked:
                scores = jnp.where(seen, scores, NEGATIVE)
            score_ref[key, head] = scores
            top_ref[head] = jnp.maximum(
                top_ref[head], jnp.max(scores.reshape(block // 8, 8, block), axis=0)
            )

    def plain(key, carry):
        visit(key, False)
        return carry

    def edge(key, carry):
        visit(key, True)
        return carry

    lax.fori_loop(0, ranges[0, step], plain, 0)
    lax.fori_loop(ranges[0, step], ranges[1, step], edge, 0)
    lax.fori_loop(ranges[2, step], ranges[3, step], edge, 0)
    for head in range(heads):
        top_ref[head, :1] = jnp.max(top_ref[head], axis=0, keepdims=True) * scale

    def add(key, carry):
        for head in range(heads):
            weights = jnp.exp2(score_ref[key, head] * scale - top_ref[head, :1])
            sum_ref[head] += matmul(vt_ref[key, head], weights.astype(jnp.bfloat16))
        return carry

    lax.fori_loop(0, ranges[1, step], add, 0)
    lax.fori_loop(ranges[2, step], ranges[3, step], add, 0)
    for head in range(heads):
        total = sum_ref[head, HEAD_DIM : HEAD_DIM + 1]
        context = sum_ref[head, :HEAD_DIM] / total
        ctx_ref[head * HEAD_DIM : (head + 1) * HEAD_DIM] = context.astype(jnp.bfloat16)
        lse_ref[head] = top_ref[head, :1] + jnp.log(total) * LOG2E
    part_ref[rows, :] = matmul(ctx_ref[...], proj_ref[...], ((0,), (0,))).astype(jnp.bfloat16)
    send_ranks(part_ref, (p0, p1, p2, p3), ranks, left, (step + 1) * block, block, False)

    @pl.when(step == pl.num_programs(0) - 1)
    def _():
        await_ranks(part_ref, (p0, p1, p2, p3), ranks, left)


def attention_forward(ranges, start, ranks, x, w, proj):
    tokens, width = start.shape[1], x[0].shape[1]
    local = w.shape[2]
    heads = local // HEAD_DIM
    block = QUERY_BLOCK
    fine = BLOCK
    count = tokens // block
    low = jnp.bfloat16
    head_rows = pl.BlockSpec((heads, tokens, HEAD_DIM), lambda i, r, n: (0, 0, 0))
    flops = 2 * tokens * width * local * 4 + tokens * tokens * local * 2
    return pl.pallas_call(
        forward_kernel,
        grid_spec=pltpu.PrefetchScalarGridSpec(
            num_scalar_prefetch=2,
            grid=(count,),
            in_specs=[
                *[HBM] * 4,
                pl.BlockSpec((3, width, local), lambda i, r, n: (0, 0, 0)),
                pl.BlockSpec((local, width), lambda i, r, n: (0, 0)),
                pl.BlockSpec((1, block), lambda i, r, n: (0, i)),
            ],
            out_specs=[
                *[HBM] * 4,
                pl.BlockSpec((heads, block, HEAD_DIM), lambda i, r, n: (0, i, 0)),
                pl.BlockSpec((heads, HEAD_DIM, block), lambda i, r, n: (0, 0, i)),
                head_rows,
                pl.BlockSpec((block // fine, heads, HEAD_DIM, fine), lambda i, r, n: (i, 0, 0, 0)),
                head_rows,
                pl.BlockSpec((local, block), lambda i, r, n: (0, i)),
                pl.BlockSpec((heads, 1, block), lambda i, r, n: (0, 0, i)),
            ],
            scratch_shapes=[
                pltpu.VMEM((tokens, width), low),
                pltpu.VMEM((tokens, width), low),
                pltpu.VMEM((count, heads, HEAD_DIM + 16, block), low),
                pltpu.VMEM((count, heads, block, block), jnp.float32),
                pltpu.VMEM((heads, 8, block), jnp.float32),
                pltpu.VMEM((heads, HEAD_DIM + 16, block), jnp.float32),
                pltpu.SemaphoreType.DMA((4,)),
                pltpu.SemaphoreType.DMA((4,)),
            ],
        ),
        out_shape=[
            *[jax.ShapeDtypeStruct(x[0].shape, low)] * 4,
            jax.ShapeDtypeStruct((heads, tokens, HEAD_DIM), low),
            jax.ShapeDtypeStruct((heads, HEAD_DIM, tokens), low),
            jax.ShapeDtypeStruct((heads, tokens, HEAD_DIM), low),
            jax.ShapeDtypeStruct((tokens // fine, heads, HEAD_DIM, fine), low),
            jax.ShapeDtypeStruct((heads, tokens, HEAD_DIM), low),
            jax.ShapeDtypeStruct((local, tokens), low),
            jax.ShapeDtypeStruct((heads, 1, tokens), jnp.float32),
        ],
        compiler_params=pltpu.CompilerParams(vmem_limit_bytes=56 << 20),
        cost_estimate=pl.CostEstimate(
            flops=4 * flops, transcendentals=tokens * tokens * heads // 2, bytes_accessed=40 << 20
        ),
        name="attention_forward",
    )(ranges, ranks, *x, w, proj, start)


def backward_kernel(
    ranges, ranks, g0, g1, g2, g3, x0, x1, x2, x3,
    ctx_ref, lse_ref, q_ref, qt_ref, start_ref, k_ref, kt_ref, v_ref, w_ref, proj_ref,
    p0, p1, p2, p3, weights_ref,
    g_ref, x_ref, part_ref, wgrad_ref, pgrad_ref,
    dk_ref, dv_ref, dqt_ref, out_ref, outt_ref, inner_ref, arrived, left,
):
    number = pl.program_id(0)
    step = pl.num_programs(0) - 1 - number
    heads = q_ref.shape[0]
    block = q_ref.shape[1]
    rows = pl.ds(pl.multiple_of(step * block, block), block)

    @pl.when(number == 0)
    def _():
        copies(
            [(g, rank_rows(g_ref, ranks[b], g)) for b, g in enumerate((g0, g1, g2, g3))]
            + [(x, rank_rows(x_ref, ranks[b], x)) for b, x in enumerate((x0, x1, x2, x3))],
            arrived,
        )
        dk_ref[...] = jnp.zeros_like(dk_ref)
        dv_ref[...] = jnp.zeros_like(dv_ref)
        wgrad_ref[...] = jnp.zeros_like(wgrad_ref)
        pgrad_ref[...] = jnp.zeros_like(pgrad_ref)

    upstream = g_ref[rows, :]
    outer = matmul(upstream, proj_ref[...], ((1,), (1,)))
    low = outer.astype(jnp.bfloat16)
    turned = outer.T.astype(jnp.bfloat16)
    for head in range(heads):
        part = slice(head * HEAD_DIM, (head + 1) * HEAD_DIM)
        out_ref[head] = low[:, part]
        outt_ref[head] = turned[part]
        inner_ref[head] = jnp.sum(
            turned[part].astype(jnp.float32) * ctx_ref[part].astype(jnp.float32),
            axis=0,
            keepdims=True,
        )
    pgrad_ref[...] += matmul(ctx_ref[...], upstream)
    dqt_ref[...] = jnp.zeros_like(dqt_ref)
    prompt = ranges[4, step]
    scale = LOG2E * HEAD_DIM ** (-0.5)

    def visit(key, masked):
        place = pl.ds(pl.multiple_of(key * block, block), block)
        if masked:
            key_at = key * block + lax.broadcasted_iota(jnp.int32, (block, block), 0)
            query_at = step * block + lax.broadcasted_iota(jnp.int32, (block, block), 1)
            seen = (key_at <= query_at) & ((key_at < prompt) | (key_at >= start_ref[...]))
        made = [
            (
                matmul(k_ref[head, place, :], qt_ref[head]),
                matmul(v_ref[head, place, :], outt_ref[head]),
            )
            for head in range(heads)
        ]
        for head in range(heads):
            scores, dprob = made[head]
            scores = scores * scale
            if masked:
                scores = jnp.where(seen, scores, NEGATIVE)
            prob = jnp.exp2(scores - lse_ref[head])
            dscore = (prob * (dprob - inner_ref[head])).astype(jnp.bfloat16)
            made[head] = prob.astype(jnp.bfloat16), dscore
        for head in range(heads):
            prob, dscore = made[head]
            dv_ref[head, place, :] += matmul(prob, out_ref[head])
            dk_ref[head, place, :] += matmul(dscore, q_ref[head])
            dqt_ref[head] += matmul(kt_ref[key, head], dscore)

    def plain(key, carry):
        visit(key, False)
        return carry

    def edge(key, carry):
        visit(key, True)
        return carry

    lax.fori_loop(0, ranges[0, step], plain, 0)
    lax.fori_loop(ranges[0, step], ranges[1, step], edge, 0)
    lax.fori_loop(ranges[2, step], ranges[3, step], edge, 0)
    small = HEAD_DIM ** (-0.5)
    x = x_ref[rows, :]
    total = None
    for kind in range(3):
        if kind == 0:
            grad = jnp.concatenate([dqt_ref[head] for head in range(heads)], axis=0).T * small
        elif kind == 1:
            grad = jnp.concatenate([dk_ref[head, rows, :] for head in range(heads)], axis=1) * small
        else:
            grad = jnp.concatenate([dv_ref[head, rows, :] for head in range(heads)], axis=1)
        grad = grad.astype(jnp.bfloat16)
        wgrad_ref[kind] += matmul(x, grad, ((0,), (0,)))
        term = matmul(grad, w_ref[kind], ((1,), (1,)))
        total = term if total is None else total + term
    part_ref[rows, :] = total.astype(jnp.bfloat16)
    send_ranks(part_ref, (p0, p1, p2, p3), ranks, left, step * block, block, True)

    @pl.when(step == 0)
    def _():
        weights_ref[:3] = wgrad_ref[...].astype(jnp.bfloat16)
        weights_ref[3] = pgrad_ref[...].T.astype(jnp.bfloat16)
        await_ranks(part_ref, (p0, p1, p2, p3), ranks, left)


def attention_backward(ranges, start, ranks, upstream, x, saved, w, proj):
    q, qt, k, kt, v, ctx, lse = saved
    tokens, width = start.shape[1], x[0].shape[1]
    local = w.shape[2]
    heads = local // HEAD_DIM
    block = BLOCK
    count = tokens // block
    low = jnp.bfloat16

    def at(i):
        return count - 1 - i

    head_rows = pl.BlockSpec((heads, tokens, HEAD_DIM), lambda i, r, n: (0, 0, 0))
    flops = 2 * tokens * width * local * 8 + tokens * tokens * local * 5
    return pl.pallas_call(
        backward_kernel,
        grid_spec=pltpu.PrefetchScalarGridSpec(
            num_scalar_prefetch=2,
            grid=(count,),
            in_specs=[
                *[HBM] * 8,
                pl.BlockSpec((local, block), lambda i, r, n: (0, at(i))),
                pl.BlockSpec((heads, 1, block), lambda i, r, n: (0, 0, at(i))),
                pl.BlockSpec((heads, block, HEAD_DIM), lambda i, r, n: (0, at(i), 0)),
                pl.BlockSpec((heads, HEAD_DIM, block), lambda i, r, n: (0, 0, at(i))),
                pl.BlockSpec((1, block), lambda i, r, n: (0, at(i))),
                head_rows,
                pl.BlockSpec((count, heads, HEAD_DIM, block), lambda i, r, n: (0, 0, 0, 0)),
                head_rows,
                pl.BlockSpec((3, width, local), lambda i, r, n: (0, 0, 0)),
                pl.BlockSpec((local, width), lambda i, r, n: (0, 0)),
            ],
            out_specs=[
                *[HBM] * 4,
                pl.BlockSpec((4, width, local), lambda i, r, n: (0, 0, 0)),
            ],
            scratch_shapes=[
                pltpu.VMEM((tokens, width), low),
                pltpu.VMEM((tokens, width), low),
                pltpu.VMEM((tokens, width), low),
                pltpu.VMEM((3, width, local), jnp.float32),
                pltpu.VMEM((local, width), jnp.float32),
                pltpu.VMEM((heads, tokens, HEAD_DIM), jnp.float32),
                pltpu.VMEM((heads, tokens, HEAD_DIM), jnp.float32),
                pltpu.VMEM((heads, HEAD_DIM, block), jnp.float32),
                pltpu.VMEM((heads, block, HEAD_DIM), low),
                pltpu.VMEM((heads, HEAD_DIM, block), low),
                pltpu.VMEM((heads, 1, block), jnp.float32),
                pltpu.SemaphoreType.DMA((8,)),
                pltpu.SemaphoreType.DMA((4,)),
            ],
        ),
        out_shape=[
            *[jax.ShapeDtypeStruct(x[0].shape, low)] * 4,
            jax.ShapeDtypeStruct((4, width, local), low),
        ],
        compiler_params=pltpu.CompilerParams(vmem_limit_bytes=56 << 20),
        cost_estimate=pl.CostEstimate(
            flops=4 * flops, transcendentals=tokens * tokens * heads // 2, bytes_accessed=40 << 20
        ),
        name="attention_backward",
    )(ranges, ranks, *upstream, *x, ctx, lse, q, qt, start, k, kt, v, w, proj)


def route_rows(route, priority, experts, capacity, row_count, ranks):
    own_start = ranks[0] * row_count
    own_route = lax.dynamic_slice_in_dim(route, own_start, row_count, 0)
    own_priority = lax.dynamic_slice_in_dim(priority, own_start, row_count, 0)
    ahead = (route[None, :] == own_route[:, None]) & (priority[None, :] < own_priority[:, None])
    kept = jnp.sum(ahead.astype(jnp.int32), axis=1) < capacity
    kinds = jnp.arange(experts, dtype=jnp.int32)
    block_hot = (route.reshape(-1, row_count)[:, :, None] == kinds).astype(jnp.int32)
    lengths = (jnp.sum(block_hot, axis=1) + ALIGN - 1) // ALIGN * ALIGN
    starts = jnp.cumsum(lengths, axis=1) - lengths
    own_hot = (own_route[:, None] == kinds).astype(jnp.int32)
    index = jnp.arange(row_count, dtype=jnp.int32)
    before = (own_route[None, :] == own_route[:, None]) & (index[None, :] < index[:, None])
    own_starts = lax.dynamic_slice_in_dim(starts, ranks[0], 1, 0)
    place = jnp.sum(before.astype(jnp.int32), axis=1) + jnp.sum(own_hot * own_starts, axis=1)
    slots = jnp.arange(row_count + experts * ALIGN, dtype=jnp.int32)
    order = (slots[:, None] == place[None, :]).astype(jnp.bfloat16)
    picked = [
        lax.dynamic_slice_in_dim(array, ranks[b], 1, 0)[0]
        for array in (starts, lengths)
        for b in range(4)
    ]
    home = at_home().astype(jnp.int32)[None]
    return (kept, order, jnp.concatenate([*picked, home]), own_hot)


def sort_rows(order, rows):
    return jnp.dot(order, rows, preferred_element_type=jnp.float32).astype(jnp.bfloat16)


def unsort_rows(order, rows):
    return matmul(order, rows.astype(jnp.bfloat16), ((0,), (0,)))


def each_tile(table, expert, experts, visit):
    for block in range(4):
        start = table[block * experts + expert]
        length = table[(4 + block) * experts + expert]

        def tile(number, carry, block=block, start=start, length=length):
            place = pl.ds(pl.multiple_of(start + number * TILE, ALIGN), TILE)
            visit(block, place, length - number * TILE)
            return carry

        lax.fori_loop(0, (length + TILE - 1) // TILE, tile, 0)


def fetch_weights(choice, kept, given, targets, semaphores):
    for place, target in enumerate(targets):
        for expert in range(target.shape[0]):
            ready = semaphores.at[place, expert]

            @pl.when(choice == 1)
            def _(place=place, target=target, expert=expert, ready=ready):
                pltpu.make_async_copy(kept[place].at[expert], target.at[expert], ready).start()

            @pl.when(choice == 0)
            def _(place=place, target=target, expert=expert, ready=ready):
                pltpu.make_async_copy(given[place].at[expert], target.at[expert], ready).start()


def await_weights(kept, targets, expert, semaphores):
    for place, target in enumerate(targets):
        pltpu.make_async_copy(
            kept[place].at[expert], target.at[expert], semaphores.at[place, expert]
        ).wait()


def within(rows, left):
    return jnp.where(lax.broadcasted_iota(jnp.int32, rows.shape, 0) < left, rows, 0)


def moe_forward_kernel(
    table, x0, x1, x2, x3, own_up, own_down, new_up, new_down,
    y0, y1, y2, y3, hidden_out, slope_out,
    x_ref, y_ref, hidden_ref, slope_ref, up_ref, down_ref, semaphores, ready,
):
    expert = pl.program_id(0)
    experts = pl.num_programs(0)
    count = x0.shape[0]
    kept, given, held = (own_up, own_down), (new_up, new_down), (up_ref, down_ref)

    @pl.when(expert == 0)
    def _():
        fetch_weights(table[8 * experts], kept, given, held, ready)
        for ref in (hidden_ref, slope_ref, y_ref):
            ref[...] = jnp.zeros_like(ref)
        x_ref[:, count:, :] = jnp.zeros((4, TILE, x_ref.shape[2]), jnp.bfloat16)
        copies([(x, x_ref.at[b, :count]) for b, x in enumerate((x0, x1, x2, x3))], semaphores)

    await_weights(kept, held, expert, ready)

    def visit(block, place, left):
        u = matmul(x_ref[block, place, :], up_ref[expert])
        bend = jnp.tanh(0.7978845608028654 * (u + 0.044715 * u * u * u))
        hidden = (0.5 * u * (1.0 + bend)).astype(jnp.bfloat16)
        slope = 0.5 * (1.0 + bend) + 0.5 * u * (1.0 - bend * bend) * (
            0.7978845608028654 * (1.0 + 3.0 * 0.044715 * u * u)
        )
        hidden_ref[block, place, :] = hidden
        slope_ref[block, place, :] = slope.astype(jnp.bfloat16)
        y_ref[block, place, :] = matmul(hidden, down_ref[expert]).astype(jnp.bfloat16)

    each_tile(table, expert, experts, visit)

    @pl.when(expert == experts - 1)
    def _():
        copies(
            [(y_ref.at[b, :count], y) for b, y in enumerate((y0, y1, y2, y3))]
            + [(hidden_ref, hidden_out), (slope_ref, slope_out)],
            semaphores,
        )


def moe_backward_kernel(
    table, d0, d1, d2, d3, slope_in, own_up, own_down, new_up, new_down,
    y0, y1, y2, y3, grad_out,
    d_ref, slope_ref, y_ref, grad_ref, up_ref, down_ref, semaphores, ready,
):
    expert = pl.program_id(0)
    experts = pl.num_programs(0)
    count = d0.shape[0]
    kept, given, held = (own_up, own_down), (new_up, new_down), (up_ref, down_ref)

    @pl.when(expert == 0)
    def _():
        fetch_weights(table[8 * experts], kept, given, held, ready)
        for ref in (grad_ref, y_ref):
            ref[...] = jnp.zeros_like(ref)
        d_ref[:, count:, :] = jnp.zeros((4, TILE, d_ref.shape[2]), jnp.bfloat16)
        copies(
            [(d, d_ref.at[b, :count]) for b, d in enumerate((d0, d1, d2, d3))]
            + [(slope_in, slope_ref)],
            semaphores,
        )

    await_weights(kept, held, expert, ready)

    def visit(block, place, left):
        upstream = within(d_ref[block, place, :], left)
        slope = slope_ref[block, place, :].astype(jnp.float32)
        grad = (matmul(upstream, down_ref[expert], ((1,), (1,))) * slope).astype(jnp.bfloat16)
        grad_ref[block, place, :] = grad
        y_ref[block, place, :] = matmul(grad, up_ref[expert], ((1,), (1,))).astype(jnp.bfloat16)

    each_tile(table, expert, experts, visit)

    @pl.when(expert == experts - 1)
    def _():
        copies(
            [(y_ref.at[b, :count], y) for b, y in enumerate((y0, y1, y2, y3))]
            + [(grad_ref, grad_out)],
            semaphores,
        )


def moe_weights_kernel(
    table, a0, a1, a2, a3, b_in, out_ref, a_ref, b_ref, sum_ref, semaphores
):
    expert = pl.program_id(0)
    experts = pl.num_programs(0)
    count = a0.shape[0]

    @pl.when(expert == 0)
    def _():
        a_ref[:, count:, :] = jnp.zeros((4, TILE, a_ref.shape[2]), jnp.bfloat16)
        copies(
            [(a, a_ref.at[b, :count]) for b, a in enumerate((a0, a1, a2, a3))] + [(b_in, b_ref)],
            semaphores,
        )

    sum_ref[...] = jnp.zeros_like(sum_ref)

    def visit(block, place, left):
        sum_ref[...] += matmul(
            within(a_ref[block, place, :], left), b_ref[block, place, :], ((0,), (0,))
        )

    each_tile(table, expert, experts, visit)
    out_ref[0] = sum_ref[...].astype(jnp.bfloat16)


def moe_call(kernel, name, table, arrays, outs, scratch, sums, experts, cost):
    low = jnp.bfloat16
    specs = [HBM] * len(outs)
    ready = [pltpu.SemaphoreType.DMA((2, experts))]
    if sums:
        specs = [pl.BlockSpec((1,) + outs[0][1:], lambda e, t: (e, 0, 0))]
        ready = []
    return pl.pallas_call(
        kernel,
        grid_spec=pltpu.PrefetchScalarGridSpec(
            num_scalar_prefetch=1,
            grid=(experts,),
            in_specs=[HBM] * len(arrays),
            out_specs=specs,
            scratch_shapes=[
                *[pltpu.VMEM(shape, low) for shape in scratch],
                *[pltpu.VMEM(shape, jnp.float32) for shape in sums],
                pltpu.SemaphoreType.DMA((10,)),
                *ready,
            ],
        ),
        out_shape=[jax.ShapeDtypeStruct(shape, low) for shape in outs],
        compiler_params=pltpu.CompilerParams(vmem_limit_bytes=58 << 20),
        cost_estimate=pl.CostEstimate(flops=cost, transcendentals=0, bytes_accessed=40 << 20),
        name=name,
    )(table, *arrays)


def moe_forward(table, x, own, new):
    count, width = x[0].shape
    experts, _, hidden = own[0].shape
    wide, tall = (4, count + TILE, width), (4, count + TILE, hidden)
    *y, hid, slope = moe_call(
        moe_forward_kernel, "moe_forward", table, [*x, *own, *new],
        [(count, width)] * 4 + [tall, tall],
        [wide, wide, tall, tall, own[0].shape, own[1].shape], [], experts,
        20 * count * width * hidden,
    )
    return (y, hid, slope)


def moe_backward(table, d, slope, own, new):
    count, width = d[0].shape
    experts, _, hidden = own[0].shape
    wide, tall = (4, count + TILE, width), (4, count + TILE, hidden)
    *y, grad = moe_call(
        moe_backward_kernel, "moe_backward", table, [*d, slope, *own, *new],
        [(count, width)] * 4 + [tall],
        [wide, tall, wide, tall, own[0].shape, own[1].shape], [], experts,
        20 * count * width * hidden,
    )
    return (y, grad)


def moe_weights(table, blocks, tall, experts):
    count, width = blocks[0].shape
    hidden = tall.shape[2]
    return moe_call(
        moe_weights_kernel, "moe_weights", table, [*blocks, tall], [(experts, width, hidden)],
        [(4, count + TILE, width), tall.shape], [(width, hidden)], experts,
        10 * count * width * hidden,
    )[0]


def at_home():
    return lax.axis_index("c") == lax.axis_index("zh")


def swap_roles(value):
    moved = lax.ppermute(value, ("c", "zh"), [(1, 2), (2, 1)])
    return jnp.where(at_home(), value, moved)


def flip(value, axis):
    return lax.ppermute(value, axis, [(0, 1), (1, 0)])


def flip_some(value, home):
    moves = [(0, 1), (1, 0), (6, 7), (7, 6)] if home else [(2, 3), (3, 2), (4, 5), (5, 4)]
    return lax.ppermute(value, ("c", "zh", "zl"), moves)


def tie(*values):
    return lax.optimization_barrier(values)


def gather_blocks(rows):
    across = flip(rows, "zl")
    return [rows, flip(rows, "c"), across, flip(across, "c")]


def far_rows(blocks):
    return (
        flip(blocks[3], "c").astype(jnp.float32) + blocks[2].astype(jnp.float32)
    ).astype(blocks[2].dtype)


def near_rows(blocks):
    return blocks[0].astype(jnp.float32) + flip(blocks[1], "c").astype(jnp.float32)


def scatter_blocks(blocks):
    return near_rows(blocks) + flip(far_rows(blocks), "zl").astype(jnp.float32)


def halve(value, axis, dimension):
    count = value.shape[dimension] // 2
    side = lax.axis_index(axis)
    kept = lax.dynamic_slice_in_dim(value, side * count, count, dimension)
    sent = lax.dynamic_slice_in_dim(value, (1 - side) * count, count, dimension)
    total = kept.astype(jnp.float32) + flip(sent, axis).astype(jnp.float32)
    return total.astype(value.dtype)


def send_home(value, dimension):
    count = value.shape[dimension] // 2
    high = lax.axis_index("zh")
    straight = lax.dynamic_slice_in_dim(value, high * count, count, dimension)
    turned = lax.dynamic_slice_in_dim(value, (1 - high) * count, count, dimension)
    turned = lax.ppermute(turned, ("c", "zh"), [(0, 2), (1, 0), (2, 3), (3, 1)])
    return [straight, lax.ppermute(straight, ("c", "zh"), [(1, 2), (2, 1)]), turned]


def sum_home(straight, moved, turned):
    straight = jnp.where(at_home(), straight, moved)
    return straight.astype(jnp.float32) + turned.astype(jnp.float32)


def piece_of(weight, users):
    flat = weight.reshape(-1, weight.shape[-1])
    part = flat.shape[0] // lax.axis_size(users)
    return lax.dynamic_slice_in_dim(flat, lax.axis_index(users) * part, part, 0)


def share(piece, users, shape):
    return lax.all_gather(piece, users, axis=0, tiled=True).reshape(shape)


def share_small(piece, users, shape):
    for bit in reversed(users):
        given = flip(piece, bit)
        low = lax.axis_index(bit) == 0
        piece = jnp.concatenate([jnp.where(low, piece, given), jnp.where(low, given, piece)], axis=0)
    return piece.reshape(shape)


def body(
    high_bits,
    block_input,
    attention_gain,
    qkv_weight,
    proj_weight,
    moe_gain,
    centroids,
    expert_up,
    expert_down,
    out_grad,
    routes,
    priority,
    segments,
):
    row_count = block_input.shape[1]
    model_width = block_input.shape[2]
    experts = expert_up.shape[0]
    token_count = segments.shape[1]
    capacity = 9 * token_count // (8 * experts)
    local_width = qkv_weight.shape[2]
    users = (*high_bits, "c")
    core, near = lax.axis_index("c"), lax.axis_index("zl")
    ranks = jnp.stack(
        [2 * core + near, 2 * (1 - core) + near, 2 * core + 1 - near, 3 - 2 * core - near]
    )
    home = at_home()
    staying = block_input[0]
    coming = lax.ppermute(staying, ("c", "zh"), [(1, 2), (2, 1)])
    small = jnp.concatenate([qkv_weight, proj_weight.reshape(1, model_width, local_width)], axis=0)
    small_piece = flip(piece_of(small, users), "zh")

    def normed(rows):
        return (normalize_plain(rows.astype(jnp.float32))[0] * attention_gain).astype(jnp.bfloat16)

    normed_staying = normed(staying)
    home_across = flip_some(normed_staying, True)
    indices = jnp.stack([routes[0, :, 0], priority[0], segments[0]])
    indices = jnp.where(home, indices, flip(indices, "c"))
    segment = indices[2]
    ranges, start = key_ranges(segment, QUERY_BLOCK)
    coming, small_piece, home_across, ranges, start = tie(
        coming, small_piece, home_across, ranges, start
    )
    small_other = share(small_piece, users, small.shape)
    normed_coming = normed(coming)
    away_across = flip_some(normed_coming, False)
    across = jnp.where(home, home_across, away_across)
    across, up_piece, down_piece = tie(
        across, piece_of(expert_up, users), piece_of(expert_down, users)
    )
    up_piece, down_piece = flip(up_piece, "zh"), flip(down_piece, "zh")
    normed_one = jnp.where(home, normed_staying, normed_coming)
    normed_one = [normed_one, flip(normed_one, "c"), across, flip(across, "c")]
    inputs = jnp.where(home, staying, coming).astype(jnp.float32)
    unit_one, inverse_one = normalize_plain(inputs)
    small = jnp.where(home, small, small_other)
    qkv_used, proj_used = small[:3], small[3].reshape(local_width, model_width)
    *attended, q, qt, k, kt, v, ctx, lse = attention_forward(
        ranges, start, ranks, normed_one, qkv_used, proj_used
    )
    saved = (q, qt, k, kt, v, ctx, lse)
    attended[3], up_piece, down_piece, indices, upstream = tie(
        attended[3], up_piece, down_piece, indices, out_grad[0]
    )
    away_upstream = lax.ppermute(upstream, ("c", "zh"), [(1, 2), (2, 1)])
    new_experts = [share(piece, users, expert_up.shape) for piece in (up_piece, down_piece)]
    back_ranges = key_ranges(indices[2], BLOCK)[0]
    kept_rows, order, table, hot_rows = route_rows(
        indices[0], indices[1], experts, capacity, row_count, ranks
    )
    own_experts = (expert_up, expert_down)
    far, back_ranges, order, table, kept_rows = tie(
        flip(far_rows(attended), "zl"), back_ranges, order, table, kept_rows
    )
    upstream = jnp.where(home, upstream, away_upstream).astype(jnp.float32)
    attended = near_rows(attended) + far.astype(jnp.float32)
    mixed_one = inputs + attended
    unit_two, inverse_two = normalize_plain(mixed_one)
    normed_two_rows = (unit_two * moe_gain).astype(jnp.bfloat16)
    centroid_rows = jnp.dot(
        hot_rows.astype(jnp.bfloat16), centroids, preferred_element_type=jnp.float32
    )
    normed_two_float = normed_two_rows.astype(jnp.float32)
    gate_prob = jax.nn.sigmoid(jnp.sum(normed_two_float * centroid_rows, axis=-1))
    gate_used = jnp.where(kept_rows, gate_prob, 0.0)
    grad_eo_rows = (gate_used[:, None] * upstream).astype(jnp.bfloat16)
    sorted_rows = sort_rows(order, normed_two_rows)
    beside, across = flip(sorted_rows, "c"), flip(sorted_rows, "zl")
    across, grad_sorted = tie(across, sort_rows(order, grad_eo_rows))
    grad_beside, grad_across = flip(grad_sorted, "c"), flip(grad_sorted, "zl")
    dispatched = [sorted_rows, beside, across, flip(across, "c")]
    returned, hidden, slope = moe_forward(table, dispatched, own_experts, new_experts)
    grad_across, *returned = tie(grad_across, *returned)
    returned_far, grad_corner = tie(far_rows(returned), flip(grad_across, "c"))
    grad_dispatched = [grad_sorted, grad_beside, grad_across, grad_corner]
    returned_far = flip(returned_far, "zl")
    returned_near = near_rows(returned)
    back_moe, grad_upward = moe_backward(table, grad_dispatched, slope, own_experts, new_experts)
    returned_far, back_moe[3] = tie(returned_far, back_moe[3])
    back_far, hidden = tie(far_rows(back_moe), hidden)
    back_far = flip(back_far, "zl")
    down_part = moe_weights(table, grad_dispatched, hidden, experts)
    down_rest = lax.psum_scatter(down_part, high_bits, scatter_dimension=1, tiled=True)
    expert_out = unsort_rows(order, returned_near + returned_far.astype(jnp.float32))
    mixed_two = (mixed_one + gate_used[:, None] * expert_out).astype(jnp.bfloat16)
    grad_gate = jnp.where(kept_rows, jnp.sum(upstream * expert_out, axis=-1), 0.0)
    grad_score = grad_gate * gate_prob * (1.0 - gate_prob)
    grad_score, grad_upward = tie(grad_score, grad_upward)
    up_part = moe_weights(table, dispatched, grad_upward, experts)
    back_far, up_part = tie(back_far, up_part)
    back_moe = near_rows(back_moe) + back_far.astype(jnp.float32)
    grad_two = unsort_rows(order, back_moe) + grad_score[:, None] * centroid_rows
    centroid_part = jnp.einsum(
        "te,td->ed",
        hot_rows.astype(jnp.float32),
        grad_score[:, None] * normed_two_float,
        precision=highest,
    )
    moe_gain_part = jnp.sum(grad_two * unit_two, axis=0)
    grad_mixed = upstream + normalize_back(grad_two, unit_two, inverse_two, moe_gain)
    grad_att = gather_blocks(grad_mixed.astype(jnp.bfloat16))
    up_rest = lax.psum_scatter(up_part, high_bits, scatter_dimension=1, tiled=True)
    early = jnp.concatenate([moe_gain_part[None], centroid_part], axis=0)
    everyone = (*users, "zh", "zl")
    early = jnp.swapaxes(early.reshape(experts + 1, lax.axis_size(everyone), -1), 0, 1)
    early = jnp.sum(lax.all_to_all(early, everyone, 0, 0, tiled=True), axis=0)
    grad_att[2], early = tie(grad_att[2], early)
    grad_att[3] = flip(grad_att[2], "c")
    down_rest, mixed_two, grad_att[3] = tie(down_rest, mixed_two, grad_att[3])
    down_home = send_home(down_rest, 1)
    away_output = lax.ppermute(mixed_two, ("c", "zh"), [(1, 2), (2, 1)])
    *grad_one, weights_part = attention_backward(
        back_ranges, start, ranks, grad_att, normed_one, saved, qkv_used, proj_used
    )
    grad_one[3], away_output, *down_home = tie(grad_one[3], away_output, *down_home)
    block_output = jnp.where(home, mixed_two, away_output)[None]
    one_far = far_rows(grad_one)
    one_near = near_rows(grad_one)

    def finish(far):
        grad = normalize_back(
            one_near + far.astype(jnp.float32), unit_one, inverse_one, attention_gain
        )
        return (grad_mixed + grad).astype(jnp.bfloat16)

    going = flip_some(one_far, False)
    going, one_far, *up_home = tie(going, one_far, *send_home(up_rest, 1))
    kept_far = flip_some(one_far, True)
    weights_part = halve(weights_part, high_bits[0], 1)
    going, weights_part = tie(finish(going), weights_part)
    going = lax.ppermute(going, ("c", "zh"), [(1, 2), (2, 1)])
    input_grad = jnp.where(home, finish(kept_far), going)[None]
    down_summed = jnp.swapaxes(sum_home(*down_home), 1, 2)
    up_summed = sum_home(*up_home)
    for bit in high_bits[1:]:
        weights_part = halve(weights_part, bit, 1)
    weights_part = sum_home(*send_home(weights_part, 1))
    qkv_summed, proj_summed = weights_part[:3], weights_part[3].T
    gain_two_sum, centroid_sum = early[0], early[1:]
    slice_rows = qkv_summed.shape[1]
    own_rows = lax.dynamic_slice_in_dim(
        qkv_weight, lax.axis_index(users) * slice_rows, slice_rows, 1
    )
    gain_one = jnp.sum(own_rows.astype(jnp.float32) * qkv_summed, axis=(0, 2))
    for bit in ("zh", "zl"):
        gain_one = halve(gain_one, bit, 0)
    entries = gain_one.shape[0]
    own_gain = lax.axis_index((*users, "zh", "zl")) * entries
    gain_one_sum = gain_one / lax.dynamic_slice_in_dim(attention_gain, own_gain, entries, 0)
    return (
        block_output,
        input_grad,
        gain_one_sum,
        gain_two_sum,
        centroid_sum,
        qkv_summed,
        proj_summed,
        up_summed,
        down_summed,
    )


def solution(mesh):
    shape = mesh.devices.shape
    high_bits = tuple(f"u{place}" for place in range((shape[0] // 2).bit_length() - 1))
    dp, tensor = (*high_bits, "c"), ("zh", "zl")
    mesh = Mesh(mesh.devices.reshape((2,) * len(dp + tensor)), dp + tensor)

    def program(*arguments):
        return body(high_bits, *arguments)

    return jax.shard_map(
        program,
        mesh=mesh,
        in_specs=(
            P(dp, tensor, None),
            P(),
            P(None, None, tensor),
            P(tensor, None),
            P(),
            P(),
            P(None, None, tensor),
            P(None, tensor, None),
            P(dp, tensor, None),
            P(dp, None, None),
            P(dp, None),
            P(dp, None),
        ),
        out_specs=(
            P(dp, tensor, None),
            P(dp, tensor, None),
            P(dp + tensor),
            P(dp + tensor),
            P(None, dp + tensor),
            P(None, dp, tensor),
            P(tensor, dp),
            P(None, dp, tensor),
            P(None, tensor, dp),
        ),
        check_vma=False,
    )
```

```python
import jax
import jax.numpy as jnp
from jax import lax
from jax.experimental import pallas as pl
from jax.experimental.pallas import tpu as pltpu
from jax.sharding import Mesh
from jax.sharding import PartitionSpec as P

HEAD_DIM = 64
QUERY_BLOCK = 512
BLOCK = 256
LOG2E = 1.4426950408889634
NEGATIVE = -1e30
TILE = 256
CHUNK = 256
TOKEN = (16, 128)
ALIGN = 16
CONTINUATIONS = 8
HBM = pl.BlockSpec(memory_space=pl.ANY)

epsilon = 1e-05
highest = lax.Precision.HIGHEST


def normalize_plain(values):
    centered = values - jnp.mean(values, axis=-1, keepdims=True)
    variance = jnp.mean(centered * centered, axis=-1, keepdims=True)
    inverse = lax.rsqrt(variance + epsilon)
    return (centered * inverse, inverse)


def normalize_back(upstream, unit_rows, inverse, gain_row):
    scaled = upstream * gain_row
    centered = scaled - jnp.mean(scaled, axis=-1, keepdims=True)
    return inverse * (centered - unit_rows * jnp.mean(scaled * unit_rows, axis=-1, keepdims=True))


def matmul(a, b, dims=((1,), (0,))):
    return lax.dot_general(a, b, (dims, ((), ())), preferred_element_type=jnp.float32)


def key_ranges(segment, block):
    token_count = segment.shape[0]
    numbers = jnp.arange(1, CONTINUATIONS + 1, dtype=jnp.int32)[:, None]
    earlier = jnp.sum((segment[None, :] < numbers).astype(jnp.int32), axis=1, keepdims=True)
    prompt = earlier[0, 0]
    start = jnp.sum(jnp.where(segment[None, :] == numbers, earlier, 0), axis=0)
    first = jnp.arange(token_count // block, dtype=jnp.int32) * block
    whole = jnp.minimum(prompt, first) // block
    shared = (jnp.minimum(prompt, first + block) + block - 1) // block
    own = jnp.maximum(shared, start.reshape(-1, block)[:, 0] // block)
    last = first // block + 1
    return (jnp.stack([whole, shared, own, last, jnp.full_like(whole, prompt)]), start[None, :])


def copies(pairs, semaphores):
    moved = [
        pltpu.make_async_copy(source, target, semaphores.at[place])
        for place, (source, target) in enumerate(pairs)
    ]
    for copy in moved:
        copy.start()
    for copy in moved:
        copy.wait()


def rank_rows(ref, rank, like):
    count = like.shape[0]
    return ref.at[pl.ds(pl.multiple_of(rank * count, count), count)]


def send_ranks(ref, targets, ranks, semaphores, edge, block, down):
    count = targets[0].shape[0]
    for rank in range(4):
        if down:
            first = rank * count
            due = (edge <= first) & (edge + block > first)
        else:
            last = (rank + 1) * count
            due = (edge >= last) & (edge - block < last)

        @pl.when(due)
        def _(rank=rank):
            for b, target in enumerate(targets):

                @pl.when(ranks[b] == rank)
                def _(b=b, target=target):
                    source = ref.at[rank * count : (rank + 1) * count]
                    pltpu.make_async_copy(source, target, semaphores.at[b]).start()


def await_ranks(ref, targets, ranks, semaphores):
    for b, target in enumerate(targets):
        pltpu.make_async_copy(rank_rows(ref, ranks[b], target), target, semaphores.at[b]).wait()


def forward_kernel(
    ranges, ranks, x0, x1, x2, x3, w_ref, proj_ref, start_ref,
    p0, p1, p2, p3, q_ref, qt_ref, k_ref, kt_ref, v_ref, ctx_ref, lse_ref,
    x_ref, part_ref, vt_ref, score_ref, top_ref, sum_ref, arrived, left,
):
    step = pl.program_id(0)
    heads = q_ref.shape[0]
    block = q_ref.shape[1]
    rows = pl.ds(pl.multiple_of(step * block, block), block)

    @pl.when(step == 0)
    def _():
        copies(
            [(x, rank_rows(x_ref, ranks[b], x)) for b, x in enumerate((x0, x1, x2, x3))], arrived
        )

    x = x_ref[rows, :]
    kinds = []
    for kind in range(3):
        made = matmul(x, w_ref[kind])
        kinds.append((made.astype(jnp.bfloat16), made.T.astype(jnp.bfloat16)))
    for head in range(heads):
        part = slice(head * HEAD_DIM, (head + 1) * HEAD_DIM)
        q_ref[head] = kinds[0][0][:, part]
        k_ref[head, rows, :] = kinds[1][0][:, part]
        v_ref[head, rows, :] = kinds[2][0][:, part]
        qt_ref[head] = kinds[0][1][part]
        for piece in range(kt_ref.shape[0]):
            columns = slice(piece * kt_ref.shape[3], (piece + 1) * kt_ref.shape[3])
            kt_ref[piece, head] = kinds[1][1][part, columns]
        vt_ref[step, head, :HEAD_DIM] = kinds[2][1][part]
        vt_ref[step, head, HEAD_DIM:] = jnp.ones((16, block), jnp.bfloat16)
    top_ref[...] = jnp.full_like(top_ref, NEGATIVE)
    sum_ref[...] = jnp.zeros_like(sum_ref)
    prompt = ranges[4, step]
    scale = LOG2E * HEAD_DIM ** (-0.5)

    def visit(key, masked):
        place = pl.ds(pl.multiple_of(key * block, block), block)
        if masked:
            key_at = key * block + lax.broadcasted_iota(jnp.int32, (block, block), 0)
            query_at = step * block + lax.broadcasted_iota(jnp.int32, (block, block), 1)
            seen = (key_at <= query_at) & ((key_at < prompt) | (key_at >= start_ref[...]))
        for head in range(heads):
            scores = matmul(k_ref[head, place, :], qt_ref[head])
            if masked:
                scores = jnp.where(seen, scores, NEGATIVE)
            score_ref[key, head] = scores
            top_ref[head] = jnp.maximum(
                top_ref[head], jnp.max(scores.reshape(block // 8, 8, block), axis=0)
            )

    def plain(key, carry):
        visit(key, False)
        return carry

    def edge(key, carry):
        visit(key, True)
        return carry

    lax.fori_loop(0, ranges[0, step], plain, 0)
    lax.fori_loop(ranges[0, step], ranges[1, step], edge, 0)
    lax.fori_loop(ranges[2, step], ranges[3, step], edge, 0)
    for head in range(heads):
        top_ref[head, :1] = jnp.max(top_ref[head], axis=0, keepdims=True) * scale

    def add(key, carry):
        for head in range(heads):
            weights = jnp.exp2(score_ref[key, head] * scale - top_ref[head, :1])
            sum_ref[head] += matmul(vt_ref[key, head], weights.astype(jnp.bfloat16))
        return carry

    lax.fori_loop(0, ranges[1, step], add, 0)
    lax.fori_loop(ranges[2, step], ranges[3, step], add, 0)
    for head in range(heads):
        total = sum_ref[head, HEAD_DIM : HEAD_DIM + 1]
        context = sum_ref[head, :HEAD_DIM] / total
        ctx_ref[head * HEAD_DIM : (head + 1) * HEAD_DIM] = context.astype(jnp.bfloat16)
        lse_ref[head] = top_ref[head, :1] + jnp.log(total) * LOG2E
    part_ref[rows, :] = matmul(ctx_ref[...], proj_ref[...], ((0,), (0,))).astype(jnp.bfloat16)
    send_ranks(part_ref, (p0, p1, p2, p3), ranks, left, (step + 1) * block, block, False)

    @pl.when(step == pl.num_programs(0) - 1)
    def _():
        await_ranks(part_ref, (p0, p1, p2, p3), ranks, left)


def attention_forward(ranges, start, ranks, x, w, proj):
    tokens, width = start.shape[1], x[0].shape[1]
    local = w.shape[2]
    heads = local // HEAD_DIM
    block = QUERY_BLOCK
    fine = BLOCK
    count = tokens // block
    low = jnp.bfloat16
    head_rows = pl.BlockSpec((heads, tokens, HEAD_DIM), lambda i, r, n: (0, 0, 0))
    flops = 2 * tokens * width * local * 4 + tokens * tokens * local * 2
    return pl.pallas_call(
        forward_kernel,
        grid_spec=pltpu.PrefetchScalarGridSpec(
            num_scalar_prefetch=2,
            grid=(count,),
            in_specs=[
                *[HBM] * 4,
                pl.BlockSpec((3, width, local), lambda i, r, n: (0, 0, 0)),
                pl.BlockSpec((local, width), lambda i, r, n: (0, 0)),
                pl.BlockSpec((1, block), lambda i, r, n: (0, i)),
            ],
            out_specs=[
                *[HBM] * 4,
                pl.BlockSpec((heads, block, HEAD_DIM), lambda i, r, n: (0, i, 0)),
                pl.BlockSpec((heads, HEAD_DIM, block), lambda i, r, n: (0, 0, i)),
                head_rows,
                pl.BlockSpec((block // fine, heads, HEAD_DIM, fine), lambda i, r, n: (i, 0, 0, 0)),
                head_rows,
                pl.BlockSpec((local, block), lambda i, r, n: (0, i)),
                pl.BlockSpec((heads, 1, block), lambda i, r, n: (0, 0, i)),
            ],
            scratch_shapes=[
                pltpu.VMEM((tokens, width), low),
                pltpu.VMEM((tokens, width), low),
                pltpu.VMEM((count, heads, HEAD_DIM + 16, block), low),
                pltpu.VMEM((count, heads, block, block), jnp.float32),
                pltpu.VMEM((heads, 8, block), jnp.float32),
                pltpu.VMEM((heads, HEAD_DIM + 16, block), jnp.float32),
                pltpu.SemaphoreType.DMA((4,)),
                pltpu.SemaphoreType.DMA((4,)),
            ],
        ),
        out_shape=[
            *[jax.ShapeDtypeStruct(x[0].shape, low)] * 4,
            jax.ShapeDtypeStruct((heads, tokens, HEAD_DIM), low),
            jax.ShapeDtypeStruct((heads, HEAD_DIM, tokens), low),
            jax.ShapeDtypeStruct((heads, tokens, HEAD_DIM), low),
            jax.ShapeDtypeStruct((tokens // fine, heads, HEAD_DIM, fine), low),
            jax.ShapeDtypeStruct((heads, tokens, HEAD_DIM), low),
            jax.ShapeDtypeStruct((local, tokens), low),
            jax.ShapeDtypeStruct((heads, 1, tokens), jnp.float32),
        ],
        compiler_params=pltpu.CompilerParams(vmem_limit_bytes=56 << 20),
        cost_estimate=pl.CostEstimate(
            flops=4 * flops, transcendentals=tokens * tokens * heads // 2, bytes_accessed=40 << 20
        ),
        name="attention_forward",
    )(ranges, ranks, *x, w, proj, start)


def backward_kernel(
    ranges, ranks, g0, g1, g2, g3, x0, x1, x2, x3,
    ctx_ref, lse_ref, q_ref, qt_ref, start_ref, k_ref, kt_ref, v_ref, w_ref, proj_ref,
    p0, p1, p2, p3, weights_ref,
    g_ref, x_ref, part_ref, wgrad_ref, pgrad_ref,
    dk_ref, dv_ref, dqt_ref, out_ref, outt_ref, inner_ref, arrived, left,
):
    number = pl.program_id(0)
    step = pl.num_programs(0) - 1 - number
    heads = q_ref.shape[0]
    block = q_ref.shape[1]
    rows = pl.ds(pl.multiple_of(step * block, block), block)

    @pl.when(number == 0)
    def _():
        copies(
            [(g, rank_rows(g_ref, ranks[b], g)) for b, g in enumerate((g0, g1, g2, g3))]
            + [(x, rank_rows(x_ref, ranks[b], x)) for b, x in enumerate((x0, x1, x2, x3))],
            arrived,
        )
        dk_ref[...] = jnp.zeros_like(dk_ref)
        dv_ref[...] = jnp.zeros_like(dv_ref)
        wgrad_ref[...] = jnp.zeros_like(wgrad_ref)
        pgrad_ref[...] = jnp.zeros_like(pgrad_ref)

    upstream = g_ref[rows, :]
    outer = matmul(upstream, proj_ref[...], ((1,), (1,)))
    low = outer.astype(jnp.bfloat16)
    turned = outer.T.astype(jnp.bfloat16)
    for head in range(heads):
        part = slice(head * HEAD_DIM, (head + 1) * HEAD_DIM)
        out_ref[head] = low[:, part]
        outt_ref[head] = turned[part]
        inner_ref[head] = jnp.sum(
            turned[part].astype(jnp.float32) * ctx_ref[part].astype(jnp.float32),
            axis=0,
            keepdims=True,
        )
    pgrad_ref[...] += matmul(ctx_ref[...], upstream)
    dqt_ref[...] = jnp.zeros_like(dqt_ref)
    prompt = ranges[4, step]
    scale = LOG2E * HEAD_DIM ** (-0.5)

    def visit(key, masked):
        place = pl.ds(pl.multiple_of(key * block, block), block)
        if masked:
            key_at = key * block + lax.broadcasted_iota(jnp.int32, (block, block), 0)
            query_at = step * block + lax.broadcasted_iota(jnp.int32, (block, block), 1)
            seen = (key_at <= query_at) & ((key_at < prompt) | (key_at >= start_ref[...]))
        made = [
            (
                matmul(k_ref[head, place, :], qt_ref[head]),
                matmul(v_ref[head, place, :], outt_ref[head]),
            )
            for head in range(heads)
        ]
        for head in range(heads):
            scores, dprob = made[head]
            scores = scores * scale
            if masked:
                scores = jnp.where(seen, scores, NEGATIVE)
            prob = jnp.exp2(scores - lse_ref[head])
            dscore = (prob * (dprob - inner_ref[head])).astype(jnp.bfloat16)
            made[head] = prob.astype(jnp.bfloat16), dscore
        for head in range(heads):
            prob, dscore = made[head]
            dv_ref[head, place, :] += matmul(prob, out_ref[head])
            dk_ref[head, place, :] += matmul(dscore, q_ref[head])
            dqt_ref[head] += matmul(kt_ref[key, head], dscore)

    def plain(key, carry):
        visit(key, False)
        return carry

    def edge(key, carry):
        visit(key, True)
        return carry

    lax.fori_loop(0, ranges[0, step], plain, 0)
    lax.fori_loop(ranges[0, step], ranges[1, step], edge, 0)
    lax.fori_loop(ranges[2, step], ranges[3, step], edge, 0)
    small = HEAD_DIM ** (-0.5)
    x = x_ref[rows, :]
    total = None
    for kind in range(3):
        if kind == 0:
            grad = jnp.concatenate([dqt_ref[head] for head in range(heads)], axis=0).T * small
        elif kind == 1:
            grad = jnp.concatenate([dk_ref[head, rows, :] for head in range(heads)], axis=1) * small
        else:
            grad = jnp.concatenate([dv_ref[head, rows, :] for head in range(heads)], axis=1)
        grad = grad.astype(jnp.bfloat16)
        wgrad_ref[kind] += matmul(x, grad, ((0,), (0,)))
        term = matmul(grad, w_ref[kind], ((1,), (1,)))
        total = term if total is None else total + term
    part_ref[rows, :] = total.astype(jnp.bfloat16)
    send_ranks(part_ref, (p0, p1, p2, p3), ranks, left, step * block, block, True)

    @pl.when(step == 0)
    def _():
        weights_ref[:3] = wgrad_ref[...].astype(jnp.bfloat16)
        weights_ref[3] = pgrad_ref[...].T.astype(jnp.bfloat16)
        await_ranks(part_ref, (p0, p1, p2, p3), ranks, left)


def attention_backward(ranges, start, ranks, upstream, x, saved, w, proj):
    q, qt, k, kt, v, ctx, lse = saved
    tokens, width = start.shape[1], x[0].shape[1]
    local = w.shape[2]
    heads = local // HEAD_DIM
    block = BLOCK
    count = tokens // block
    low = jnp.bfloat16

    def at(i):
        return count - 1 - i

    head_rows = pl.BlockSpec((heads, tokens, HEAD_DIM), lambda i, r, n: (0, 0, 0))
    flops = 2 * tokens * width * local * 8 + tokens * tokens * local * 5
    return pl.pallas_call(
        backward_kernel,
        grid_spec=pltpu.PrefetchScalarGridSpec(
            num_scalar_prefetch=2,
            grid=(count,),
            in_specs=[
                *[HBM] * 8,
                pl.BlockSpec((local, block), lambda i, r, n: (0, at(i))),
                pl.BlockSpec((heads, 1, block), lambda i, r, n: (0, 0, at(i))),
                pl.BlockSpec((heads, block, HEAD_DIM), lambda i, r, n: (0, at(i), 0)),
                pl.BlockSpec((heads, HEAD_DIM, block), lambda i, r, n: (0, 0, at(i))),
                pl.BlockSpec((1, block), lambda i, r, n: (0, at(i))),
                head_rows,
                pl.BlockSpec((count, heads, HEAD_DIM, block), lambda i, r, n: (0, 0, 0, 0)),
                head_rows,
                pl.BlockSpec((3, width, local), lambda i, r, n: (0, 0, 0)),
                pl.BlockSpec((local, width), lambda i, r, n: (0, 0)),
            ],
            out_specs=[
                *[HBM] * 4,
                pl.BlockSpec((4, width, local), lambda i, r, n: (0, 0, 0)),
            ],
            scratch_shapes=[
                pltpu.VMEM((tokens, width), low),
                pltpu.VMEM((tokens, width), low),
                pltpu.VMEM((tokens, width), low),
                pltpu.VMEM((3, width, local), jnp.float32),
                pltpu.VMEM((local, width), jnp.float32),
                pltpu.VMEM((heads, tokens, HEAD_DIM), jnp.float32),
                pltpu.VMEM((heads, tokens, HEAD_DIM), jnp.float32),
                pltpu.VMEM((heads, HEAD_DIM, block), jnp.float32),
                pltpu.VMEM((heads, block, HEAD_DIM), low),
                pltpu.VMEM((heads, HEAD_DIM, block), low),
                pltpu.VMEM((heads, 1, block), jnp.float32),
                pltpu.SemaphoreType.DMA((8,)),
                pltpu.SemaphoreType.DMA((4,)),
            ],
        ),
        out_shape=[
            *[jax.ShapeDtypeStruct(x[0].shape, low)] * 4,
            jax.ShapeDtypeStruct((4, width, local), low),
        ],
        compiler_params=pltpu.CompilerParams(vmem_limit_bytes=56 << 20),
        cost_estimate=pl.CostEstimate(
            flops=4 * flops, transcendentals=tokens * tokens * heads // 2, bytes_accessed=40 << 20
        ),
        name="attention_backward",
    )(ranges, ranks, *upstream, *x, ctx, lse, q, qt, start, k, kt, v, w, proj)


def route_rows(route, priority, experts, capacity, row_count, ranks):
    own_start = ranks[0] * row_count
    own_route = lax.dynamic_slice_in_dim(route, own_start, row_count, 0)
    own_priority = lax.dynamic_slice_in_dim(priority, own_start, row_count, 0)
    ahead = (route[None, :] == own_route[:, None]) & (priority[None, :] < own_priority[:, None])
    kept = jnp.sum(ahead.astype(jnp.int32), axis=1) < capacity
    kinds = jnp.arange(experts, dtype=jnp.int32)
    block_hot = (route.reshape(-1, row_count)[:, :, None] == kinds).astype(jnp.int32)
    lengths = jnp.sum(block_hot, axis=1)
    starts = jnp.cumsum(lengths, axis=1) - lengths
    own_hot = (own_route[:, None] == kinds).astype(jnp.int32)
    index = jnp.arange(row_count, dtype=jnp.int32)
    before = (own_route[None, :] == own_route[:, None]) & (index[None, :] < index[:, None])
    own_starts = lax.dynamic_slice_in_dim(starts, ranks[0], 1, 0)
    place = jnp.sum(before.astype(jnp.int32), axis=1) + jnp.sum(own_hot * own_starts, axis=1)
    order = (index[:, None] == place[None, :]).astype(jnp.bfloat16)
    picked = [
        lax.dynamic_slice_in_dim(array, ranks[b], 1, 0)[0]
        for array in (starts, lengths)
        for b in range(4)
    ]
    home = at_home().astype(jnp.int32)[None]
    return (kept, order, jnp.concatenate([*picked, home]), own_hot)


def sort_rows(order, rows):
    return jnp.dot(order, rows, preferred_element_type=jnp.float32).astype(jnp.bfloat16)


def unsort_rows(order, rows):
    return matmul(order, rows.astype(jnp.bfloat16), ((0,), (0,)))


def each_tile(table, block, expert, experts, visit):
    start = table[block * experts + expert]
    end = start + table[(4 + block) * experts + expert]
    first = start // ALIGN * ALIGN

    def tile(number, carry):
        at = first + number * TILE
        visit(pl.ds(pl.multiple_of(at, ALIGN), TILE), start - at, end - at)
        return carry

    lax.fori_loop(0, jnp.where(end > start, (end - first + TILE - 1) // TILE, 0), tile, 0)


def put_rows(ref, block, place, rows, head):
    top = pl.ds(place.start, ALIGN)
    old = ref[block, top, :]
    index = lax.broadcasted_iota(jnp.int32, old.shape, 0)
    ref[block, place, :] = rows
    ref[block, top, :] = jnp.where(index < head, old, rows[:ALIGN])


def fetch_weights(choice, kept, given, targets, semaphores):
    for place, target in enumerate(targets):
        for expert in range(target.shape[0]):
            ready = semaphores.at[place, expert]

            @pl.when(choice == 1)
            def _(place=place, target=target, expert=expert, ready=ready):
                pltpu.make_async_copy(kept[place].at[expert], target.at[expert], ready).start()

            @pl.when(choice == 0)
            def _(place=place, target=target, expert=expert, ready=ready):
                pltpu.make_async_copy(given[place].at[expert], target.at[expert], ready).start()


def await_weights(kept, targets, expert, semaphores):
    for place, target in enumerate(targets):
        pltpu.make_async_copy(
            kept[place].at[expert], target.at[expert], semaphores.at[place, expert]
        ).wait()


def within(rows, head, end):
    index = lax.broadcasted_iota(jnp.int32, rows.shape, 0)
    return jnp.where((index >= head) & (index < end), rows, 0)


def block_copies(block, pairs, semaphores):
    for place, (source, targets) in enumerate(pairs):
        for b in range(4):

            @pl.when(block == b)
            def _(place=place, source=source, targets=targets, b=b):
                target = targets[b] if isinstance(targets, tuple) else targets.at[b]
                rows = source.at[b, : target.shape[0]]
                pltpu.make_async_copy(rows, target, semaphores.at[place, b]).start()


def await_blocks(pairs, semaphores):
    for place, (source, targets) in enumerate(pairs):
        for b in range(4):
            target = targets[b] if isinstance(targets, tuple) else targets.at[b]
            rows = source.at[b, : target.shape[0]]
            pltpu.make_async_copy(rows, target, semaphores.at[place, b]).wait()


def moe_steps(table, experts, inputs, weights, outputs, tails, visit, semaphores):
    block = pl.program_id(0)
    kept, given, held = weights
    arrived, left, ready = semaphores
    count = inputs[0][1][0].shape[0]

    @pl.when(block == 0)
    def _():
        for place, (target, sources) in enumerate(inputs):
            for b in range(4):
                source = sources[b] if isinstance(sources, tuple) else sources.at[b]
                rows = target.at[b, : source.shape[0]]
                pltpu.make_async_copy(source, rows, arrived.at[place, b]).start()
        fetch_weights(table[8 * experts], kept, given, held, ready)
        for ref in tails:
            ref[:, count:, :] = jnp.zeros((4, TILE, ref.shape[2]), ref.dtype)

    for place, (target, sources) in enumerate(inputs):
        source = sources[0] if isinstance(sources, tuple) else sources.at[0]
        rows = target.at[block, : source.shape[0]]
        pltpu.make_async_copy(source, rows, arrived.at[place, block]).wait()

    def expert_rows(expert, carry):
        @pl.when(block == 0)
        def _():
            await_weights(kept, held, expert, ready)

        each_tile(
            table, block, expert, experts,
            lambda place, head, end: visit(block, expert, place, head, end),
        )
        return carry

    lax.fori_loop(0, experts, expert_rows, 0)
    block_copies(block, outputs, left)

    @pl.when(block == 3)
    def _():
        await_blocks(outputs, left)


def moe_forward_kernel(
    table, x0, x1, x2, x3, own_up, own_down, new_up, new_down,
    y0, y1, y2, y3, hidden_out, slope_out,
    x_ref, y_ref, hidden_ref, slope_ref, up_ref, down_ref, *semaphores,
):
    width = up_ref.shape[2]

    def visit(block, expert, place, head, end):
        x = x_ref[block, place, :]
        total = None
        for part in range(0, width, CHUNK):
            chunk = slice(part, part + CHUNK)
            u = matmul(x, up_ref[expert, :, chunk])
            cube = 0.7978845608028654 * u * (1.0 + 0.044715 * u * u)
            bend = 1.0 + jnp.tanh(cube)
            half = 0.5 * bend
            hidden = (u * half).astype(jnp.bfloat16)
            slope = half + u * (half * (2.0 - bend)) * (
                0.7978845608028654 * (1.0 + 3.0 * 0.044715 * u * u)
            )
            put_rows(hidden_ref.at[:, :, chunk], block, place, hidden, head)
            put_rows(slope_ref.at[:, :, chunk], block, place, slope.astype(jnp.bfloat16), head)
            term = matmul(hidden, down_ref[expert, chunk, :])
            total = term if total is None else total + term
        put_rows(y_ref, block, place, total.astype(jnp.bfloat16), head)

    moe_steps(
        table, up_ref.shape[0], [(x_ref, (x0, x1, x2, x3))],
        ((own_up, own_down), (new_up, new_down), (up_ref, down_ref)),
        [(y_ref, (y0, y1, y2, y3)), (hidden_ref, hidden_out), (slope_ref, slope_out)],
        (x_ref, hidden_ref, slope_ref), visit, semaphores,
    )


def moe_backward_kernel(
    table, d0, d1, d2, d3, slope_in, own_up, own_down, new_up, new_down,
    y0, y1, y2, y3, grad_out,
    d_ref, slope_ref, y_ref, grad_ref, up_ref, down_ref, *semaphores,
):
    width = up_ref.shape[2]

    def visit(block, expert, place, head, end):
        upstream = within(d_ref[block, place, :], head, end)
        total = None
        for part in range(0, width, CHUNK):
            chunk = slice(part, part + CHUNK)
            slope = slope_ref[block, place, chunk].astype(jnp.float32)
            grad = matmul(upstream, down_ref[expert, chunk, :], ((1,), (1,))) * slope
            grad = grad.astype(jnp.bfloat16)
            put_rows(grad_ref.at[:, :, chunk], block, place, grad, head)
            term = matmul(grad, up_ref[expert, :, chunk], ((1,), (1,)))
            total = term if total is None else total + term
        put_rows(y_ref, block, place, total.astype(jnp.bfloat16), head)

    moe_steps(
        table, up_ref.shape[0], [(d_ref, (d0, d1, d2, d3)), (slope_ref, slope_in)],
        ((own_up, own_down), (new_up, new_down), (up_ref, down_ref)),
        [(y_ref, (y0, y1, y2, y3)), (grad_ref, grad_out)],
        (d_ref, grad_ref), visit, semaphores,
    )


def moe_weights_kernel(
    table, a0, a1, a2, a3, b_in, token_in, out_ref, token_ref, a_ref, b_ref, sum_ref, semaphores
):
    expert = pl.program_id(0)
    experts = pl.num_programs(0)
    count = a0.shape[0]

    @pl.when(expert == 0)
    def _():
        token_ref[...] = jnp.zeros_like(token_ref)
        a_ref[:, count:, :] = jnp.zeros((4, TILE, a_ref.shape[2]), jnp.bfloat16)
        copies(
            [(a, a_ref.at[b, :count]) for b, a in enumerate((a0, a1, a2, a3))] + [(b_in, b_ref)],
            semaphores,
        )

    sum_ref[...] = jnp.zeros_like(sum_ref)

    def of_block(block, carry):
        def visit(place, head, end):
            rows = within(a_ref[block, place, :], head, end)
            sum_ref[...] += matmul(rows, b_ref[block, place, :], ((0,), (0,)))

        each_tile(table, block, expert, experts, visit)
        return carry

    lax.fori_loop(0, 4, of_block, 0)
    out_ref[0] = sum_ref[...].astype(jnp.bfloat16)


def moe_call(kernel, name, table, arrays, grid, specs, outs, scratch, semaphores, cost):
    return pl.pallas_call(
        kernel,
        grid_spec=pltpu.PrefetchScalarGridSpec(
            num_scalar_prefetch=1,
            grid=(grid,),
            in_specs=[HBM] * len(arrays),
            out_specs=specs,
            scratch_shapes=[
                *[pltpu.VMEM(*shape) for shape in scratch],
                *[pltpu.SemaphoreType.DMA(shape) for shape in semaphores],
            ],
        ),
        out_shape=[jax.ShapeDtypeStruct(shape, jnp.bfloat16) for shape in outs],
        compiler_params=pltpu.CompilerParams(vmem_limit_bytes=58 << 20),
        cost_estimate=pl.CostEstimate(flops=cost, transcendentals=0, bytes_accessed=40 << 20),
        name=name,
    )(table, *arrays)


def moe_forward(table, x, own, new):
    count, width = x[0].shape
    experts, _, hidden = own[0].shape
    low = jnp.bfloat16
    wide, tall = ((4, count + TILE, width), low), ((4, count + TILE, hidden), low)
    *y, hid, slope = moe_call(
        moe_forward_kernel, "moe_forward", table, [*x, *own, *new], 4, [HBM] * 6,
        [(count, width)] * 4 + [tall[0], tall[0]],
        [wide, wide, tall, tall, (own[0].shape, low), (own[1].shape, low)],
        [(1, 4), (3, 4), (2, experts)], 20 * count * width * hidden,
    )
    return (y, hid, slope)


def moe_backward(table, d, slope, own, new):
    count, width = d[0].shape
    experts, _, hidden = own[0].shape
    low = jnp.bfloat16
    wide, tall = ((4, count + TILE, width), low), ((4, count + TILE, hidden), low)
    *y, grad = moe_call(
        moe_backward_kernel, "moe_backward", table, [*d, slope, *own, *new], 4, [HBM] * 5,
        [(count, width)] * 4 + [tall[0]],
        [wide, tall, wide, tall, (own[0].shape, low), (own[1].shape, low)],
        [(2, 4), (2, 4), (2, experts)], 20 * count * width * hidden,
    )
    return (y, grad)


def moe_weights(table, blocks, tall, token, experts):
    count, width = blocks[0].shape
    hidden = tall.shape[2]
    return moe_call(
        moe_weights_kernel, "moe_weights", table, [*blocks, tall, token], experts,
        [
            pl.BlockSpec((1, width, hidden), lambda e, t: (e, 0, 0)),
            pl.BlockSpec(TOKEN, lambda e, t: (0, 0)),
        ],
        [(experts, width, hidden), TOKEN],
        [((4, count + TILE, width), jnp.bfloat16), (tall.shape, jnp.bfloat16),
         ((width, hidden), jnp.float32)],
        [(5,)], 10 * count * width * hidden,
    )


def at_home():
    return lax.axis_index("c") == lax.axis_index("zh")


def swap_roles(value):
    moved = lax.ppermute(value, ("c", "zh"), [(1, 2), (2, 1)])
    return jnp.where(at_home(), value, moved)


def flip(value, axis):
    return lax.ppermute(value, axis, [(0, 1), (1, 0)])


def flip_some(value, home):
    moves = [(0, 1), (1, 0), (6, 7), (7, 6)] if home else [(2, 3), (3, 2), (4, 5), (5, 4)]
    return lax.ppermute(value, ("c", "zh", "zl"), moves)


def tie(*values):
    return lax.optimization_barrier(values)


def gather_blocks(rows):
    across = flip(rows, "zl")
    return [rows, flip(rows, "c"), across, flip(across, "c")]


def far_rows(blocks):
    return (
        flip(blocks[3], "c").astype(jnp.float32) + blocks[2].astype(jnp.float32)
    ).astype(blocks[2].dtype)


def near_rows(blocks):
    return blocks[0].astype(jnp.float32) + flip(blocks[1], "c").astype(jnp.float32)


def scatter_blocks(blocks):
    return near_rows(blocks) + flip(far_rows(blocks), "zl").astype(jnp.float32)


def send_half(value, axis, dimension):
    count = value.shape[dimension] // 2
    side = lax.axis_index(axis)
    kept = lax.dynamic_slice_in_dim(value, side * count, count, dimension)
    sent = lax.dynamic_slice_in_dim(value, (1 - side) * count, count, dimension)
    return [kept, flip(sent, axis)]


def halve(kept, came):
    return (kept.astype(jnp.float32) + came.astype(jnp.float32)).astype(kept.dtype)


def send_home(value, dimension):
    count = value.shape[dimension] // 2
    high = lax.axis_index("zh")
    straight = lax.dynamic_slice_in_dim(value, high * count, count, dimension)
    turned = lax.dynamic_slice_in_dim(value, (1 - high) * count, count, dimension)
    turned = lax.ppermute(turned, ("c", "zh"), [(0, 2), (1, 0), (2, 3), (3, 1)])
    return [straight, lax.ppermute(straight, ("c", "zh"), [(1, 2), (2, 1)]), turned]


def sum_home(straight, moved, turned):
    straight = jnp.where(at_home(), straight, moved)
    return straight.astype(jnp.float32) + turned.astype(jnp.float32)


def piece_of(weight, users):
    flat = weight.reshape(-1, weight.shape[-1])
    part = flat.shape[0] // lax.axis_size(users)
    return lax.dynamic_slice_in_dim(flat, lax.axis_index(users) * part, part, 0)


def share(piece, users, shape):
    return lax.all_gather(piece, users, axis=0, tiled=True).reshape(shape)


def share_small(piece, users, shape):
    for bit in reversed(users):
        given = flip(piece, bit)
        low = lax.axis_index(bit) == 0
        piece = jnp.concatenate([jnp.where(low, piece, given), jnp.where(low, given, piece)], axis=0)
    return piece.reshape(shape)


def body(
    high_bits,
    block_input,
    attention_gain,
    qkv_weight,
    proj_weight,
    moe_gain,
    centroids,
    expert_up,
    expert_down,
    out_grad,
    routes,
    priority,
    segments,
):
    row_count = block_input.shape[1]
    model_width = block_input.shape[2]
    experts = expert_up.shape[0]
    token_count = segments.shape[1]
    capacity = 9 * token_count // (8 * experts)
    local_width = qkv_weight.shape[2]
    users = (*high_bits, "c")
    core, near = lax.axis_index("c"), lax.axis_index("zl")
    ranks = jnp.stack(
        [2 * core + near, 2 * (1 - core) + near, 2 * core + 1 - near, 3 - 2 * core - near]
    )
    home = at_home()
    staying = block_input[0]
    coming = lax.ppermute(staying, ("c", "zh"), [(1, 2), (2, 1)])
    small = jnp.concatenate([qkv_weight, proj_weight.reshape(1, model_width, local_width)], axis=0)
    small_piece = flip(piece_of(small, users), "zh")

    def normed(rows):
        return (normalize_plain(rows.astype(jnp.float32))[0] * attention_gain).astype(jnp.bfloat16)

    normed_staying = normed(staying)
    home_across = flip_some(normed_staying, True)
    indices = jnp.stack([routes[0, :, 0], priority[0], segments[0]])
    indices = jnp.where(home, indices, flip(indices, "c"))
    segment = indices[2]
    ranges, start = key_ranges(segment, QUERY_BLOCK)
    coming, small_piece, home_across, ranges, start = tie(
        coming, small_piece, home_across, ranges, start
    )
    small_other = share(small_piece, users, small.shape)
    normed_coming = normed(coming)
    away_across = flip_some(normed_coming, False)
    across = jnp.where(home, home_across, away_across)
    across, up_piece, down_piece = tie(
        across, piece_of(expert_up, users), piece_of(expert_down, users)
    )
    up_piece, down_piece = flip(up_piece, "zh"), flip(down_piece, "zh")
    normed_one = jnp.where(home, normed_staying, normed_coming)
    normed_one = [normed_one, flip(normed_one, "c"), across, flip(across, "c")]
    inputs = jnp.where(home, staying, coming).astype(jnp.float32)
    unit_one, inverse_one = normalize_plain(inputs)
    small = jnp.where(home, small, small_other)
    qkv_used, proj_used = small[:3], small[3].reshape(local_width, model_width)
    *attended, q, qt, k, kt, v, ctx, lse = attention_forward(
        ranges, start, ranks, normed_one, qkv_used, proj_used
    )
    saved = (q, qt, k, kt, v, ctx, lse)
    attended[3], up_piece, down_piece, indices, upstream = tie(
        attended[3], up_piece, down_piece, indices, out_grad[0]
    )
    away_upstream = lax.ppermute(upstream, ("c", "zh"), [(1, 2), (2, 1)])
    new_experts = [share(piece, users, expert_up.shape) for piece in (up_piece, down_piece)]
    back_ranges = key_ranges(indices[2], BLOCK)[0]
    kept_rows, order, table, hot_rows = route_rows(
        indices[0], indices[1], experts, capacity, row_count, ranks
    )
    own_experts = (expert_up, expert_down)
    far, back_ranges, order, table, kept_rows = tie(
        flip(far_rows(attended), "zl"), back_ranges, order, table, kept_rows
    )
    upstream = jnp.where(home, upstream, away_upstream).astype(jnp.float32)
    attended = near_rows(attended) + far.astype(jnp.float32)
    mixed_one = inputs + attended
    unit_two, inverse_two = normalize_plain(mixed_one)
    normed_two_rows = (unit_two * moe_gain).astype(jnp.bfloat16)
    centroid_rows = jnp.dot(
        hot_rows.astype(jnp.bfloat16), centroids, preferred_element_type=jnp.float32
    )
    normed_two_float = normed_two_rows.astype(jnp.float32)
    gate_prob = jax.nn.sigmoid(jnp.sum(normed_two_float * centroid_rows, axis=-1))
    gate_used = jnp.where(kept_rows, gate_prob, 0.0)
    grad_eo_rows = (gate_used[:, None] * upstream).astype(jnp.bfloat16)
    sorted_rows = sort_rows(order, normed_two_rows)
    beside, across = flip(sorted_rows, "c"), flip(sorted_rows, "zl")
    across, grad_sorted = tie(across, sort_rows(order, grad_eo_rows))
    grad_beside, grad_across = flip(grad_sorted, "c"), flip(grad_sorted, "zl")
    dispatched = [sorted_rows, beside, across, flip(across, "c")]
    returned, hidden, slope = moe_forward(table, dispatched, own_experts, new_experts)
    grad_across, *returned = tie(grad_across, *returned)
    returned_far, grad_corner = tie(far_rows(returned), flip(grad_across, "c"))
    grad_dispatched = [grad_sorted, grad_beside, grad_across, grad_corner]
    returned_far = flip(returned_far, "zl")
    returned_near = near_rows(returned)
    back_moe, grad_upward = moe_backward(table, grad_dispatched, slope, own_experts, new_experts)
    returned_far, back_moe[3] = tie(returned_far, back_moe[3])
    back_far, hidden = tie(far_rows(back_moe), hidden)
    back_far = flip(back_far, "zl")
    back_near = near_rows(back_moe)
    down_part, token = moe_weights(table, grad_dispatched, hidden, back_moe[3], experts)
    back_far, token = tie(back_far, token)
    expert_out = unsort_rows(order, returned_near + returned_far.astype(jnp.float32))
    mixed_two = (mixed_one + gate_used[:, None] * expert_out).astype(jnp.bfloat16)
    grad_gate = jnp.where(kept_rows, jnp.sum(upstream * expert_out, axis=-1), 0.0)
    grad_score = grad_gate * gate_prob * (1.0 - gate_prob)
    down_rest = lax.psum_scatter(down_part, high_bits, scatter_dimension=1, tiled=True)
    back_moe = back_near + back_far.astype(jnp.float32)
    grad_two = unsort_rows(order, back_moe) + grad_score[:, None] * centroid_rows
    centroid_part = jnp.einsum(
        "te,td->ed",
        hot_rows.astype(jnp.float32),
        grad_score[:, None] * normed_two_float,
        precision=highest,
    )
    moe_gain_part = jnp.sum(grad_two * unit_two, axis=0)
    grad_mixed = upstream + normalize_back(grad_two, unit_two, inverse_two, moe_gain)
    grad_mixed, grad_upward = tie(grad_mixed, grad_upward)
    up_part, _ = moe_weights(table, dispatched, grad_upward, token, experts)
    grad_att = gather_blocks(grad_mixed.astype(jnp.bfloat16))
    early = jnp.concatenate([moe_gain_part[None], centroid_part], axis=0)
    everyone = (*users, "zh", "zl")
    early = jnp.swapaxes(early.reshape(experts + 1, lax.axis_size(everyone), -1), 0, 1)
    early = jnp.sum(lax.all_to_all(early, everyone, 0, 0, tiled=True), axis=0)
    grad_att[2], early, up_part = tie(grad_att[2], early, up_part)
    grad_att[3] = flip(grad_att[2], "c")
    up_rest = lax.psum_scatter(up_part, high_bits, scatter_dimension=1, tiled=True)
    down_rest, mixed_two, grad_att[3] = tie(down_rest, mixed_two, grad_att[3])
    down_home = send_home(down_rest, 1)
    away_output = lax.ppermute(mixed_two, ("c", "zh"), [(1, 2), (2, 1)])
    *grad_one, weights_part = attention_backward(
        back_ranges, start, ranks, grad_att, normed_one, saved, qkv_used, proj_used
    )
    grad_one[3], away_output, *down_home = tie(grad_one[3], away_output, *down_home)
    one_far = far_rows(grad_one)
    one_near = near_rows(grad_one)

    def finish(far):
        grad = normalize_back(
            one_near + far.astype(jnp.float32), unit_one, inverse_one, attention_gain
        )
        return (grad_mixed + grad).astype(jnp.bfloat16)

    going = flip_some(one_far, False)
    weights_part = lax.psum_scatter(weights_part, high_bits, scatter_dimension=1, tiled=True)
    going, one_far, weights_part, *up_home = tie(
        going, one_far, weights_part, *send_home(up_rest, 1)
    )
    going, one_far, weights_part, away_output, *homes = tie(
        finish(going), one_far, weights_part, away_output, *down_home, *up_home
    )
    down_home, up_home = homes[:3], homes[3:]
    block_output = jnp.where(home, mixed_two, away_output)[None]
    going = lax.ppermute(going, ("c", "zh"), [(1, 2), (2, 1)])
    kept_far = flip_some(one_far, True)
    input_grad = jnp.where(home, finish(kept_far), going)[None]
    down_summed = jnp.swapaxes(sum_home(*down_home), 1, 2)
    up_summed = sum_home(*up_home)
    weights_part = sum_home(*send_home(weights_part, 1))
    qkv_summed, proj_summed = weights_part[:3], weights_part[3].T
    gain_two_sum, centroid_sum = early[0], early[1:]
    entries = gain_two_sum.shape[0]
    own_entries = lax.axis_index(everyone) * entries
    slice_rows = qkv_summed.shape[1]
    own_rows = lax.dynamic_slice_in_dim(
        qkv_weight, lax.axis_index(users) * slice_rows, slice_rows, 1
    )
    gain_one = jnp.sum(own_rows.astype(jnp.float32) * qkv_summed, axis=(0, 2))
    for bit in ("zh", "zl"):
        gain_one = halve(*send_half(gain_one, bit, 0))
    gain_one_sum = gain_one / lax.dynamic_slice_in_dim(attention_gain, own_entries, entries, 0)
    return (
        block_output,
        input_grad,
        gain_one_sum,
        gain_two_sum,
        centroid_sum,
        qkv_summed,
        proj_summed,
        up_summed,
        down_summed,
    )


def solution(mesh):
    shape = mesh.devices.shape
    high_bits = tuple(f"u{place}" for place in range((shape[0] // 2).bit_length() - 1))
    dp, tensor = (*high_bits, "c"), ("zh", "zl")
    mesh = Mesh(mesh.devices.reshape((2,) * len(dp + tensor)), dp + tensor)

    def program(*arguments):
        return body(high_bits, *arguments)

    return jax.shard_map(
        program,
        mesh=mesh,
        in_specs=(
            P(dp, tensor, None),
            P(),
            P(None, None, tensor),
            P(tensor, None),
            P(),
            P(),
            P(None, None, tensor),
            P(None, tensor, None),
            P(dp, tensor, None),
            P(dp, None, None),
            P(dp, None),
            P(dp, None),
        ),
        out_specs=(
            P(dp, tensor, None),
            P(dp, tensor, None),
            P(dp + tensor),
            P(dp + tensor),
            P(None, dp + tensor),
            P(None, dp, tensor),
            P(tensor, dp),
            P(None, dp, tensor),
            P(None, tensor, dp),
        ),
        check_vma=False,
    )
```

```python
import jax
import jax.numpy as jnp
from jax import lax
from jax.experimental import pallas as pl
from jax.experimental.pallas import tpu as pltpu
from jax.sharding import Mesh
from jax.sharding import PartitionSpec as P

HEAD_DIM = 64
FORWARD_BLOCKS = (512, 512)
BACKWARD_BLOCKS = (512, 256)
LOG2E = 1.4426950408889634
NEGATIVE = -1e30
TILE = 256
CHUNK = 256
TOKEN = (16, 128)
ALIGN = 16
CONTINUATIONS = 8
HBM = pl.BlockSpec(memory_space=pl.ANY)

epsilon = 1e-05
highest = lax.Precision.HIGHEST


def normalize_plain(values):
    centered = values - jnp.mean(values, axis=-1, keepdims=True)
    variance = jnp.mean(centered * centered, axis=-1, keepdims=True)
    inverse = lax.rsqrt(variance + epsilon)
    return (centered * inverse, inverse)


def normalize_back(upstream, unit_rows, inverse, gain_row):
    scaled = upstream * gain_row
    centered = scaled - jnp.mean(scaled, axis=-1, keepdims=True)
    return inverse * (centered - unit_rows * jnp.mean(scaled * unit_rows, axis=-1, keepdims=True))


def matmul(a, b, dims=((1,), (0,))):
    return lax.dot_general(a, b, (dims, ((), ())), preferred_element_type=jnp.float32)


def key_ranges(segment, blocks):
    block, fine = blocks
    token_count = segment.shape[0]
    numbers = jnp.arange(1, CONTINUATIONS + 1, dtype=jnp.int32)[:, None]
    earlier = jnp.sum((segment[None, :] < numbers).astype(jnp.int32), axis=1, keepdims=True)
    prompt = earlier[0, 0]
    start = jnp.sum(jnp.where(segment[None, :] == numbers, earlier, 0), axis=0)
    first = jnp.arange(token_count // block, dtype=jnp.int32) * block
    whole = jnp.minimum(prompt, first) // fine
    shared = (jnp.minimum(prompt, first + block) + fine - 1) // fine
    own = jnp.maximum(shared, start.reshape(-1, block)[:, 0] // fine)
    last = (first + block) // fine
    return (jnp.stack([whole, shared, own, last, jnp.full_like(whole, prompt)]), start[None, :])


def copies(pairs, semaphores):
    moved = [
        pltpu.make_async_copy(source, target, semaphores.at[place])
        for place, (source, target) in enumerate(pairs)
    ]
    for copy in moved:
        copy.start()
    for copy in moved:
        copy.wait()


def rank_rows(ref, rank, like):
    count = like.shape[0]
    return ref.at[pl.ds(pl.multiple_of(rank * count, count), count)]


def send_ranks(ref, targets, ranks, semaphores, edge, block, down):
    count = targets[0].shape[0]
    for rank in range(4):
        if down:
            first = rank * count
            due = (edge <= first) & (edge + block > first)
        else:
            last = (rank + 1) * count
            due = (edge >= last) & (edge - block < last)

        @pl.when(due)
        def _(rank=rank):
            for b, target in enumerate(targets):

                @pl.when(ranks[b] == rank)
                def _(b=b, target=target):
                    source = ref.at[rank * count : (rank + 1) * count]
                    pltpu.make_async_copy(source, target, semaphores.at[b]).start()


def take_ranks(ref, sources, ranks, semaphores, edge, block, first):
    count = sources[0].shape[0]

    @pl.when(first)
    def _():
        for b, source in enumerate(sources):
            target = rank_rows(ref, ranks[b], source)
            pltpu.make_async_copy(source, target, semaphores.at[b]).start()

    for b, source in enumerate(sources):
        begin = ranks[b] * count
        before = jnp.where(first, 0, edge)

        @pl.when((begin >= before) & (begin < edge + block))
        def _(b=b, source=source):
            target = rank_rows(ref, ranks[b], source)
            pltpu.make_async_copy(source, target, semaphores.at[b]).wait()


def await_ranks(ref, targets, ranks, semaphores):
    for b, target in enumerate(targets):
        pltpu.make_async_copy(rank_rows(ref, ranks[b], target), target, semaphores.at[b]).wait()


def forward_kernel(
    ranges, ranks, x0, x1, x2, x3, w_ref, proj_ref, start_ref,
    p0, p1, p2, p3, qt_ref, k_ref, kt_ref, v_ref, ctx_ref, lse_ref,
    x_ref, part_ref, vt_ref, score_ref, top_ref, sum_ref, arrived, left,
):
    step = pl.program_id(0)
    heads = qt_ref.shape[0]
    block = qt_ref.shape[2]
    fine = vt_ref.shape[3]
    step_keys = kt_ref.shape[3]
    rows = pl.ds(pl.multiple_of(step * block, block), block)

    take_ranks(x_ref, (x0, x1, x2, x3), ranks, arrived, step * block, block, step == 0)
    x = x_ref[rows, :]
    for kind in range(3):
        made = matmul(x, w_ref[kind]).astype(jnp.bfloat16)
        turned = made.T
        for head in range(heads):
            part = slice(head * HEAD_DIM, (head + 1) * HEAD_DIM)
            if kind == 0:
                qt_ref[head] = turned[part]
            if kind == 1:
                k_ref[head, rows, :] = made[:, part]
            if kind == 2:
                v_ref[head, rows, :] = made[:, part]
            for piece in range(block // step_keys if kind == 1 else 0):
                columns = slice(piece * step_keys, (piece + 1) * step_keys)
                kt_ref[piece, head] = turned[part, columns]
            for piece in range(block // fine if kind == 2 else 0):
                columns = slice(piece * fine, (piece + 1) * fine)
                at = step * (block // fine) + piece
                vt_ref[at, head, :HEAD_DIM] = turned[part, columns]
                vt_ref[at, head, HEAD_DIM:] = jnp.ones((16, fine), jnp.bfloat16)
    top_ref[...] = jnp.full_like(top_ref, NEGATIVE)
    sum_ref[...] = jnp.zeros_like(sum_ref)
    prompt = ranges[4, step]
    scale = LOG2E * HEAD_DIM ** (-0.5)

    def visit(key, masked):
        place = pl.ds(pl.multiple_of(key * fine, fine), fine)
        if masked:
            key_at = key * fine + lax.broadcasted_iota(jnp.int32, (fine, block), 0)
            query_at = step * block + lax.broadcasted_iota(jnp.int32, (fine, block), 1)
            seen = (key_at <= query_at) & ((key_at < prompt) | (key_at >= start_ref[...]))
        for head in range(heads):
            scores = matmul(k_ref[head, place, :], qt_ref[head])
            if masked:
                scores = jnp.where(seen, scores, NEGATIVE)
            score_ref[key, head] = scores
            top_ref[head] = jnp.maximum(
                top_ref[head], jnp.max(scores.reshape(fine // 8, 8, block), axis=0)
            )

    def plain(key, carry):
        visit(key, False)
        return carry

    def edge(key, carry):
        visit(key, True)
        return carry

    lax.fori_loop(0, ranges[0, step], plain, 0)
    lax.fori_loop(ranges[0, step], ranges[1, step], edge, 0)
    lax.fori_loop(ranges[2, step], ranges[3, step], edge, 0)
    for head in range(heads):
        top_ref[head, :1] = jnp.max(top_ref[head], axis=0, keepdims=True) * scale

    def add(key, carry):
        for head in range(heads):
            weights = jnp.exp2(score_ref[key, head] * scale - top_ref[head, :1])
            sum_ref[head] += matmul(vt_ref[key, head], weights.astype(jnp.bfloat16))
        return carry

    lax.fori_loop(0, ranges[1, step], add, 0)
    lax.fori_loop(ranges[2, step], ranges[3, step], add, 0)
    for head in range(heads):
        total = sum_ref[head, HEAD_DIM : HEAD_DIM + 1]
        context = sum_ref[head, :HEAD_DIM] / total
        ctx_ref[head * HEAD_DIM : (head + 1) * HEAD_DIM] = context.astype(jnp.bfloat16)
        lse_ref[head] = top_ref[head, :1] + jnp.log(total) * LOG2E
    part_ref[rows, :] = matmul(ctx_ref[...], proj_ref[...], ((0,), (0,))).astype(jnp.bfloat16)
    send_ranks(part_ref, (p0, p1, p2, p3), ranks, left, (step + 1) * block, block, False)

    @pl.when(step == pl.num_programs(0) - 1)
    def _():
        await_ranks(part_ref, (p0, p1, p2, p3), ranks, left)


def attention_forward(ranges, start, ranks, x, w, proj):
    tokens, width = start.shape[1], x[0].shape[1]
    local = w.shape[2]
    heads = local // HEAD_DIM
    block, fine = FORWARD_BLOCKS
    step_keys = BACKWARD_BLOCKS[1]
    count = tokens // block
    low = jnp.bfloat16
    head_rows = pl.BlockSpec((heads, tokens, HEAD_DIM), lambda i, r, n: (0, 0, 0))
    flops = 2 * tokens * width * local * 4 + tokens * tokens * local * 2
    return pl.pallas_call(
        forward_kernel,
        grid_spec=pltpu.PrefetchScalarGridSpec(
            num_scalar_prefetch=2,
            grid=(count,),
            in_specs=[
                *[HBM] * 4,
                pl.BlockSpec((3, width, local), lambda i, r, n: (0, 0, 0)),
                pl.BlockSpec((local, width), lambda i, r, n: (0, 0)),
                pl.BlockSpec((1, block), lambda i, r, n: (0, i)),
            ],
            out_specs=[
                *[HBM] * 4,
                pl.BlockSpec((heads, HEAD_DIM, block), lambda i, r, n: (0, 0, i)),
                head_rows,
                pl.BlockSpec(
                    (block // step_keys, heads, HEAD_DIM, step_keys), lambda i, r, n: (i, 0, 0, 0)
                ),
                head_rows,
                pl.BlockSpec((local, block), lambda i, r, n: (0, i)),
                pl.BlockSpec((heads, 1, block), lambda i, r, n: (0, 0, i)),
            ],
            scratch_shapes=[
                pltpu.VMEM((tokens, width), low),
                pltpu.VMEM((tokens, width), low),
                pltpu.VMEM((tokens // fine, heads, HEAD_DIM + 16, fine), low),
                pltpu.VMEM((tokens // fine, heads, fine, block), jnp.float32),
                pltpu.VMEM((heads, 8, block), jnp.float32),
                pltpu.VMEM((heads, HEAD_DIM + 16, block), jnp.float32),
                pltpu.SemaphoreType.DMA((4,)),
                pltpu.SemaphoreType.DMA((4,)),
            ],
        ),
        out_shape=[
            *[jax.ShapeDtypeStruct(x[0].shape, low)] * 4,
            jax.ShapeDtypeStruct((heads, HEAD_DIM, tokens), low),
            jax.ShapeDtypeStruct((heads, tokens, HEAD_DIM), low),
            jax.ShapeDtypeStruct((tokens // step_keys, heads, HEAD_DIM, step_keys), low),
            jax.ShapeDtypeStruct((heads, tokens, HEAD_DIM), low),
            jax.ShapeDtypeStruct((local, tokens), low),
            jax.ShapeDtypeStruct((heads, 1, tokens), jnp.float32),
        ],
        compiler_params=pltpu.CompilerParams(vmem_limit_bytes=56 << 20),
        cost_estimate=pl.CostEstimate(
            flops=4 * flops, transcendentals=tokens * tokens * heads // 2, bytes_accessed=40 << 20
        ),
        name="attention_forward",
    )(ranges, ranks, *x, w, proj, start)


def backward_kernel(
    ranges, ranks, g0, g1, g2, g3, x0, x1, x2, x3,
    ctx_ref, lse_ref, qt_ref, start_ref, k_ref, kt_ref, v_ref, w_ref, proj_ref,
    p0, p1, p2, p3, weights_ref,
    g_ref, x_ref, part_ref, wgrad_ref, pgrad_ref,
    dk_ref, dv_ref, dq_ref, outer_ref, inner_ref, grad_ref, prob_ref, dscore_ref, arrived, left,
):
    number = pl.program_id(0)
    step = pl.num_programs(0) - 1 - number
    heads = qt_ref.shape[0]
    block = qt_ref.shape[2]
    fine = kt_ref.shape[3]
    local = heads * HEAD_DIM
    rows = pl.ds(pl.multiple_of(step * block, block), block)

    @pl.when(number == 0)
    def _():
        for place, (ref, sources) in enumerate(((g_ref, (g0, g1, g2, g3)), (x_ref, (x0, x1, x2, x3)))):
            for b, source in enumerate(sources):
                target = rank_rows(ref, ranks[b], source)
                pltpu.make_async_copy(source, target, arrived.at[place, b]).start()
        dk_ref[...] = jnp.zeros_like(dk_ref)
        dv_ref[...] = jnp.zeros_like(dv_ref)
        wgrad_ref[...] = jnp.zeros_like(wgrad_ref)
        pgrad_ref[...] = jnp.zeros_like(pgrad_ref)
        await_copies(g_ref, (g0, g1, g2, g3), ranks, arrived.at[0])

    upstream = g_ref[rows, :]
    outer = matmul(upstream, proj_ref[...], ((1,), (1,))).astype(jnp.bfloat16).T
    for head in range(heads):
        part = slice(head * HEAD_DIM, (head + 1) * HEAD_DIM)
        outer_ref[head] = outer[part]
        inner_ref[head] = jnp.sum(
            outer[part].astype(jnp.float32) * ctx_ref[part].astype(jnp.float32),
            axis=0,
            keepdims=True,
        )
    pgrad_ref[...] += matmul(ctx_ref[...], upstream)
    dq_ref[...] = jnp.zeros_like(dq_ref)
    prompt = ranges[4, step]
    scale = LOG2E * HEAD_DIM ** (-0.5)

    def add(key, head):
        prob, dscore = prob_ref[head], dscore_ref[head]
        dv_ref[key, head] += matmul(outer_ref[head], prob, ((1,), (1,)))
        dk_ref[key, head] += matmul(qt_ref[head], dscore, ((1,), (1,)))
        dq_ref[head] += matmul(kt_ref[key, head], dscore)

    def visit(number, before, masked):
        key = jnp.where(number < ranges[1, step], number, number - ranges[1, step] + ranges[2, step])
        place = pl.ds(pl.multiple_of(key * fine, fine), fine)
        if masked:
            key_at = key * fine + lax.broadcasted_iota(jnp.int32, (fine, block), 0)
            query_at = step * block + lax.broadcasted_iota(jnp.int32, (fine, block), 1)
            seen = (key_at <= query_at) & ((key_at < prompt) | (key_at >= start_ref[...]))
        for head in range(heads):
            scores = matmul(k_ref[head, place, :], qt_ref[head]) * scale
            dprob = matmul(v_ref[head, place, :], outer_ref[head])
            if before is not None:
                add(before, head)
            if masked:
                scores = jnp.where(seen, scores, NEGATIVE)
            prob = jnp.exp2(scores - lse_ref[head])
            prob_ref[head] = prob.astype(jnp.bfloat16)
            dscore_ref[head] = (prob * (dprob - inner_ref[head])).astype(jnp.bfloat16)
        return key

    visits = ranges[1, step] + ranges[3, step] - ranges[2, step]
    plain = jnp.maximum(ranges[0, step], 1)
    key = visit(0, None, True)
    key = lax.fori_loop(1, plain, lambda number, before: visit(number, before, False), key)
    key = lax.fori_loop(plain, visits, lambda number, before: visit(number, before, True), key)
    for head in range(heads):
        add(key, head)
    small = HEAD_DIM ** (-0.5)

    @pl.when(number == 0)
    def _():
        await_copies(x_ref, (x0, x1, x2, x3), ranks, arrived.at[1])

    for head in range(heads):
        part = slice(head * HEAD_DIM, (head + 1) * HEAD_DIM)
        grad_ref[0, part] = (dq_ref[head] * small).astype(jnp.bfloat16)
        for piece in range(block // fine):
            at = step * (block // fine) + piece
            columns = slice(piece * fine, (piece + 1) * fine)
            grad_ref[1, part, columns] = (dk_ref[at, head] * small).astype(jnp.bfloat16)
            grad_ref[2, part, columns] = dv_ref[at, head].astype(jnp.bfloat16)
    x = x_ref[rows, :]
    total = None
    for kind in range(3):
        wgrad_ref[kind] += matmul(grad_ref[kind], x)
        term = matmul(grad_ref[kind].T, w_ref[kind], ((1,), (1,)))
        total = term if total is None else total + term
    part_ref[rows, :] = total.astype(jnp.bfloat16)
    send_ranks(part_ref, (p0, p1, p2, p3), ranks, left, step * block, block, True)

    @pl.when(step == 0)
    def _():
        for kind in range(3):
            weights_ref[kind] = wgrad_ref[kind].T.astype(jnp.bfloat16)
        weights_ref[3] = pgrad_ref[...].T.astype(jnp.bfloat16)
        await_ranks(part_ref, (p0, p1, p2, p3), ranks, left)


def await_copies(ref, sources, ranks, semaphores):
    for b, source in enumerate(sources):
        target = rank_rows(ref, ranks[b], source)
        pltpu.make_async_copy(source, target, semaphores.at[b]).wait()


def attention_backward(ranges, start, ranks, upstream, x, saved, w, proj):
    qt, k, kt, v, ctx, lse = saved
    tokens, width = start.shape[1], x[0].shape[1]
    local = w.shape[2]
    heads = local // HEAD_DIM
    block, fine = BACKWARD_BLOCKS
    count = tokens // block
    low = jnp.bfloat16

    def at(i):
        return count - 1 - i

    head_rows = pl.BlockSpec((heads, tokens, HEAD_DIM), lambda i, r, n: (0, 0, 0))
    flops = 2 * tokens * width * local * 8 + tokens * tokens * local * 5
    return pl.pallas_call(
        backward_kernel,
        grid_spec=pltpu.PrefetchScalarGridSpec(
            num_scalar_prefetch=2,
            grid=(count,),
            in_specs=[
                *[HBM] * 8,
                pl.BlockSpec((local, block), lambda i, r, n: (0, at(i))),
                pl.BlockSpec((heads, 1, block), lambda i, r, n: (0, 0, at(i))),
                pl.BlockSpec((heads, HEAD_DIM, block), lambda i, r, n: (0, 0, at(i))),
                pl.BlockSpec((1, block), lambda i, r, n: (0, at(i))),
                head_rows,
                pl.BlockSpec((tokens // fine, heads, HEAD_DIM, fine), lambda i, r, n: (0, 0, 0, 0)),
                head_rows,
                pl.BlockSpec((3, width, local), lambda i, r, n: (0, 0, 0)),
                pl.BlockSpec((local, width), lambda i, r, n: (0, 0)),
            ],
            out_specs=[
                *[HBM] * 4,
                pl.BlockSpec((4, width, local), lambda i, r, n: (0, 0, 0)),
            ],
            scratch_shapes=[
                pltpu.VMEM((tokens, width), low),
                pltpu.VMEM((tokens, width), low),
                pltpu.VMEM((tokens, width), low),
                pltpu.VMEM((3, local, width), jnp.float32),
                pltpu.VMEM((local, width), jnp.float32),
                pltpu.VMEM((tokens // fine, heads, HEAD_DIM, fine), jnp.float32),
                pltpu.VMEM((tokens // fine, heads, HEAD_DIM, fine), jnp.float32),
                pltpu.VMEM((heads, HEAD_DIM, block), jnp.float32),
                pltpu.VMEM((heads, HEAD_DIM, block), low),
                pltpu.VMEM((heads, 1, block), jnp.float32),
                pltpu.VMEM((3, local, block), low),
                pltpu.VMEM((heads, fine, block), low),
                pltpu.VMEM((heads, fine, block), low),
                pltpu.SemaphoreType.DMA((2, 4)),
                pltpu.SemaphoreType.DMA((4,)),
            ],
        ),
        out_shape=[
            *[jax.ShapeDtypeStruct(x[0].shape, low)] * 4,
            jax.ShapeDtypeStruct((4, width, local), low),
        ],
        compiler_params=pltpu.CompilerParams(vmem_limit_bytes=56 << 20),
        cost_estimate=pl.CostEstimate(
            flops=4 * flops, transcendentals=tokens * tokens * heads // 2, bytes_accessed=40 << 20
        ),
        name="attention_backward",
    )(ranges, ranks, *upstream, *x, ctx, lse, qt, start, k, kt, v, w, proj)


def route_rows(route, priority, experts, capacity, row_count, ranks):
    own_start = ranks[0] * row_count
    own_route = lax.dynamic_slice_in_dim(route, own_start, row_count, 0)
    own_priority = lax.dynamic_slice_in_dim(priority, own_start, row_count, 0)
    ahead = (route[None, :] == own_route[:, None]) & (priority[None, :] < own_priority[:, None])
    kept = jnp.sum(ahead.astype(jnp.int32), axis=1) < capacity
    kinds = jnp.arange(experts, dtype=jnp.int32)
    block_hot = (route.reshape(-1, row_count)[:, :, None] == kinds).astype(jnp.int32)
    lengths = jnp.sum(block_hot, axis=1)
    starts = jnp.cumsum(lengths, axis=1) - lengths
    own_hot = (own_route[:, None] == kinds).astype(jnp.int32)
    index = jnp.arange(row_count, dtype=jnp.int32)
    before = (own_route[None, :] == own_route[:, None]) & (index[None, :] < index[:, None])
    own_starts = lax.dynamic_slice_in_dim(starts, ranks[0], 1, 0)
    place = jnp.sum(before.astype(jnp.int32), axis=1) + jnp.sum(own_hot * own_starts, axis=1)
    order = (index[:, None] == place[None, :]).astype(jnp.bfloat16)
    picked = [
        lax.dynamic_slice_in_dim(array, ranks[b], 1, 0)[0]
        for array in (starts, lengths)
        for b in range(4)
    ]
    home = at_home().astype(jnp.int32)[None]
    return (kept, order, jnp.concatenate([*picked, home]), own_hot)


def sort_rows(order, rows):
    return jnp.dot(order, rows, preferred_element_type=jnp.float32).astype(jnp.bfloat16)


def unsort_rows(order, rows):
    return matmul(order, rows.astype(jnp.bfloat16), ((0,), (0,)))


def each_tile(table, block, expert, experts, visit):
    start = table[block * experts + expert]
    end = start + table[(4 + block) * experts + expert]
    first = start // ALIGN * ALIGN

    def tile(number, carry):
        at = first + number * TILE
        visit(pl.ds(pl.multiple_of(at, ALIGN), TILE), start - at, end - at)
        return carry

    lax.fori_loop(0, jnp.where(end > start, (end - first + TILE - 1) // TILE, 0), tile, 0)


def put_rows(ref, block, place, rows, head):
    top = pl.ds(place.start, ALIGN)
    old = ref[block, top, :]
    index = lax.broadcasted_iota(jnp.int32, old.shape, 0)
    ref[block, place, :] = rows
    ref[block, top, :] = jnp.where(index < head, old, rows[:ALIGN])


def fetch_weights(choice, kept, given, targets, semaphores):
    for place, target in enumerate(targets):
        for expert in range(target.shape[0]):
            ready = semaphores.at[place, expert]

            @pl.when(choice == 1)
            def _(place=place, target=target, expert=expert, ready=ready):
                pltpu.make_async_copy(kept[place].at[expert], target.at[expert], ready).start()

            @pl.when(choice == 0)
            def _(place=place, target=target, expert=expert, ready=ready):
                pltpu.make_async_copy(given[place].at[expert], target.at[expert], ready).start()


def await_weights(kept, targets, expert, semaphores):
    for place, target in enumerate(targets):
        pltpu.make_async_copy(
            kept[place].at[expert], target.at[expert], semaphores.at[place, expert]
        ).wait()


def within(rows, head, end):
    index = lax.broadcasted_iota(jnp.int32, rows.shape, 0)
    return jnp.where((index >= head) & (index < end), rows, 0)


def block_copies(block, pairs, semaphores):
    for place, (source, targets) in enumerate(pairs):
        for b in range(4):

            @pl.when(block == b)
            def _(place=place, source=source, targets=targets, b=b):
                target = targets[b] if isinstance(targets, tuple) else targets.at[b]
                rows = source.at[b, : target.shape[0]]
                pltpu.make_async_copy(rows, target, semaphores.at[place, b]).start()


def await_blocks(pairs, semaphores):
    for place, (source, targets) in enumerate(pairs):
        for b in range(4):
            target = targets[b] if isinstance(targets, tuple) else targets.at[b]
            rows = source.at[b, : target.shape[0]]
            pltpu.make_async_copy(rows, target, semaphores.at[place, b]).wait()


def moe_steps(table, experts, inputs, weights, outputs, tails, visit, semaphores):
    block = pl.program_id(0)
    kept, given, held = weights
    arrived, left, ready = semaphores
    count = inputs[0][1][0].shape[0]

    @pl.when(block == 0)
    def _():
        for place, (target, sources) in enumerate(inputs):
            for b in range(4):
                source = sources[b] if isinstance(sources, tuple) else sources.at[b]
                rows = target.at[b, : source.shape[0]]
                pltpu.make_async_copy(source, rows, arrived.at[place, b]).start()
        fetch_weights(table[8 * experts], kept, given, held, ready)
        for ref in tails:
            ref[:, count:, :] = jnp.zeros((4, TILE, ref.shape[2]), ref.dtype)

    for place, (target, sources) in enumerate(inputs):
        source = sources[0] if isinstance(sources, tuple) else sources.at[0]
        rows = target.at[block, : source.shape[0]]
        pltpu.make_async_copy(source, rows, arrived.at[place, block]).wait()

    def expert_rows(expert, carry):
        @pl.when(block == 0)
        def _():
            await_weights(kept, held, expert, ready)

        each_tile(
            table, block, expert, experts,
            lambda place, head, end: visit(block, expert, place, head, end),
        )
        return carry

    lax.fori_loop(0, experts, expert_rows, 0)
    block_copies(block, outputs, left)

    @pl.when(block == 3)
    def _():
        await_blocks(outputs, left)


def moe_forward_kernel(
    table, x0, x1, x2, x3, own_up, own_down, new_up, new_down,
    y0, y1, y2, y3, hidden_out, slope_out,
    x_ref, y_ref, hidden_ref, slope_ref, up_ref, down_ref, *semaphores,
):
    width = up_ref.shape[2]

    def visit(block, expert, place, head, end):
        x = x_ref[block, place, :]
        total = None
        for part in range(0, width, CHUNK):
            chunk = slice(part, part + CHUNK)
            u = matmul(x, up_ref[expert, :, chunk])
            cube = 0.7978845608028654 * u * (1.0 + 0.044715 * u * u)
            bend = 1.0 + jnp.tanh(cube)
            half = 0.5 * bend
            hidden = (u * half).astype(jnp.bfloat16)
            slope = half + u * (half * (2.0 - bend)) * (
                0.7978845608028654 * (1.0 + 3.0 * 0.044715 * u * u)
            )
            put_rows(hidden_ref.at[:, :, chunk], block, place, hidden, head)
            put_rows(slope_ref.at[:, :, chunk], block, place, slope.astype(jnp.bfloat16), head)
            term = matmul(hidden, down_ref[expert, chunk, :])
            total = term if total is None else total + term
        put_rows(y_ref, block, place, total.astype(jnp.bfloat16), head)

    moe_steps(
        table, up_ref.shape[0], [(x_ref, (x0, x1, x2, x3))],
        ((own_up, own_down), (new_up, new_down), (up_ref, down_ref)),
        [(y_ref, (y0, y1, y2, y3)), (hidden_ref, hidden_out), (slope_ref, slope_out)],
        (x_ref, hidden_ref, slope_ref), visit, semaphores,
    )


def moe_backward_kernel(
    table, d0, d1, d2, d3, slope_in, own_up, own_down, new_up, new_down,
    y0, y1, y2, y3, grad_out,
    d_ref, slope_ref, y_ref, grad_ref, up_ref, down_ref, *semaphores,
):
    width = up_ref.shape[2]

    def visit(block, expert, place, head, end):
        upstream = within(d_ref[block, place, :], head, end)
        total = None
        for part in range(0, width, CHUNK):
            chunk = slice(part, part + CHUNK)
            slope = slope_ref[block, place, chunk].astype(jnp.float32)
            grad = matmul(upstream, down_ref[expert, chunk, :], ((1,), (1,))) * slope
            grad = grad.astype(jnp.bfloat16)
            put_rows(grad_ref.at[:, :, chunk], block, place, grad, head)
            term = matmul(grad, up_ref[expert, :, chunk], ((1,), (1,)))
            total = term if total is None else total + term
        put_rows(y_ref, block, place, total.astype(jnp.bfloat16), head)

    moe_steps(
        table, up_ref.shape[0], [(d_ref, (d0, d1, d2, d3)), (slope_ref, slope_in)],
        ((own_up, own_down), (new_up, new_down), (up_ref, down_ref)),
        [(y_ref, (y0, y1, y2, y3)), (grad_ref, grad_out)],
        (d_ref, grad_ref), visit, semaphores,
    )


def moe_weights_kernel(
    table, a0, a1, a2, a3, b_in, token_in, out_ref, token_ref, a_ref, b_ref, sum_ref, semaphores
):
    expert = pl.program_id(0)
    experts = pl.num_programs(0)
    count = a0.shape[0]

    @pl.when(expert == 0)
    def _():
        token_ref[...] = jnp.zeros_like(token_ref)
        a_ref[:, count:, :] = jnp.zeros((4, TILE, a_ref.shape[2]), jnp.bfloat16)
        copies(
            [(a, a_ref.at[b, :count]) for b, a in enumerate((a0, a1, a2, a3))] + [(b_in, b_ref)],
            semaphores,
        )

    sum_ref[...] = jnp.zeros_like(sum_ref)

    def of_block(block, carry):
        def visit(place, head, end):
            rows = within(a_ref[block, place, :], head, end)
            sum_ref[...] += matmul(rows, b_ref[block, place, :], ((0,), (0,)))

        each_tile(table, block, expert, experts, visit)
        return carry

    lax.fori_loop(0, 4, of_block, 0)
    out_ref[0] = sum_ref[...].astype(jnp.bfloat16)


def moe_call(kernel, name, table, arrays, grid, specs, outs, scratch, semaphores, cost):
    return pl.pallas_call(
        kernel,
        grid_spec=pltpu.PrefetchScalarGridSpec(
            num_scalar_prefetch=1,
            grid=(grid,),
            in_specs=[HBM] * len(arrays),
            out_specs=specs,
            scratch_shapes=[
                *[pltpu.VMEM(*shape) for shape in scratch],
                *[pltpu.SemaphoreType.DMA(shape) for shape in semaphores],
            ],
        ),
        out_shape=[jax.ShapeDtypeStruct(shape, jnp.bfloat16) for shape in outs],
        compiler_params=pltpu.CompilerParams(vmem_limit_bytes=58 << 20),
        cost_estimate=pl.CostEstimate(flops=cost, transcendentals=0, bytes_accessed=40 << 20),
        name=name,
    )(table, *arrays)


def moe_forward(table, x, own, new):
    count, width = x[0].shape
    experts, _, hidden = own[0].shape
    low = jnp.bfloat16
    wide, tall = ((4, count + TILE, width), low), ((4, count + TILE, hidden), low)
    *y, hid, slope = moe_call(
        moe_forward_kernel, "moe_forward", table, [*x, *own, *new], 4, [HBM] * 6,
        [(count, width)] * 4 + [tall[0], tall[0]],
        [wide, wide, tall, tall, (own[0].shape, low), (own[1].shape, low)],
        [(1, 4), (3, 4), (2, experts)], 20 * count * width * hidden,
    )
    return (y, hid, slope)


def moe_backward(table, d, slope, own, new):
    count, width = d[0].shape
    experts, _, hidden = own[0].shape
    low = jnp.bfloat16
    wide, tall = ((4, count + TILE, width), low), ((4, count + TILE, hidden), low)
    *y, grad = moe_call(
        moe_backward_kernel, "moe_backward", table, [*d, slope, *own, *new], 4, [HBM] * 5,
        [(count, width)] * 4 + [tall[0]],
        [wide, tall, wide, tall, (own[0].shape, low), (own[1].shape, low)],
        [(2, 4), (2, 4), (2, experts)], 20 * count * width * hidden,
    )
    return (y, grad)


def moe_weights(table, blocks, tall, token, experts):
    count, width = blocks[0].shape
    hidden = tall.shape[2]
    return moe_call(
        moe_weights_kernel, "moe_weights", table, [*blocks, tall, token], experts,
        [
            pl.BlockSpec((1, width, hidden), lambda e, t: (e, 0, 0)),
            pl.BlockSpec(TOKEN, lambda e, t: (0, 0)),
        ],
        [(experts, width, hidden), TOKEN],
        [((4, count + TILE, width), jnp.bfloat16), (tall.shape, jnp.bfloat16),
         ((width, hidden), jnp.float32)],
        [(5,)], 10 * count * width * hidden,
    )


def at_home():
    return lax.axis_index("c") == lax.axis_index("zh")


def swap_roles(value):
    moved = lax.ppermute(value, ("c", "zh"), [(1, 2), (2, 1)])
    return jnp.where(at_home(), value, moved)


def flip(value, axis):
    return lax.ppermute(value, axis, [(0, 1), (1, 0)])


def flip_some(value, home):
    moves = [(0, 1), (1, 0), (6, 7), (7, 6)] if home else [(2, 3), (3, 2), (4, 5), (5, 4)]
    return lax.ppermute(value, ("c", "zh", "zl"), moves)


def tie(*values):
    return lax.optimization_barrier(values)


def gather_blocks(rows):
    across = flip(rows, "zl")
    return [rows, flip(rows, "c"), across, flip(across, "c")]


def far_rows(blocks):
    return (
        flip(blocks[3], "c").astype(jnp.float32) + blocks[2].astype(jnp.float32)
    ).astype(blocks[2].dtype)


def near_rows(blocks):
    return blocks[0].astype(jnp.float32) + flip(blocks[1], "c").astype(jnp.float32)


def scatter_blocks(blocks):
    return near_rows(blocks) + flip(far_rows(blocks), "zl").astype(jnp.float32)


def send_half(value, axis, dimension):
    count = value.shape[dimension] // 2
    side = lax.axis_index(axis)
    kept = lax.dynamic_slice_in_dim(value, side * count, count, dimension)
    sent = lax.dynamic_slice_in_dim(value, (1 - side) * count, count, dimension)
    return [kept, flip(sent, axis)]


def halve(kept, came):
    return (kept.astype(jnp.float32) + came.astype(jnp.float32)).astype(kept.dtype)


def send_home(value, dimension):
    count = value.shape[dimension] // 2
    high = lax.axis_index("zh")
    straight = lax.dynamic_slice_in_dim(value, high * count, count, dimension)
    turned = lax.dynamic_slice_in_dim(value, (1 - high) * count, count, dimension)
    turned = lax.ppermute(turned, ("c", "zh"), [(0, 2), (1, 0), (2, 3), (3, 1)])
    return [straight, lax.ppermute(straight, ("c", "zh"), [(1, 2), (2, 1)]), turned]


def sum_home(straight, moved, turned):
    straight = jnp.where(at_home(), straight, moved)
    return straight.astype(jnp.float32) + turned.astype(jnp.float32)


def piece_of(weight, users):
    flat = weight.reshape(-1, weight.shape[-1])
    part = flat.shape[0] // lax.axis_size(users)
    return lax.dynamic_slice_in_dim(flat, lax.axis_index(users) * part, part, 0)


def share(piece, users, shape):
    return lax.all_gather(piece, users, axis=0, tiled=True).reshape(shape)


def share_small(piece, users, shape):
    for bit in reversed(users):
        given = flip(piece, bit)
        low = lax.axis_index(bit) == 0
        piece = jnp.concatenate([jnp.where(low, piece, given), jnp.where(low, given, piece)], axis=0)
    return piece.reshape(shape)


def body(
    high_bits,
    block_input,
    attention_gain,
    qkv_weight,
    proj_weight,
    moe_gain,
    centroids,
    expert_up,
    expert_down,
    out_grad,
    routes,
    priority,
    segments,
):
    row_count = block_input.shape[1]
    model_width = block_input.shape[2]
    experts = expert_up.shape[0]
    token_count = segments.shape[1]
    capacity = 9 * token_count // (8 * experts)
    local_width = qkv_weight.shape[2]
    users = (*high_bits, "c")
    core, near = lax.axis_index("c"), lax.axis_index("zl")
    ranks = jnp.stack(
        [2 * core + near, 2 * (1 - core) + near, 2 * core + 1 - near, 3 - 2 * core - near]
    )
    home = at_home()
    staying = block_input[0]
    coming = lax.ppermute(staying, ("c", "zh"), [(1, 2), (2, 1)])
    small = jnp.concatenate([qkv_weight, proj_weight.reshape(1, model_width, local_width)], axis=0)
    small_piece = flip(piece_of(small, users), "zh")

    def normed(rows):
        return (normalize_plain(rows.astype(jnp.float32))[0] * attention_gain).astype(jnp.bfloat16)

    normed_staying = normed(staying)
    home_across = flip_some(normed_staying, True)
    indices = jnp.stack([routes[0, :, 0], priority[0], segments[0]])
    indices = jnp.where(home, indices, flip(indices, "c"))
    segment = indices[2]
    ranges, start = key_ranges(segment, FORWARD_BLOCKS)
    coming, small_piece, home_across, ranges, start = tie(
        coming, small_piece, home_across, ranges, start
    )
    small_other = share(small_piece, users, small.shape)
    normed_coming = normed(coming)
    away_across = flip_some(normed_coming, False)
    across = jnp.where(home, home_across, away_across)
    across, up_piece, down_piece = tie(
        across, piece_of(expert_up, users), piece_of(expert_down, users)
    )
    up_piece, down_piece = flip(up_piece, "zh"), flip(down_piece, "zh")
    normed_one = jnp.where(home, normed_staying, normed_coming)
    normed_one = [normed_one, flip(normed_one, "c"), across, flip(across, "c")]
    inputs = jnp.where(home, staying, coming).astype(jnp.float32)
    unit_one, inverse_one = normalize_plain(inputs)
    small = jnp.where(home, small, small_other)
    qkv_used, proj_used = small[:3], small[3].reshape(local_width, model_width)
    *attended, qt, k, kt, v, ctx, lse = attention_forward(
        ranges, start, ranks, normed_one, qkv_used, proj_used
    )
    saved = (qt, k, kt, v, ctx, lse)
    attended[3], up_piece, down_piece, indices, upstream = tie(
        attended[3], up_piece, down_piece, indices, out_grad[0]
    )
    away_upstream = lax.ppermute(upstream, ("c", "zh"), [(1, 2), (2, 1)])
    new_experts = [share(piece, users, expert_up.shape) for piece in (up_piece, down_piece)]
    back_ranges = key_ranges(indices[2], BACKWARD_BLOCKS)[0]
    kept_rows, order, table, hot_rows = route_rows(
        indices[0], indices[1], experts, capacity, row_count, ranks
    )
    own_experts = (expert_up, expert_down)
    far, back_ranges, order, table, kept_rows = tie(
        flip(far_rows(attended), "zl"), back_ranges, order, table, kept_rows
    )
    upstream = jnp.where(home, upstream, away_upstream).astype(jnp.float32)
    attended = near_rows(attended) + far.astype(jnp.float32)
    mixed_one = inputs + attended
    unit_two, inverse_two = normalize_plain(mixed_one)
    normed_two_rows = (unit_two * moe_gain).astype(jnp.bfloat16)
    centroid_rows = jnp.dot(
        hot_rows.astype(jnp.bfloat16), centroids, preferred_element_type=jnp.float32
    )
    normed_two_float = normed_two_rows.astype(jnp.float32)
    gate_prob = jax.nn.sigmoid(jnp.sum(normed_two_float * centroid_rows, axis=-1))
    gate_used = jnp.where(kept_rows, gate_prob, 0.0)
    grad_eo_rows = (gate_used[:, None] * upstream).astype(jnp.bfloat16)
    sorted_rows = sort_rows(order, normed_two_rows)
    beside, across = flip(sorted_rows, "c"), flip(sorted_rows, "zl")
    across, grad_sorted = tie(across, sort_rows(order, grad_eo_rows))
    grad_beside, grad_across = flip(grad_sorted, "c"), flip(grad_sorted, "zl")
    dispatched = [sorted_rows, beside, across, flip(across, "c")]
    returned, hidden, slope = moe_forward(table, dispatched, own_experts, new_experts)
    grad_across, *returned = tie(grad_across, *returned)
    returned_far, grad_corner = tie(far_rows(returned), flip(grad_across, "c"))
    grad_dispatched = [grad_sorted, grad_beside, grad_across, grad_corner]
    returned_far = flip(returned_far, "zl")
    returned_near = near_rows(returned)
    back_moe, grad_upward = moe_backward(table, grad_dispatched, slope, own_experts, new_experts)
    returned_far, back_moe[3] = tie(returned_far, back_moe[3])
    back_far, hidden = tie(far_rows(back_moe), hidden)
    back_far = flip(back_far, "zl")
    back_near = near_rows(back_moe)
    down_part, token = moe_weights(table, grad_dispatched, hidden, back_moe[3], experts)
    back_far, token = tie(back_far, token)
    expert_out = unsort_rows(order, returned_near + returned_far.astype(jnp.float32))
    mixed_two = (mixed_one + gate_used[:, None] * expert_out).astype(jnp.bfloat16)
    grad_gate = jnp.where(kept_rows, jnp.sum(upstream * expert_out, axis=-1), 0.0)
    grad_score = grad_gate * gate_prob * (1.0 - gate_prob)
    down_rest = lax.psum_scatter(down_part, high_bits, scatter_dimension=1, tiled=True)
    back_moe = back_near + back_far.astype(jnp.float32)
    grad_two = unsort_rows(order, back_moe) + grad_score[:, None] * centroid_rows
    centroid_part = jnp.einsum(
        "te,td->ed",
        hot_rows.astype(jnp.float32),
        grad_score[:, None] * normed_two_float,
        precision=highest,
    )
    moe_gain_part = jnp.sum(grad_two * unit_two, axis=0)
    grad_mixed = upstream + normalize_back(grad_two, unit_two, inverse_two, moe_gain)
    grad_mixed, grad_upward = tie(grad_mixed, grad_upward)
    up_part, _ = moe_weights(table, dispatched, grad_upward, token, experts)
    grad_att = gather_blocks(grad_mixed.astype(jnp.bfloat16))
    early = jnp.concatenate([moe_gain_part[None], centroid_part], axis=0)
    everyone = (*users, "zh", "zl")
    early = jnp.swapaxes(early.reshape(experts + 1, lax.axis_size(everyone), -1), 0, 1)
    early = jnp.sum(lax.all_to_all(early, everyone, 0, 0, tiled=True), axis=0)
    grad_att[2], early, up_part = tie(grad_att[2], early, up_part)
    grad_att[3] = flip(grad_att[2], "c")
    up_rest = lax.psum_scatter(up_part, high_bits, scatter_dimension=1, tiled=True)
    down_rest, mixed_two, grad_att[3] = tie(down_rest, mixed_two, grad_att[3])
    down_home = send_home(down_rest, 1)
    away_output = lax.ppermute(mixed_two, ("c", "zh"), [(1, 2), (2, 1)])
    *grad_one, weights_part = attention_backward(
        back_ranges, start, ranks, grad_att, normed_one, saved, qkv_used, proj_used
    )
    grad_one[3], away_output, *down_home = tie(grad_one[3], away_output, *down_home)
    one_far = far_rows(grad_one)
    one_near = near_rows(grad_one)

    def finish(far):
        grad = normalize_back(
            one_near + far.astype(jnp.float32), unit_one, inverse_one, attention_gain
        )
        return (grad_mixed + grad).astype(jnp.bfloat16)

    going = flip_some(one_far, False)
    weights_part = lax.psum_scatter(weights_part, high_bits, scatter_dimension=1, tiled=True)
    going, one_far, weights_part, *up_home = tie(
        going, one_far, weights_part, *send_home(up_rest, 1)
    )
    going, one_far, weights_part, away_output, *homes = tie(
        finish(going), one_far, weights_part, away_output, *down_home, *up_home
    )
    down_home, up_home = homes[:3], homes[3:]
    block_output = jnp.where(home, mixed_two, away_output)[None]
    going = lax.ppermute(going, ("c", "zh"), [(1, 2), (2, 1)])
    kept_far = flip_some(one_far, True)
    input_grad = jnp.where(home, finish(kept_far), going)[None]
    down_summed = jnp.swapaxes(sum_home(*down_home), 1, 2)
    up_summed = sum_home(*up_home)
    weights_part = sum_home(*send_home(weights_part, 1))
    qkv_summed, proj_summed = weights_part[:3], weights_part[3].T
    gain_two_sum, centroid_sum = early[0], early[1:]
    entries = gain_two_sum.shape[0]
    own_entries = lax.axis_index(everyone) * entries
    slice_rows = qkv_summed.shape[1]
    own_rows = lax.dynamic_slice_in_dim(
        qkv_weight, lax.axis_index(users) * slice_rows, slice_rows, 1
    )
    gain_one = jnp.sum(own_rows.astype(jnp.float32) * qkv_summed, axis=(0, 2))
    for bit in ("zh", "zl"):
        gain_one = halve(*send_half(gain_one, bit, 0))
    gain_one_sum = gain_one / lax.dynamic_slice_in_dim(attention_gain, own_entries, entries, 0)
    return (
        block_output,
        input_grad,
        gain_one_sum,
        gain_two_sum,
        centroid_sum,
        qkv_summed,
        proj_summed,
        up_summed,
        down_summed,
    )


def solution(mesh):
    shape = mesh.devices.shape
    high_bits = tuple(f"u{place}" for place in range((shape[0] // 2).bit_length() - 1))
    dp, tensor = (*high_bits, "c"), ("zh", "zl")
    mesh = Mesh(mesh.devices.reshape((2,) * len(dp + tensor)), dp + tensor)

    def program(*arguments):
        return body(high_bits, *arguments)

    return jax.shard_map(
        program,
        mesh=mesh,
        in_specs=(
            P(dp, tensor, None),
            P(),
            P(None, None, tensor),
            P(tensor, None),
            P(),
            P(),
            P(None, None, tensor),
            P(None, tensor, None),
            P(dp, tensor, None),
            P(dp, None, None),
            P(dp, None),
            P(dp, None),
        ),
        out_specs=(
            P(dp, tensor, None),
            P(dp, tensor, None),
            P(dp + tensor),
            P(dp + tensor),
            P(None, dp + tensor),
            P(None, dp, tensor),
            P(tensor, dp),
            P(None, dp, tensor),
            P(None, tensor, dp),
        ),
        check_vma=False,
    )
```

```python
import jax
import jax.numpy as jnp
from jax import lax
from jax.experimental import pallas as pl
from jax.experimental.pallas import tpu as pltpu
from jax.sharding import Mesh
from jax.sharding import PartitionSpec as P

HEAD_DIM = 64
FORWARD_BLOCKS = (512, 512)
BACKWARD_BLOCKS = (512, 256)
LOG2E = 1.4426950408889634
NEGATIVE = -1e30
TILE = 256
CHUNK = 256
TOKEN = (16, 128)
ALIGN = 16
CONTINUATIONS = 8
HBM = pl.BlockSpec(memory_space=pl.ANY)

epsilon = 1e-05
highest = lax.Precision.HIGHEST


def normalize_plain(values):
    centered = values - jnp.mean(values, axis=-1, keepdims=True)
    variance = jnp.mean(centered * centered, axis=-1, keepdims=True)
    inverse = lax.rsqrt(variance + epsilon)
    return (centered * inverse, inverse)


def normalize_back(upstream, unit_rows, inverse, gain_row):
    scaled = upstream * gain_row
    centered = scaled - jnp.mean(scaled, axis=-1, keepdims=True)
    return inverse * (centered - unit_rows * jnp.mean(scaled * unit_rows, axis=-1, keepdims=True))


def matmul(a, b, dims=((1,), (0,))):
    return lax.dot_general(a, b, (dims, ((), ())), preferred_element_type=jnp.float32)


def key_ranges(segment, blocks):
    block, fine = blocks
    token_count = segment.shape[0]
    numbers = jnp.arange(1, CONTINUATIONS + 1, dtype=jnp.int32)[:, None]
    earlier = jnp.sum((segment[None, :] < numbers).astype(jnp.int32), axis=1, keepdims=True)
    prompt = earlier[0, 0]
    start = jnp.sum(jnp.where(segment[None, :] == numbers, earlier, 0), axis=0)
    first = jnp.arange(token_count // block, dtype=jnp.int32) * block
    whole = jnp.minimum(prompt, first) // fine
    shared = (jnp.minimum(prompt, first + block) + fine - 1) // fine
    own = jnp.maximum(shared, start.reshape(-1, block)[:, 0] // fine)
    last = (first + block) // fine
    return (jnp.stack([whole, shared, own, last, jnp.full_like(whole, prompt)]), start[None, :])


def copies(pairs, semaphores):
    moved = [
        pltpu.make_async_copy(source, target, semaphores.at[place])
        for place, (source, target) in enumerate(pairs)
    ]
    for copy in moved:
        copy.start()
    for copy in moved:
        copy.wait()


def rank_rows(ref, rank, like):
    count = like.shape[0]
    return ref.at[pl.ds(pl.multiple_of(rank * count, count), count)]


def send_ranks(ref, targets, ranks, semaphores, edge, block, down):
    count = targets[0].shape[0]
    for rank in range(4):
        if down:
            first = rank * count
            due = (edge <= first) & (edge + block > first)
        else:
            last = (rank + 1) * count
            due = (edge >= last) & (edge - block < last)

        @pl.when(due)
        def _(rank=rank):
            for b, target in enumerate(targets):

                @pl.when(ranks[b] == rank)
                def _(b=b, target=target):
                    source = ref.at[rank * count : (rank + 1) * count]
                    pltpu.make_async_copy(source, target, semaphores.at[b]).start()


def take_ranks(ref, sources, ranks, semaphores, edge, block, first):
    count = sources[0].shape[0]

    @pl.when(first)
    def _():
        for b, source in enumerate(sources):
            target = rank_rows(ref, ranks[b], source)
            pltpu.make_async_copy(source, target, semaphores.at[b]).start()

    for b, source in enumerate(sources):
        begin = ranks[b] * count
        before = jnp.where(first, 0, edge)

        @pl.when((begin >= before) & (begin < edge + block))
        def _(b=b, source=source):
            target = rank_rows(ref, ranks[b], source)
            pltpu.make_async_copy(source, target, semaphores.at[b]).wait()


def await_ranks(ref, targets, ranks, semaphores):
    for b, target in enumerate(targets):
        pltpu.make_async_copy(rank_rows(ref, ranks[b], target), target, semaphores.at[b]).wait()


def forward_kernel(
    ranges, ranks, x0, x1, x2, x3, w_ref, start_ref,
    p0, p1, p2, p3, qt_ref, k_ref, kt_ref, v_ref, ctx_ref, lse_ref,
    x_ref, part_ref, vt_ref, score_ref, top_ref, sum_ref, arrived, left,
):
    step = pl.program_id(0)
    heads = qt_ref.shape[0]
    block = qt_ref.shape[2]
    fine = vt_ref.shape[3]
    step_keys = kt_ref.shape[3]
    rows = pl.ds(pl.multiple_of(step * block, block), block)

    take_ranks(x_ref, (x0, x1, x2, x3), ranks, arrived, step * block, block, step == 0)
    x = x_ref[rows, :]
    for kind in range(3):
        made = matmul(x, w_ref[kind]).astype(jnp.bfloat16)
        turned = made.T
        for head in range(heads):
            part = slice(head * HEAD_DIM, (head + 1) * HEAD_DIM)
            if kind == 0:
                qt_ref[head] = turned[part]
            if kind == 1:
                k_ref[head, rows, :] = made[:, part]
            if kind == 2:
                v_ref[head, rows, :] = made[:, part]
            for piece in range(block // step_keys if kind == 1 else 0):
                columns = slice(piece * step_keys, (piece + 1) * step_keys)
                kt_ref[piece, head] = turned[part, columns]
            for piece in range(block // fine if kind == 2 else 0):
                columns = slice(piece * fine, (piece + 1) * fine)
                at = step * (block // fine) + piece
                vt_ref[at, head, :HEAD_DIM] = turned[part, columns]
                vt_ref[at, head, HEAD_DIM:] = jnp.ones((16, fine), jnp.bfloat16)
    top_ref[...] = jnp.full_like(top_ref, NEGATIVE)
    sum_ref[...] = jnp.zeros_like(sum_ref)
    prompt = ranges[4, step]
    scale = LOG2E * HEAD_DIM ** (-0.5)

    def visit(key, masked):
        place = pl.ds(pl.multiple_of(key * fine, fine), fine)
        if masked:
            key_at = key * fine + lax.broadcasted_iota(jnp.int32, (fine, block), 0)
            query_at = step * block + lax.broadcasted_iota(jnp.int32, (fine, block), 1)
            seen = (key_at <= query_at) & ((key_at < prompt) | (key_at >= start_ref[...]))
        for head in range(heads):
            scores = matmul(k_ref[head, place, :], qt_ref[head])
            if masked:
                scores = jnp.where(seen, scores, NEGATIVE)
            score_ref[key, head] = scores
            top_ref[head] = jnp.maximum(
                top_ref[head], jnp.max(scores.reshape(fine // 8, 8, block), axis=0)
            )

    def plain(key, carry):
        visit(key, False)
        return carry

    def edge(key, carry):
        visit(key, True)
        return carry

    lax.fori_loop(0, ranges[0, step], plain, 0)
    lax.fori_loop(ranges[0, step], ranges[1, step], edge, 0)
    lax.fori_loop(ranges[2, step], ranges[3, step], edge, 0)
    for head in range(heads):
        top_ref[head, :1] = jnp.max(top_ref[head], axis=0, keepdims=True) * scale

    def add(key, carry):
        for head in range(heads):
            weights = jnp.exp2(score_ref[key, head] * scale - top_ref[head, :1])
            sum_ref[head] += matmul(vt_ref[key, head], weights.astype(jnp.bfloat16))
        return carry

    lax.fori_loop(0, ranges[1, step], add, 0)
    lax.fori_loop(ranges[2, step], ranges[3, step], add, 0)
    for head in range(heads):
        total = sum_ref[head, HEAD_DIM : HEAD_DIM + 1]
        context = sum_ref[head, :HEAD_DIM] / total
        ctx_ref[head * HEAD_DIM : (head + 1) * HEAD_DIM] = context.astype(jnp.bfloat16)
        lse_ref[head] = top_ref[head, :1] + jnp.log(total) * LOG2E
    part_ref[rows, :] = matmul(ctx_ref[...].T, w_ref[3], ((1,), (1,))).astype(jnp.bfloat16)
    send_ranks(part_ref, (p0, p1, p2, p3), ranks, left, (step + 1) * block, block, False)

    @pl.when(step == pl.num_programs(0) - 1)
    def _():
        await_ranks(part_ref, (p0, p1, p2, p3), ranks, left)


def attention_forward(ranges, start, ranks, x, w):
    tokens, width = start.shape[1], x[0].shape[1]
    local = w.shape[2]
    heads = local // HEAD_DIM
    block, fine = FORWARD_BLOCKS
    step_keys = BACKWARD_BLOCKS[1]
    count = tokens // block
    low = jnp.bfloat16
    head_rows = pl.BlockSpec((heads, tokens, HEAD_DIM), lambda i, r, n: (0, 0, 0))
    flops = 2 * tokens * width * local * 4 + tokens * tokens * local * 2
    return pl.pallas_call(
        forward_kernel,
        grid_spec=pltpu.PrefetchScalarGridSpec(
            num_scalar_prefetch=2,
            grid=(count,),
            in_specs=[
                *[HBM] * 4,
                pl.BlockSpec((4, width, local), lambda i, r, n: (0, 0, 0)),
                pl.BlockSpec((1, block), lambda i, r, n: (0, i)),
            ],
            out_specs=[
                *[HBM] * 4,
                pl.BlockSpec((heads, HEAD_DIM, block), lambda i, r, n: (0, 0, i)),
                head_rows,
                pl.BlockSpec(
                    (block // step_keys, heads, HEAD_DIM, step_keys), lambda i, r, n: (i, 0, 0, 0)
                ),
                head_rows,
                pl.BlockSpec((local, block), lambda i, r, n: (0, i)),
                pl.BlockSpec((heads, 1, block), lambda i, r, n: (0, 0, i)),
            ],
            scratch_shapes=[
                pltpu.VMEM((tokens, width), low),
                pltpu.VMEM((tokens, width), low),
                pltpu.VMEM((tokens // fine, heads, HEAD_DIM + 16, fine), low),
                pltpu.VMEM((tokens // fine, heads, fine, block), jnp.float32),
                pltpu.VMEM((heads, 8, block), jnp.float32),
                pltpu.VMEM((heads, HEAD_DIM + 16, block), jnp.float32),
                pltpu.SemaphoreType.DMA((4,)),
                pltpu.SemaphoreType.DMA((4,)),
            ],
        ),
        out_shape=[
            *[jax.ShapeDtypeStruct(x[0].shape, low)] * 4,
            jax.ShapeDtypeStruct((heads, HEAD_DIM, tokens), low),
            jax.ShapeDtypeStruct((heads, tokens, HEAD_DIM), low),
            jax.ShapeDtypeStruct((tokens // step_keys, heads, HEAD_DIM, step_keys), low),
            jax.ShapeDtypeStruct((heads, tokens, HEAD_DIM), low),
            jax.ShapeDtypeStruct((local, tokens), low),
            jax.ShapeDtypeStruct((heads, 1, tokens), jnp.float32),
        ],
        compiler_params=pltpu.CompilerParams(vmem_limit_bytes=56 << 20),
        cost_estimate=pl.CostEstimate(
            flops=4 * flops, transcendentals=tokens * tokens * heads // 2, bytes_accessed=40 << 20
        ),
        name="attention_forward",
    )(ranges, ranks, *x, w, start)


def backward_kernel(
    ranges, ranks, g0, g1, g2, g3, x0, x1, x2, x3,
    ctx_ref, lse_ref, qt_ref, start_ref, k_ref, kt_ref, v_ref, w_ref,
    p0, p1, p2, p3, weights_ref,
    g_ref, x_ref, part_ref, wgrad_ref, pgrad_ref,
    dk_ref, dv_ref, dq_ref, outer_ref, inner_ref, grad_ref, prob_ref, dscore_ref, arrived, left,
):
    number = pl.program_id(0)
    step = pl.num_programs(0) - 1 - number
    heads = qt_ref.shape[0]
    block = qt_ref.shape[2]
    fine = kt_ref.shape[3]
    local = heads * HEAD_DIM
    rows = pl.ds(pl.multiple_of(step * block, block), block)

    @pl.when(number == 0)
    def _():
        for place, (ref, sources) in enumerate(((g_ref, (g0, g1, g2, g3)), (x_ref, (x0, x1, x2, x3)))):
            for b, source in enumerate(sources):
                target = rank_rows(ref, ranks[b], source)
                pltpu.make_async_copy(source, target, arrived.at[place, b]).start()
        dk_ref[...] = jnp.zeros_like(dk_ref)
        dv_ref[...] = jnp.zeros_like(dv_ref)
        wgrad_ref[...] = jnp.zeros_like(wgrad_ref)
        pgrad_ref[...] = jnp.zeros_like(pgrad_ref)
        await_copies(g_ref, (g0, g1, g2, g3), ranks, arrived.at[0])

    upstream = g_ref[rows, :]
    outer = matmul(upstream, w_ref[3]).astype(jnp.bfloat16).T
    for head in range(heads):
        part = slice(head * HEAD_DIM, (head + 1) * HEAD_DIM)
        outer_ref[head] = outer[part]
        inner_ref[head] = jnp.sum(
            outer[part].astype(jnp.float32) * ctx_ref[part].astype(jnp.float32),
            axis=0,
            keepdims=True,
        )
    pgrad_ref[...] += matmul(ctx_ref[...], upstream)
    dq_ref[...] = jnp.zeros_like(dq_ref)
    prompt = ranges[4, step]
    scale = LOG2E * HEAD_DIM ** (-0.5)

    def add(key, head):
        prob, dscore = prob_ref[head], dscore_ref[head]
        dv_ref[key, head] += matmul(outer_ref[head], prob, ((1,), (1,)))
        dk_ref[key, head] += matmul(qt_ref[head], dscore, ((1,), (1,)))
        dq_ref[head] += matmul(kt_ref[key, head], dscore)

    def visit(number, before, masked):
        key = jnp.where(number < ranges[1, step], number, number - ranges[1, step] + ranges[2, step])
        place = pl.ds(pl.multiple_of(key * fine, fine), fine)
        if masked:
            key_at = key * fine + lax.broadcasted_iota(jnp.int32, (fine, block), 0)
            query_at = step * block + lax.broadcasted_iota(jnp.int32, (fine, block), 1)
            seen = (key_at <= query_at) & ((key_at < prompt) | (key_at >= start_ref[...]))
        for head in range(heads):
            scores = matmul(k_ref[head, place, :], qt_ref[head]) * scale
            dprob = matmul(v_ref[head, place, :], outer_ref[head])
            if before is not None:
                add(before, head)
            if masked:
                scores = jnp.where(seen, scores, NEGATIVE)
            prob = jnp.exp2(scores - lse_ref[head])
            prob_ref[head] = prob.astype(jnp.bfloat16)
            dscore_ref[head] = (prob * (dprob - inner_ref[head])).astype(jnp.bfloat16)
        return key

    visits = ranges[1, step] + ranges[3, step] - ranges[2, step]
    plain = jnp.maximum(ranges[0, step], 1)
    key = visit(0, None, True)
    key = lax.fori_loop(1, plain, lambda number, before: visit(number, before, False), key)
    key = lax.fori_loop(plain, visits, lambda number, before: visit(number, before, True), key)
    for head in range(heads):
        add(key, head)
    small = HEAD_DIM ** (-0.5)

    @pl.when(number == 0)
    def _():
        await_copies(x_ref, (x0, x1, x2, x3), ranks, arrived.at[1])

    for head in range(heads):
        part = slice(head * HEAD_DIM, (head + 1) * HEAD_DIM)
        grad_ref[0, part] = (dq_ref[head] * small).astype(jnp.bfloat16)
        for piece in range(block // fine):
            at = step * (block // fine) + piece
            columns = slice(piece * fine, (piece + 1) * fine)
            grad_ref[1, part, columns] = (dk_ref[at, head] * small).astype(jnp.bfloat16)
            grad_ref[2, part, columns] = dv_ref[at, head].astype(jnp.bfloat16)
    x = x_ref[rows, :]
    total = None
    for kind in range(3):
        wgrad_ref[kind] += matmul(grad_ref[kind], x)
        term = matmul(grad_ref[kind].T, w_ref[kind], ((1,), (1,)))
        total = term if total is None else total + term
    part_ref[rows, :] = total.astype(jnp.bfloat16)
    send_ranks(part_ref, (p0, p1, p2, p3), ranks, left, step * block, block, True)

    @pl.when(step == 0)
    def _():
        for kind in range(3):
            weights_ref[kind] = wgrad_ref[kind].T.astype(jnp.bfloat16)
        weights_ref[3] = pgrad_ref[...].T.astype(jnp.bfloat16)
        await_ranks(part_ref, (p0, p1, p2, p3), ranks, left)


def await_copies(ref, sources, ranks, semaphores):
    for b, source in enumerate(sources):
        target = rank_rows(ref, ranks[b], source)
        pltpu.make_async_copy(source, target, semaphores.at[b]).wait()


def attention_backward(ranges, start, ranks, upstream, x, saved, w):
    qt, k, kt, v, ctx, lse = saved
    tokens, width = start.shape[1], x[0].shape[1]
    local = w.shape[2]
    heads = local // HEAD_DIM
    block, fine = BACKWARD_BLOCKS
    count = tokens // block
    low = jnp.bfloat16

    def at(i):
        return count - 1 - i

    head_rows = pl.BlockSpec((heads, tokens, HEAD_DIM), lambda i, r, n: (0, 0, 0))
    flops = 2 * tokens * width * local * 8 + tokens * tokens * local * 5
    return pl.pallas_call(
        backward_kernel,
        grid_spec=pltpu.PrefetchScalarGridSpec(
            num_scalar_prefetch=2,
            grid=(count,),
            in_specs=[
                *[HBM] * 8,
                pl.BlockSpec((local, block), lambda i, r, n: (0, at(i))),
                pl.BlockSpec((heads, 1, block), lambda i, r, n: (0, 0, at(i))),
                pl.BlockSpec((heads, HEAD_DIM, block), lambda i, r, n: (0, 0, at(i))),
                pl.BlockSpec((1, block), lambda i, r, n: (0, at(i))),
                head_rows,
                pl.BlockSpec((tokens // fine, heads, HEAD_DIM, fine), lambda i, r, n: (0, 0, 0, 0)),
                head_rows,
                pl.BlockSpec((4, width, local), lambda i, r, n: (0, 0, 0)),
            ],
            out_specs=[
                *[HBM] * 4,
                pl.BlockSpec((4, width, local), lambda i, r, n: (0, 0, 0)),
            ],
            scratch_shapes=[
                pltpu.VMEM((tokens, width), low),
                pltpu.VMEM((tokens, width), low),
                pltpu.VMEM((tokens, width), low),
                pltpu.VMEM((3, local, width), jnp.float32),
                pltpu.VMEM((local, width), jnp.float32),
                pltpu.VMEM((tokens // fine, heads, HEAD_DIM, fine), jnp.float32),
                pltpu.VMEM((tokens // fine, heads, HEAD_DIM, fine), jnp.float32),
                pltpu.VMEM((heads, HEAD_DIM, block), jnp.float32),
                pltpu.VMEM((heads, HEAD_DIM, block), low),
                pltpu.VMEM((heads, 1, block), jnp.float32),
                pltpu.VMEM((3, local, block), low),
                pltpu.VMEM((heads, fine, block), low),
                pltpu.VMEM((heads, fine, block), low),
                pltpu.SemaphoreType.DMA((2, 4)),
                pltpu.SemaphoreType.DMA((4,)),
            ],
        ),
        out_shape=[
            *[jax.ShapeDtypeStruct(x[0].shape, low)] * 4,
            jax.ShapeDtypeStruct((4, width, local), low),
        ],
        compiler_params=pltpu.CompilerParams(vmem_limit_bytes=56 << 20),
        cost_estimate=pl.CostEstimate(
            flops=4 * flops, transcendentals=tokens * tokens * heads // 2, bytes_accessed=40 << 20
        ),
        name="attention_backward",
    )(ranges, ranks, *upstream, *x, ctx, lse, qt, start, k, kt, v, w)


def route_rows(route, priority, experts, capacity, row_count, ranks):
    own_start = ranks[0] * row_count
    own_route = lax.dynamic_slice_in_dim(route, own_start, row_count, 0)
    own_priority = lax.dynamic_slice_in_dim(priority, own_start, row_count, 0)
    ahead = (route[None, :] == own_route[:, None]) & (priority[None, :] < own_priority[:, None])
    kept = jnp.sum(ahead.astype(jnp.int32), axis=1) < capacity
    kinds = jnp.arange(experts, dtype=jnp.int32)
    block_hot = (route.reshape(-1, row_count)[:, :, None] == kinds).astype(jnp.int32)
    lengths = jnp.sum(block_hot, axis=1)
    starts = jnp.cumsum(lengths, axis=1) - lengths
    own_hot = (own_route[:, None] == kinds).astype(jnp.int32)
    index = jnp.arange(row_count, dtype=jnp.int32)
    before = (own_route[None, :] == own_route[:, None]) & (index[None, :] < index[:, None])
    own_starts = lax.dynamic_slice_in_dim(starts, ranks[0], 1, 0)
    place = jnp.sum(before.astype(jnp.int32), axis=1) + jnp.sum(own_hot * own_starts, axis=1)
    order = (index[:, None] == place[None, :]).astype(jnp.bfloat16)
    picked = [
        lax.dynamic_slice_in_dim(array, ranks[b], 1, 0)[0]
        for array in (starts, lengths)
        for b in range(4)
    ]
    home = at_home().astype(jnp.int32)[None]
    return (kept, order, jnp.concatenate([*picked, home]), own_hot)


def sort_rows(order, rows):
    return jnp.dot(order, rows, preferred_element_type=jnp.float32).astype(jnp.bfloat16)


def unsort_rows(order, rows):
    return matmul(order, rows.astype(jnp.bfloat16), ((0,), (0,)))


def each_tile(table, block, expert, experts, visit):
    start = table[block * experts + expert]
    end = start + table[(4 + block) * experts + expert]
    first = start // ALIGN * ALIGN

    def tile(number, carry):
        at = first + number * TILE
        visit(pl.ds(pl.multiple_of(at, ALIGN), TILE), start - at, end - at)
        return carry

    lax.fori_loop(0, jnp.where(end > start, (end - first + TILE - 1) // TILE, 0), tile, 0)


def put_rows(ref, block, place, rows, head):
    top = pl.ds(place.start, ALIGN)
    old = ref[block, top, :]
    index = lax.broadcasted_iota(jnp.int32, old.shape, 0)
    ref[block, place, :] = rows
    ref[block, top, :] = jnp.where(index < head, old, rows[:ALIGN])


def fetch_weights(choice, kept, given, targets, semaphores):
    for place, target in enumerate(targets):
        for expert in range(target.shape[0]):
            ready = semaphores.at[place, expert]

            @pl.when(choice == 1)
            def _(place=place, target=target, expert=expert, ready=ready):
                pltpu.make_async_copy(kept[place].at[expert], target.at[expert], ready).start()

            @pl.when(choice == 0)
            def _(place=place, target=target, expert=expert, ready=ready):
                pltpu.make_async_copy(given[place].at[expert], target.at[expert], ready).start()


def await_weights(kept, targets, expert, semaphores):
    for place, target in enumerate(targets):
        pltpu.make_async_copy(
            kept[place].at[expert], target.at[expert], semaphores.at[place, expert]
        ).wait()


def within(rows, head, end):
    index = lax.broadcasted_iota(jnp.int32, rows.shape, 0)
    return jnp.where((index >= head) & (index < end), rows, 0)


def block_copies(block, pairs, semaphores):
    for place, (source, targets) in enumerate(pairs):
        for b in range(4):

            @pl.when(block == b)
            def _(place=place, source=source, targets=targets, b=b):
                target = targets[b] if isinstance(targets, tuple) else targets.at[b]
                rows = source.at[b, : target.shape[0]]
                pltpu.make_async_copy(rows, target, semaphores.at[place, b]).start()


def await_blocks(pairs, semaphores):
    for place, (source, targets) in enumerate(pairs):
        for b in range(4):
            target = targets[b] if isinstance(targets, tuple) else targets.at[b]
            rows = source.at[b, : target.shape[0]]
            pltpu.make_async_copy(rows, target, semaphores.at[place, b]).wait()


def moe_steps(table, experts, inputs, weights, outputs, tails, visit, semaphores):
    block = pl.program_id(0)
    kept, given, held = weights
    arrived, left, ready = semaphores
    count = inputs[0][1][0].shape[0]

    @pl.when(block == 0)
    def _():
        for place, (target, sources) in enumerate(inputs):
            for b in range(4):
                source = sources[b] if isinstance(sources, tuple) else sources.at[b]
                rows = target.at[b, : source.shape[0]]
                pltpu.make_async_copy(source, rows, arrived.at[place, b]).start()
        fetch_weights(table[8 * experts], kept, given, held, ready)
        for ref in tails:
            ref[:, count:, :] = jnp.zeros((4, TILE, ref.shape[2]), ref.dtype)

    for place, (target, sources) in enumerate(inputs):
        source = sources[0] if isinstance(sources, tuple) else sources.at[0]
        rows = target.at[block, : source.shape[0]]
        pltpu.make_async_copy(source, rows, arrived.at[place, block]).wait()

    def expert_rows(expert, carry):
        @pl.when(block == 0)
        def _():
            await_weights(kept, held, expert, ready)

        each_tile(
            table, block, expert, experts,
            lambda place, head, end: visit(block, expert, place, head, end),
        )
        return carry

    lax.fori_loop(0, experts, expert_rows, 0)
    block_copies(block, outputs, left)

    @pl.when(block == 3)
    def _():
        await_blocks(outputs, left)


def moe_forward_kernel(
    table, x0, x1, x2, x3, own_up, own_down, new_up, new_down,
    y0, y1, y2, y3, hidden_out, slope_out,
    x_ref, y_ref, hidden_ref, slope_ref, up_ref, down_ref, *semaphores,
):
    width = up_ref.shape[2]

    def visit(block, expert, place, head, end):
        x = x_ref[block, place, :]
        total = None
        for part in range(0, width, CHUNK):
            chunk = slice(part, part + CHUNK)
            u = matmul(x, up_ref[expert, :, chunk])
            cube = 0.7978845608028654 * u * (1.0 + 0.044715 * u * u)
            bend = 1.0 + jnp.tanh(cube)
            half = 0.5 * bend
            hidden = (u * half).astype(jnp.bfloat16)
            slope = half + u * (half * (2.0 - bend)) * (
                0.7978845608028654 * (1.0 + 3.0 * 0.044715 * u * u)
            )
            put_rows(hidden_ref.at[:, :, chunk], block, place, hidden, head)
            put_rows(slope_ref.at[:, :, chunk], block, place, slope.astype(jnp.bfloat16), head)
            term = matmul(hidden, down_ref[expert, chunk, :])
            total = term if total is None else total + term
        put_rows(y_ref, block, place, total.astype(jnp.bfloat16), head)

    moe_steps(
        table, up_ref.shape[0], [(x_ref, (x0, x1, x2, x3))],
        ((own_up, own_down), (new_up, new_down), (up_ref, down_ref)),
        [(y_ref, (y0, y1, y2, y3)), (hidden_ref, hidden_out), (slope_ref, slope_out)],
        (x_ref, hidden_ref, slope_ref), visit, semaphores,
    )


def moe_backward_kernel(
    table, d0, d1, d2, d3, slope_in, own_up, own_down, new_up, new_down,
    y0, y1, y2, y3, grad_out,
    d_ref, slope_ref, y_ref, grad_ref, up_ref, down_ref, *semaphores,
):
    width = up_ref.shape[2]

    def visit(block, expert, place, head, end):
        upstream = within(d_ref[block, place, :], head, end)
        total = None
        for part in range(0, width, CHUNK):
            chunk = slice(part, part + CHUNK)
            slope = slope_ref[block, place, chunk].astype(jnp.float32)
            grad = matmul(upstream, down_ref[expert, chunk, :], ((1,), (1,))) * slope
            grad = grad.astype(jnp.bfloat16)
            put_rows(grad_ref.at[:, :, chunk], block, place, grad, head)
            term = matmul(grad, up_ref[expert, :, chunk], ((1,), (1,)))
            total = term if total is None else total + term
        put_rows(y_ref, block, place, total.astype(jnp.bfloat16), head)

    moe_steps(
        table, up_ref.shape[0], [(d_ref, (d0, d1, d2, d3)), (slope_ref, slope_in)],
        ((own_up, own_down), (new_up, new_down), (up_ref, down_ref)),
        [(y_ref, (y0, y1, y2, y3)), (grad_ref, grad_out)],
        (d_ref, grad_ref), visit, semaphores,
    )


def moe_weights_kernel(
    table, a0, a1, a2, a3, b_in, token_in, out_ref, token_ref, a_ref, b_ref, sum_ref, semaphores
):
    expert = pl.program_id(0)
    experts = pl.num_programs(0)
    count = a0.shape[0]

    @pl.when(expert == 0)
    def _():
        token_ref[...] = jnp.zeros_like(token_ref)
        a_ref[:, count:, :] = jnp.zeros((4, TILE, a_ref.shape[2]), jnp.bfloat16)
        copies(
            [(a, a_ref.at[b, :count]) for b, a in enumerate((a0, a1, a2, a3))] + [(b_in, b_ref)],
            semaphores,
        )

    sum_ref[...] = jnp.zeros_like(sum_ref)

    def of_block(block, carry):
        def visit(place, head, end):
            rows = within(a_ref[block, place, :], head, end)
            sum_ref[...] += matmul(rows, b_ref[block, place, :], ((0,), (0,)))

        each_tile(table, block, expert, experts, visit)
        return carry

    lax.fori_loop(0, 4, of_block, 0)
    out_ref[0] = sum_ref[...].astype(jnp.bfloat16)


def moe_call(kernel, name, table, arrays, grid, specs, outs, scratch, semaphores, cost):
    return pl.pallas_call(
        kernel,
        grid_spec=pltpu.PrefetchScalarGridSpec(
            num_scalar_prefetch=1,
            grid=(grid,),
            in_specs=[HBM] * len(arrays),
            out_specs=specs,
            scratch_shapes=[
                *[pltpu.VMEM(*shape) for shape in scratch],
                *[pltpu.SemaphoreType.DMA(shape) for shape in semaphores],
            ],
        ),
        out_shape=[jax.ShapeDtypeStruct(shape, jnp.bfloat16) for shape in outs],
        compiler_params=pltpu.CompilerParams(vmem_limit_bytes=58 << 20),
        cost_estimate=pl.CostEstimate(flops=cost, transcendentals=0, bytes_accessed=40 << 20),
        name=name,
    )(table, *arrays)


def moe_forward(table, x, own, new):
    count, width = x[0].shape
    experts, _, hidden = own[0].shape
    low = jnp.bfloat16
    wide, tall = ((4, count + TILE, width), low), ((4, count + TILE, hidden), low)
    *y, hid, slope = moe_call(
        moe_forward_kernel, "moe_forward", table, [*x, *own, *new], 4, [HBM] * 6,
        [(count, width)] * 4 + [tall[0], tall[0]],
        [wide, wide, tall, tall, (own[0].shape, low), (own[1].shape, low)],
        [(1, 4), (3, 4), (2, experts)], 20 * count * width * hidden,
    )
    return (y, hid, slope)


def moe_backward(table, d, slope, own, new):
    count, width = d[0].shape
    experts, _, hidden = own[0].shape
    low = jnp.bfloat16
    wide, tall = ((4, count + TILE, width), low), ((4, count + TILE, hidden), low)
    *y, grad = moe_call(
        moe_backward_kernel, "moe_backward", table, [*d, slope, *own, *new], 4, [HBM] * 5,
        [(count, width)] * 4 + [tall[0]],
        [wide, tall, wide, tall, (own[0].shape, low), (own[1].shape, low)],
        [(2, 4), (2, 4), (2, experts)], 20 * count * width * hidden,
    )
    return (y, grad)


def moe_weights(table, blocks, tall, token, experts):
    count, width = blocks[0].shape
    hidden = tall.shape[2]
    return moe_call(
        moe_weights_kernel, "moe_weights", table, [*blocks, tall, token], experts,
        [
            pl.BlockSpec((1, width, hidden), lambda e, t: (e, 0, 0)),
            pl.BlockSpec(TOKEN, lambda e, t: (0, 0)),
        ],
        [(experts, width, hidden), TOKEN],
        [((4, count + TILE, width), jnp.bfloat16), (tall.shape, jnp.bfloat16),
         ((width, hidden), jnp.float32)],
        [(5,)], 10 * count * width * hidden,
    )


def at_home():
    return lax.axis_index("c") == lax.axis_index("zh")


def swap_roles(value):
    moved = lax.ppermute(value, ("c", "zh"), [(1, 2), (2, 1)])
    return jnp.where(at_home(), value, moved)


def flip(value, axis):
    return lax.ppermute(value, axis, [(0, 1), (1, 0)])


def flip_some(value, home):
    moves = [(0, 1), (1, 0), (6, 7), (7, 6)] if home else [(2, 3), (3, 2), (4, 5), (5, 4)]
    return lax.ppermute(value, ("c", "zh", "zl"), moves)


def tie(*values):
    return lax.optimization_barrier(values)


def gather_blocks(rows):
    across = flip(rows, "zl")
    return [rows, flip(rows, "c"), across, flip(across, "c")]


def far_rows(blocks):
    return (
        flip(blocks[3], "c").astype(jnp.float32) + blocks[2].astype(jnp.float32)
    ).astype(blocks[2].dtype)


def near_rows(blocks):
    return blocks[0].astype(jnp.float32) + flip(blocks[1], "c").astype(jnp.float32)


def scatter_blocks(blocks):
    return near_rows(blocks) + flip(far_rows(blocks), "zl").astype(jnp.float32)


def send_half(value, axis, dimension):
    count = value.shape[dimension] // 2
    side = lax.axis_index(axis)
    kept = lax.dynamic_slice_in_dim(value, side * count, count, dimension)
    sent = lax.dynamic_slice_in_dim(value, (1 - side) * count, count, dimension)
    return [kept, flip(sent, axis)]


def halve(kept, came):
    return (kept.astype(jnp.float32) + came.astype(jnp.float32)).astype(kept.dtype)


def send_home(value, dimension):
    count = value.shape[dimension] // 2
    high = lax.axis_index("zh")
    straight = lax.dynamic_slice_in_dim(value, high * count, count, dimension)
    turned = lax.dynamic_slice_in_dim(value, (1 - high) * count, count, dimension)
    turned = lax.ppermute(turned, ("c", "zh"), [(0, 2), (1, 0), (2, 3), (3, 1)])
    return [straight, lax.ppermute(straight, ("c", "zh"), [(1, 2), (2, 1)]), turned]


def sum_home(straight, moved, turned):
    straight = jnp.where(at_home(), straight, moved)
    return straight.astype(jnp.float32) + turned.astype(jnp.float32)


def piece_of(weight, users):
    flat = weight.reshape(-1, weight.shape[-1])
    part = flat.shape[0] // lax.axis_size(users)
    return lax.dynamic_slice_in_dim(flat, lax.axis_index(users) * part, part, 0)


def share(piece, users, shape):
    return lax.all_gather(piece, users, axis=0, tiled=True).reshape(shape)


def share_small(piece, users, shape):
    for bit in reversed(users):
        given = flip(piece, bit)
        low = lax.axis_index(bit) == 0
        piece = jnp.concatenate([jnp.where(low, piece, given), jnp.where(low, given, piece)], axis=0)
    return piece.reshape(shape)


def body(
    high_bits,
    block_input,
    attention_gain,
    qkv_weight,
    proj_weight,
    moe_gain,
    centroids,
    expert_up,
    expert_down,
    out_grad,
    routes,
    priority,
    segments,
):
    row_count = block_input.shape[1]
    model_width = block_input.shape[2]
    experts = expert_up.shape[0]
    token_count = segments.shape[1]
    capacity = 9 * token_count // (8 * experts)
    users = (*high_bits, "c")
    core, near = lax.axis_index("c"), lax.axis_index("zl")
    ranks = jnp.stack(
        [2 * core + near, 2 * (1 - core) + near, 2 * core + 1 - near, 3 - 2 * core - near]
    )
    home = at_home()
    staying = block_input[0]
    coming = lax.ppermute(staying, ("c", "zh"), [(1, 2), (2, 1)])
    small = jnp.concatenate([qkv_weight, proj_weight.T[None]], axis=0)
    small_piece = flip(piece_of(small, users), "zh")

    def normed(rows):
        return (normalize_plain(rows.astype(jnp.float32))[0] * attention_gain).astype(jnp.bfloat16)

    normed_staying = normed(staying)
    home_across = flip_some(normed_staying, True)
    indices = jnp.stack([routes[0, :, 0], priority[0], segments[0]])
    indices = jnp.where(home, indices, flip(indices, "c"))
    segment = indices[2]
    ranges, start = key_ranges(segment, FORWARD_BLOCKS)
    coming, small_piece, home_across, ranges, start = tie(
        coming, small_piece, home_across, ranges, start
    )
    small_other = share(small_piece, users, small.shape)
    normed_coming = normed(coming)
    away_across = flip_some(normed_coming, False)
    across = jnp.where(home, home_across, away_across)
    across, up_piece, down_piece = tie(
        across, piece_of(expert_up, users), piece_of(expert_down, users)
    )
    up_piece, down_piece = flip(up_piece, "zh"), flip(down_piece, "zh")
    normed_one = jnp.where(home, normed_staying, normed_coming)
    normed_one = [normed_one, flip(normed_one, "c"), across, flip(across, "c")]
    inputs = jnp.where(home, staying, coming).astype(jnp.float32)
    unit_one, inverse_one = normalize_plain(inputs)
    small = jnp.where(home, small, small_other)
    *attended, qt, k, kt, v, ctx, lse = attention_forward(
        ranges, start, ranks, normed_one, small
    )
    saved = (qt, k, kt, v, ctx, lse)
    attended[3], up_piece, down_piece, indices = tie(
        attended[3], up_piece, down_piece, indices
    )
    new_experts = [share(piece, users, expert_up.shape) for piece in (up_piece, down_piece)]
    back_ranges = key_ranges(indices[2], BACKWARD_BLOCKS)[0]
    kept_rows, order, table, hot_rows = route_rows(
        indices[0], indices[1], experts, capacity, row_count, ranks
    )
    own_experts = (expert_up, expert_down)
    far, back_ranges, order, table, kept_rows, upstream = tie(
        flip(far_rows(attended), "zl"), back_ranges, order, table, kept_rows, out_grad[0]
    )
    away_upstream = lax.ppermute(upstream, ("c", "zh"), [(1, 2), (2, 1)])
    upstream = jnp.where(home, upstream, away_upstream).astype(jnp.float32)
    attended = near_rows(attended) + far.astype(jnp.float32)
    mixed_one = inputs + attended
    unit_two, inverse_two = normalize_plain(mixed_one)
    normed_two_rows = (unit_two * moe_gain).astype(jnp.bfloat16)
    centroid_rows = jnp.dot(
        hot_rows.astype(jnp.bfloat16), centroids, preferred_element_type=jnp.float32
    )
    normed_two_float = normed_two_rows.astype(jnp.float32)
    gate_prob = jax.nn.sigmoid(jnp.sum(normed_two_float * centroid_rows, axis=-1))
    gate_used = jnp.where(kept_rows, gate_prob, 0.0)
    grad_eo_rows = (gate_used[:, None] * upstream).astype(jnp.bfloat16)
    sorted_rows = sort_rows(order, normed_two_rows)
    beside, across = flip(sorted_rows, "c"), flip(sorted_rows, "zl")
    across, grad_sorted = tie(across, sort_rows(order, grad_eo_rows))
    grad_beside, grad_across = flip(grad_sorted, "c"), flip(grad_sorted, "zl")
    dispatched = [sorted_rows, beside, across, flip(across, "c")]
    returned, hidden, slope = moe_forward(table, dispatched, own_experts, new_experts)
    grad_across, *returned = tie(grad_across, *returned)
    returned_far, grad_corner = tie(far_rows(returned), flip(grad_across, "c"))
    grad_dispatched = [grad_sorted, grad_beside, grad_across, grad_corner]
    returned_far = flip(returned_far, "zl")
    returned_near = near_rows(returned)
    back_moe, grad_upward = moe_backward(table, grad_dispatched, slope, own_experts, new_experts)
    returned_far, back_moe[3] = tie(returned_far, back_moe[3])
    back_far, hidden = tie(far_rows(back_moe), hidden)
    back_far = flip(back_far, "zl")
    back_near = near_rows(back_moe)
    down_part, token = moe_weights(table, grad_dispatched, hidden, back_moe[3], experts)
    back_far, token = tie(back_far, token)
    expert_out = unsort_rows(order, returned_near + returned_far.astype(jnp.float32))
    mixed_two = (mixed_one + gate_used[:, None] * expert_out).astype(jnp.bfloat16)
    grad_gate = jnp.where(kept_rows, jnp.sum(upstream * expert_out, axis=-1), 0.0)
    grad_score = grad_gate * gate_prob * (1.0 - gate_prob)
    down_rest = lax.psum_scatter(down_part, high_bits, scatter_dimension=1, tiled=True)
    back_moe = back_near + back_far.astype(jnp.float32)
    grad_two = unsort_rows(order, back_moe) + grad_score[:, None] * centroid_rows
    centroid_part = jnp.einsum(
        "te,td->ed",
        hot_rows.astype(jnp.float32),
        grad_score[:, None] * normed_two_float,
        precision=highest,
    )
    moe_gain_part = jnp.sum(grad_two * unit_two, axis=0)
    grad_mixed = upstream + normalize_back(grad_two, unit_two, inverse_two, moe_gain)
    grad_mixed, grad_upward = tie(grad_mixed, grad_upward)
    up_part, _ = moe_weights(table, dispatched, grad_upward, token, experts)
    grad_att = gather_blocks(grad_mixed.astype(jnp.bfloat16))
    early = jnp.concatenate([moe_gain_part[None], centroid_part], axis=0)
    everyone = (*users, "zh", "zl")
    early = jnp.swapaxes(early.reshape(experts + 1, lax.axis_size(everyone), -1), 0, 1)
    early = jnp.sum(lax.all_to_all(early, everyone, 0, 0, tiled=True), axis=0)
    grad_att[2], early, up_part = tie(grad_att[2], early, up_part)
    grad_att[3] = flip(grad_att[2], "c")
    up_rest = lax.psum_scatter(up_part, high_bits, scatter_dimension=1, tiled=True)
    down_rest, mixed_two, grad_att[3] = tie(down_rest, mixed_two, grad_att[3])
    down_home = send_home(down_rest, 1)
    away_output = lax.ppermute(mixed_two, ("c", "zh"), [(1, 2), (2, 1)])
    *grad_one, weights_part = attention_backward(
        back_ranges, start, ranks, grad_att, normed_one, saved, small
    )
    grad_one[3], away_output, *down_home = tie(grad_one[3], away_output, *down_home)
    one_far = far_rows(grad_one)
    one_near = near_rows(grad_one)

    def finish(far):
        grad = normalize_back(
            one_near + far.astype(jnp.float32), unit_one, inverse_one, attention_gain
        )
        return (grad_mixed + grad).astype(jnp.bfloat16)

    going = flip_some(one_far, False)
    weights_part = lax.psum_scatter(weights_part, high_bits, scatter_dimension=1, tiled=True)
    going, one_far, weights_part, *up_home = tie(
        going, one_far, weights_part, *send_home(up_rest, 1)
    )
    going, one_far, weights_part, away_output, *homes = tie(
        finish(going), one_far, weights_part, away_output, *down_home, *up_home
    )
    down_home, up_home = homes[:3], homes[3:]
    block_output = jnp.where(home, mixed_two, away_output)[None]
    going = lax.ppermute(going, ("c", "zh"), [(1, 2), (2, 1)])
    kept_far = flip_some(one_far, True)
    input_grad = jnp.where(home, finish(kept_far), going)[None]
    down_summed = jnp.swapaxes(sum_home(*down_home), 1, 2)
    up_summed = sum_home(*up_home)
    weights_part = sum_home(*send_home(weights_part, 1))
    qkv_summed, proj_summed = weights_part[:3], weights_part[3].T
    gain_two_sum, centroid_sum = early[0], early[1:]
    entries = gain_two_sum.shape[0]
    own_entries = lax.axis_index(everyone) * entries
    slice_rows = qkv_summed.shape[1]
    own_rows = lax.dynamic_slice_in_dim(
        qkv_weight, lax.axis_index(users) * slice_rows, slice_rows, 1
    )
    gain_one = jnp.sum(own_rows.astype(jnp.float32) * qkv_summed, axis=(0, 2))
    for bit in ("zh", "zl"):
        gain_one = halve(*send_half(gain_one, bit, 0))
    gain_one_sum = gain_one / lax.dynamic_slice_in_dim(attention_gain, own_entries, entries, 0)
    return (
        block_output,
        input_grad,
        gain_one_sum,
        gain_two_sum,
        centroid_sum,
        qkv_summed,
        proj_summed,
        up_summed,
        down_summed,
    )


def solution(mesh):
    shape = mesh.devices.shape
    high_bits = tuple(f"u{place}" for place in range((shape[0] // 2).bit_length() - 1))
    dp, tensor = (*high_bits, "c"), ("zh", "zl")
    mesh = Mesh(mesh.devices.reshape((2,) * len(dp + tensor)), dp + tensor)

    def program(*arguments):
        return body(high_bits, *arguments)

    return jax.shard_map(
        program,
        mesh=mesh,
        in_specs=(
            P(dp, tensor, None),
            P(),
            P(None, None, tensor),
            P(tensor, None),
            P(),
            P(),
            P(None, None, tensor),
            P(None, tensor, None),
            P(dp, tensor, None),
            P(dp, None, None),
            P(dp, None),
            P(dp, None),
        ),
        out_specs=(
            P(dp, tensor, None),
            P(dp, tensor, None),
            P(dp + tensor),
            P(dp + tensor),
            P(None, dp + tensor),
            P(None, dp, tensor),
            P(tensor, dp),
            P(None, dp, tensor),
            P(None, tensor, dp),
        ),
        check_vma=False,
    )
```

```python
import jax
import jax.numpy as jnp
from jax import lax
from jax.experimental import pallas as pl
from jax.experimental.pallas import tpu as pltpu
from jax.sharding import Mesh
from jax.sharding import PartitionSpec as P

HEAD_DIM = 64
FORWARD_BLOCKS = (512, 512)
BACKWARD_BLOCKS = (512, 256)
LOG2E = 1.4426950408889634
NEGATIVE = -1e30
TILE = 256
CHUNK = 256
TOKEN = (16, 128)
ALIGN = 16
CONTINUATIONS = 8
HBM = pl.BlockSpec(memory_space=pl.ANY)

epsilon = 1e-05
highest = lax.Precision.HIGHEST


def normalize_plain(values):
    centered = values - jnp.mean(values, axis=-1, keepdims=True)
    variance = jnp.mean(centered * centered, axis=-1, keepdims=True)
    inverse = lax.rsqrt(variance + epsilon)
    return (centered * inverse, inverse)


def normalize_back(upstream, unit_rows, inverse, gain_row):
    scaled = upstream * gain_row
    centered = scaled - jnp.mean(scaled, axis=-1, keepdims=True)
    return inverse * (centered - unit_rows * jnp.mean(scaled * unit_rows, axis=-1, keepdims=True))


def matmul(a, b, dims=((1,), (0,))):
    return lax.dot_general(a, b, (dims, ((), ())), preferred_element_type=jnp.float32)


def key_ranges(segment, blocks):
    block, fine = blocks
    token_count = segment.shape[0]
    numbers = jnp.arange(1, CONTINUATIONS + 1, dtype=jnp.int32)[:, None]
    earlier = jnp.sum((segment[None, :] < numbers).astype(jnp.int32), axis=1, keepdims=True)
    prompt = earlier[0, 0]
    start = jnp.sum(jnp.where(segment[None, :] == numbers, earlier, 0), axis=0)
    first = jnp.arange(token_count // block, dtype=jnp.int32) * block
    whole = jnp.minimum(prompt, first) // fine
    shared = (jnp.minimum(prompt, first + block) + fine - 1) // fine
    own = jnp.maximum(shared, start.reshape(-1, block)[:, 0] // fine)
    last = (first + block) // fine
    return (jnp.stack([whole, shared, own, last, jnp.full_like(whole, prompt)]), start[None, :])


def copies(pairs, semaphores):
    moved = [
        pltpu.make_async_copy(source, target, semaphores.at[place])
        for place, (source, target) in enumerate(pairs)
    ]
    for copy in moved:
        copy.start()
    for copy in moved:
        copy.wait()


def rank_rows(ref, rank, like):
    count = like.shape[0]
    return ref.at[pl.ds(pl.multiple_of(rank * count, count), count)]


def send_ranks(ref, targets, ranks, semaphores, edge, block, down):
    count = targets[0].shape[0]
    for rank in range(4):
        if down:
            first = rank * count
            due = (edge <= first) & (edge + block > first)
        else:
            last = (rank + 1) * count
            due = (edge >= last) & (edge - block < last)

        @pl.when(due)
        def _(rank=rank):
            for b, target in enumerate(targets):

                @pl.when(ranks[b] == rank)
                def _(b=b, target=target):
                    source = ref.at[rank * count : (rank + 1) * count]
                    pltpu.make_async_copy(source, target, semaphores.at[b]).start()


def take_ranks(ref, sources, ranks, semaphores, edge, block, first):
    count = sources[0].shape[0]

    @pl.when(first)
    def _():
        for b, source in enumerate(sources):
            target = rank_rows(ref, ranks[b], source)
            pltpu.make_async_copy(source, target, semaphores.at[b]).start()

    for b, source in enumerate(sources):
        begin = ranks[b] * count
        before = jnp.where(first, 0, edge)

        @pl.when((begin >= before) & (begin < edge + block))
        def _(b=b, source=source):
            target = rank_rows(ref, ranks[b], source)
            pltpu.make_async_copy(source, target, semaphores.at[b]).wait()


def await_ranks(ref, targets, ranks, semaphores):
    for b, target in enumerate(targets):
        pltpu.make_async_copy(rank_rows(ref, ranks[b], target), target, semaphores.at[b]).wait()


def forward_kernel(
    ranges, ranks, x0, x1, x2, x3, w_ref, start_ref,
    p0, p1, p2, p3, qt_ref, k_ref, kt_ref, v_ref, ctx_ref, lse_ref,
    x_ref, part_ref, vt_ref, score_ref, top_ref, sum_ref, arrived, left,
):
    step = pl.program_id(0)
    heads = qt_ref.shape[0]
    block = qt_ref.shape[2]
    fine = vt_ref.shape[3]
    step_keys = kt_ref.shape[3]
    rows = pl.ds(pl.multiple_of(step * block, block), block)

    take_ranks(x_ref, (x0, x1, x2, x3), ranks, arrived, step * block, block, step == 0)
    x = x_ref[rows, :]
    for kind in range(3):
        made = matmul(x, w_ref[kind]).astype(jnp.bfloat16)
        turned = made.T
        for head in range(heads):
            part = slice(head * HEAD_DIM, (head + 1) * HEAD_DIM)
            if kind == 0:
                qt_ref[head] = turned[part]
            if kind == 1:
                k_ref[head, rows, :] = made[:, part]
            if kind == 2:
                v_ref[head, rows, :] = made[:, part]
            for piece in range(block // step_keys if kind == 1 else 0):
                columns = slice(piece * step_keys, (piece + 1) * step_keys)
                kt_ref[piece, head] = turned[part, columns]
            for piece in range(block // fine if kind == 2 else 0):
                columns = slice(piece * fine, (piece + 1) * fine)
                at = step * (block // fine) + piece
                vt_ref[at, head, :HEAD_DIM] = turned[part, columns]
                vt_ref[at, head, HEAD_DIM:] = jnp.ones((16, fine), jnp.bfloat16)
    top_ref[...] = jnp.full_like(top_ref, NEGATIVE)
    sum_ref[...] = jnp.zeros_like(sum_ref)
    prompt = ranges[4, step]
    scale = LOG2E * HEAD_DIM ** (-0.5)

    def visit(key, masked):
        place = pl.ds(pl.multiple_of(key * fine, fine), fine)
        if masked:
            key_at = key * fine + lax.broadcasted_iota(jnp.int32, (fine, block), 0)
            query_at = step * block + lax.broadcasted_iota(jnp.int32, (fine, block), 1)
            seen = (key_at <= query_at) & ((key_at < prompt) | (key_at >= start_ref[...]))
        for head in range(heads):
            scores = matmul(k_ref[head, place, :], qt_ref[head])
            if masked:
                scores = jnp.where(seen, scores, NEGATIVE)
            score_ref[key, head] = scores
            top_ref[head] = jnp.maximum(
                top_ref[head], jnp.max(scores.reshape(fine // 8, 8, block), axis=0)
            )

    def plain(key, carry):
        visit(key, False)
        return carry

    def edge(key, carry):
        visit(key, True)
        return carry

    lax.fori_loop(0, ranges[0, step], plain, 0)
    lax.fori_loop(ranges[0, step], ranges[1, step], edge, 0)
    lax.fori_loop(ranges[2, step], ranges[3, step], edge, 0)
    for head in range(heads):
        top_ref[head, :1] = jnp.max(top_ref[head], axis=0, keepdims=True) * scale

    def add(key, carry):
        for head in range(heads):
            weights = jnp.exp2(score_ref[key, head] * scale - top_ref[head, :1])
            sum_ref[head] += matmul(vt_ref[key, head], weights.astype(jnp.bfloat16))
        return carry

    lax.fori_loop(0, ranges[1, step], add, 0)
    lax.fori_loop(ranges[2, step], ranges[3, step], add, 0)
    for head in range(heads):
        total = sum_ref[head, HEAD_DIM : HEAD_DIM + 1]
        context = sum_ref[head, :HEAD_DIM] / total
        ctx_ref[head * HEAD_DIM : (head + 1) * HEAD_DIM] = context.astype(jnp.bfloat16)
        lse_ref[head] = top_ref[head, :1] + jnp.log(total) * LOG2E
    part_ref[rows, :] = matmul(ctx_ref[...].T, w_ref[3], ((1,), (1,))).astype(jnp.bfloat16)
    send_ranks(part_ref, (p0, p1, p2, p3), ranks, left, (step + 1) * block, block, False)

    @pl.when(step == pl.num_programs(0) - 1)
    def _():
        await_ranks(part_ref, (p0, p1, p2, p3), ranks, left)


def attention_forward(ranges, start, ranks, x, w):
    tokens, width = start.shape[1], x[0].shape[1]
    local = w.shape[2]
    heads = local // HEAD_DIM
    block, fine = FORWARD_BLOCKS
    step_keys = BACKWARD_BLOCKS[1]
    count = tokens // block
    low = jnp.bfloat16
    head_rows = pl.BlockSpec((heads, tokens, HEAD_DIM), lambda i, r, n: (0, 0, 0))
    flops = 2 * tokens * width * local * 4 + tokens * tokens * local * 2
    return pl.pallas_call(
        forward_kernel,
        grid_spec=pltpu.PrefetchScalarGridSpec(
            num_scalar_prefetch=2,
            grid=(count,),
            in_specs=[
                *[HBM] * 4,
                pl.BlockSpec((4, width, local), lambda i, r, n: (0, 0, 0)),
                pl.BlockSpec((1, block), lambda i, r, n: (0, i)),
            ],
            out_specs=[
                *[HBM] * 4,
                pl.BlockSpec((heads, HEAD_DIM, block), lambda i, r, n: (0, 0, i)),
                head_rows,
                pl.BlockSpec(
                    (block // step_keys, heads, HEAD_DIM, step_keys), lambda i, r, n: (i, 0, 0, 0)
                ),
                head_rows,
                pl.BlockSpec((local, block), lambda i, r, n: (0, i)),
                pl.BlockSpec((heads, 1, block), lambda i, r, n: (0, 0, i)),
            ],
            scratch_shapes=[
                pltpu.VMEM((tokens, width), low),
                pltpu.VMEM((tokens, width), low),
                pltpu.VMEM((tokens // fine, heads, HEAD_DIM + 16, fine), low),
                pltpu.VMEM((tokens // fine, heads, fine, block), jnp.float32),
                pltpu.VMEM((heads, 8, block), jnp.float32),
                pltpu.VMEM((heads, HEAD_DIM + 16, block), jnp.float32),
                pltpu.SemaphoreType.DMA((4,)),
                pltpu.SemaphoreType.DMA((4,)),
            ],
        ),
        out_shape=[
            *[jax.ShapeDtypeStruct(x[0].shape, low)] * 4,
            jax.ShapeDtypeStruct((heads, HEAD_DIM, tokens), low),
            jax.ShapeDtypeStruct((heads, tokens, HEAD_DIM), low),
            jax.ShapeDtypeStruct((tokens // step_keys, heads, HEAD_DIM, step_keys), low),
            jax.ShapeDtypeStruct((heads, tokens, HEAD_DIM), low),
            jax.ShapeDtypeStruct((local, tokens), low),
            jax.ShapeDtypeStruct((heads, 1, tokens), jnp.float32),
        ],
        compiler_params=pltpu.CompilerParams(vmem_limit_bytes=56 << 20),
        cost_estimate=pl.CostEstimate(
            flops=4 * flops, transcendentals=tokens * tokens * heads // 2, bytes_accessed=40 << 20
        ),
        name="attention_forward",
    )(ranges, ranks, *x, w, start)


def backward_kernel(
    ranges, ranks, g0, g1, g2, g3, x0, x1, x2, x3,
    ctx_ref, lse_ref, qt_ref, start_ref, k_ref, kt_ref, v_ref, w_ref,
    p0, p1, p2, p3, weights_ref,
    g_ref, x_ref, part_ref, wgrad_ref, pgrad_ref,
    dk_ref, dv_ref, dq_ref, outer_ref, inner_ref, grad_ref, prob_ref, dscore_ref, arrived, left,
):
    number = pl.program_id(0)
    step = pl.num_programs(0) - 1 - number
    heads = qt_ref.shape[0]
    block = qt_ref.shape[2]
    fine = kt_ref.shape[3]
    local = heads * HEAD_DIM
    rows = pl.ds(pl.multiple_of(step * block, block), block)

    @pl.when(number == 0)
    def _():
        for place, (ref, sources) in enumerate(((g_ref, (g0, g1, g2, g3)), (x_ref, (x0, x1, x2, x3)))):
            for b, source in enumerate(sources):
                target = rank_rows(ref, ranks[b], source)
                pltpu.make_async_copy(source, target, arrived.at[place, b]).start()
        dk_ref[...] = jnp.zeros_like(dk_ref)
        dv_ref[...] = jnp.zeros_like(dv_ref)
        wgrad_ref[...] = jnp.zeros_like(wgrad_ref)
        pgrad_ref[...] = jnp.zeros_like(pgrad_ref)
        await_copies(g_ref, (g0, g1, g2, g3), ranks, arrived.at[0])

    upstream = g_ref[rows, :]
    outer = matmul(upstream, w_ref[3]).astype(jnp.bfloat16).T
    for head in range(heads):
        part = slice(head * HEAD_DIM, (head + 1) * HEAD_DIM)
        outer_ref[head] = outer[part]
        inner_ref[head] = jnp.sum(
            outer[part].astype(jnp.float32) * ctx_ref[part].astype(jnp.float32),
            axis=0,
            keepdims=True,
        )
    pgrad_ref[...] += matmul(ctx_ref[...], upstream)
    dq_ref[...] = jnp.zeros_like(dq_ref)
    prompt = ranges[4, step]
    scale = LOG2E * HEAD_DIM ** (-0.5)

    def add(key, head):
        prob, dscore = prob_ref[head], dscore_ref[head]
        dv_ref[key, head] += matmul(outer_ref[head], prob, ((1,), (1,)))
        dk_ref[key, head] += matmul(qt_ref[head], dscore, ((1,), (1,)))
        dq_ref[head] += matmul(kt_ref[key, head], dscore)

    def visit(number, before, masked):
        key = jnp.where(number < ranges[1, step], number, number - ranges[1, step] + ranges[2, step])
        place = pl.ds(pl.multiple_of(key * fine, fine), fine)
        if masked:
            key_at = key * fine + lax.broadcasted_iota(jnp.int32, (fine, block), 0)
            query_at = step * block + lax.broadcasted_iota(jnp.int32, (fine, block), 1)
            seen = (key_at <= query_at) & ((key_at < prompt) | (key_at >= start_ref[...]))
        for head in range(heads):
            scores = matmul(k_ref[head, place, :], qt_ref[head]) * scale
            dprob = matmul(v_ref[head, place, :], outer_ref[head])
            if before is not None:
                add(before, head)
            if masked:
                scores = jnp.where(seen, scores, NEGATIVE)
            prob = jnp.exp2(scores - lse_ref[head])
            prob_ref[head] = prob.astype(jnp.bfloat16)
            dscore_ref[head] = (prob * (dprob - inner_ref[head])).astype(jnp.bfloat16)
        return key

    visits = ranges[1, step] + ranges[3, step] - ranges[2, step]
    plain = jnp.maximum(ranges[0, step], 1)
    key = visit(0, None, True)
    key = lax.fori_loop(1, plain, lambda number, before: visit(number, before, False), key)
    key = lax.fori_loop(plain, visits, lambda number, before: visit(number, before, True), key)
    for head in range(heads):
        add(key, head)
    small = HEAD_DIM ** (-0.5)

    @pl.when(number == 0)
    def _():
        await_copies(x_ref, (x0, x1, x2, x3), ranks, arrived.at[1])

    for head in range(heads):
        part = slice(head * HEAD_DIM, (head + 1) * HEAD_DIM)
        grad_ref[0, part] = (dq_ref[head] * small).astype(jnp.bfloat16)
        for piece in range(block // fine):
            at = step * (block // fine) + piece
            columns = slice(piece * fine, (piece + 1) * fine)
            grad_ref[1, part, columns] = (dk_ref[at, head] * small).astype(jnp.bfloat16)
            grad_ref[2, part, columns] = dv_ref[at, head].astype(jnp.bfloat16)
    x = x_ref[rows, :]
    total = None
    for kind in range(3):
        wgrad_ref[kind] += matmul(grad_ref[kind], x)
        term = matmul(grad_ref[kind].T, w_ref[kind], ((1,), (1,)))
        total = term if total is None else total + term
    part_ref[rows, :] = total.astype(jnp.bfloat16)
    send_ranks(part_ref, (p0, p1, p2, p3), ranks, left, step * block, block, True)

    @pl.when(step == 0)
    def _():
        for kind in range(3):
            weights_ref[kind] = wgrad_ref[kind].T.astype(jnp.bfloat16)
        weights_ref[3] = pgrad_ref[...].T.astype(jnp.bfloat16)
        await_ranks(part_ref, (p0, p1, p2, p3), ranks, left)


def await_copies(ref, sources, ranks, semaphores):
    for b, source in enumerate(sources):
        target = rank_rows(ref, ranks[b], source)
        pltpu.make_async_copy(source, target, semaphores.at[b]).wait()


def attention_backward(ranges, start, ranks, upstream, x, saved, w):
    qt, k, kt, v, ctx, lse = saved
    tokens, width = start.shape[1], x[0].shape[1]
    local = w.shape[2]
    heads = local // HEAD_DIM
    block, fine = BACKWARD_BLOCKS
    count = tokens // block
    low = jnp.bfloat16

    def at(i):
        return count - 1 - i

    head_rows = pl.BlockSpec((heads, tokens, HEAD_DIM), lambda i, r, n: (0, 0, 0))
    flops = 2 * tokens * width * local * 8 + tokens * tokens * local * 5
    return pl.pallas_call(
        backward_kernel,
        grid_spec=pltpu.PrefetchScalarGridSpec(
            num_scalar_prefetch=2,
            grid=(count,),
            in_specs=[
                *[HBM] * 8,
                pl.BlockSpec((local, block), lambda i, r, n: (0, at(i))),
                pl.BlockSpec((heads, 1, block), lambda i, r, n: (0, 0, at(i))),
                pl.BlockSpec((heads, HEAD_DIM, block), lambda i, r, n: (0, 0, at(i))),
                pl.BlockSpec((1, block), lambda i, r, n: (0, at(i))),
                head_rows,
                pl.BlockSpec((tokens // fine, heads, HEAD_DIM, fine), lambda i, r, n: (0, 0, 0, 0)),
                head_rows,
                pl.BlockSpec((4, width, local), lambda i, r, n: (0, 0, 0)),
            ],
            out_specs=[
                *[HBM] * 4,
                pl.BlockSpec((4, width, local), lambda i, r, n: (0, 0, 0)),
            ],
            scratch_shapes=[
                pltpu.VMEM((tokens, width), low),
                pltpu.VMEM((tokens, width), low),
                pltpu.VMEM((tokens, width), low),
                pltpu.VMEM((3, local, width), jnp.float32),
                pltpu.VMEM((local, width), jnp.float32),
                pltpu.VMEM((tokens // fine, heads, HEAD_DIM, fine), jnp.float32),
                pltpu.VMEM((tokens // fine, heads, HEAD_DIM, fine), jnp.float32),
                pltpu.VMEM((heads, HEAD_DIM, block), jnp.float32),
                pltpu.VMEM((heads, HEAD_DIM, block), low),
                pltpu.VMEM((heads, 1, block), jnp.float32),
                pltpu.VMEM((3, local, block), low),
                pltpu.VMEM((heads, fine, block), low),
                pltpu.VMEM((heads, fine, block), low),
                pltpu.SemaphoreType.DMA((2, 4)),
                pltpu.SemaphoreType.DMA((4,)),
            ],
        ),
        out_shape=[
            *[jax.ShapeDtypeStruct(x[0].shape, low)] * 4,
            jax.ShapeDtypeStruct((4, width, local), low),
        ],
        compiler_params=pltpu.CompilerParams(vmem_limit_bytes=56 << 20),
        cost_estimate=pl.CostEstimate(
            flops=4 * flops, transcendentals=tokens * tokens * heads // 2, bytes_accessed=40 << 20
        ),
        name="attention_backward",
    )(ranges, ranks, *upstream, *x, ctx, lse, qt, start, k, kt, v, w)


def route_rows(route, priority, experts, capacity, row_count, ranks):
    own_start = ranks[0] * row_count
    own_route = lax.dynamic_slice_in_dim(route, own_start, row_count, 0)
    own_priority = lax.dynamic_slice_in_dim(priority, own_start, row_count, 0)
    ahead = (route[None, :] == own_route[:, None]) & (priority[None, :] < own_priority[:, None])
    kept = jnp.sum(ahead.astype(jnp.int32), axis=1) < capacity
    kinds = jnp.arange(experts, dtype=jnp.int32)
    block_hot = (route.reshape(-1, row_count)[:, :, None] == kinds).astype(jnp.int32)
    lengths = jnp.sum(block_hot, axis=1)
    starts = jnp.cumsum(lengths, axis=1) - lengths
    own_hot = (own_route[:, None] == kinds).astype(jnp.int32)
    index = jnp.arange(row_count, dtype=jnp.int32)
    before = (own_route[None, :] == own_route[:, None]) & (index[None, :] < index[:, None])
    own_starts = lax.dynamic_slice_in_dim(starts, ranks[0], 1, 0)
    place = jnp.sum(before.astype(jnp.int32), axis=1) + jnp.sum(own_hot * own_starts, axis=1)
    order = (index[:, None] == place[None, :]).astype(jnp.bfloat16)
    picked = [
        lax.dynamic_slice_in_dim(array, ranks[b], 1, 0)[0]
        for array in (starts, lengths)
        for b in range(4)
    ]
    home = at_home().astype(jnp.int32)[None]
    return (kept, order, jnp.concatenate([*picked, home]), own_hot)


def sort_rows(order, rows):
    return jnp.dot(order, rows, preferred_element_type=jnp.float32).astype(jnp.bfloat16)


def unsort_rows(order, rows):
    return matmul(order, rows.astype(jnp.bfloat16), ((0,), (0,)))


def each_tile(table, block, expert, experts, visit):
    start = table[block * experts + expert]
    end = start + table[(4 + block) * experts + expert]
    first = start // ALIGN * ALIGN

    def tile(number, carry):
        at = first + number * TILE
        visit(pl.ds(pl.multiple_of(at, ALIGN), TILE), start - at, end - at)
        return carry

    lax.fori_loop(0, jnp.where(end > start, (end - first + TILE - 1) // TILE, 0), tile, 0)


def put_rows(ref, block, place, rows, head):
    top = pl.ds(place.start, ALIGN)
    old = ref[block, top, :]
    index = lax.broadcasted_iota(jnp.int32, old.shape, 0)
    ref[block, place, :] = rows
    ref[block, top, :] = jnp.where(index < head, old, rows[:ALIGN])


def fetch_weights(choice, kept, given, targets, semaphores):
    for place, target in enumerate(targets):
        for expert in range(target.shape[0]):
            ready = semaphores.at[place, expert]

            @pl.when(choice == 1)
            def _(place=place, target=target, expert=expert, ready=ready):
                pltpu.make_async_copy(kept[place].at[expert], target.at[expert], ready).start()

            @pl.when(choice == 0)
            def _(place=place, target=target, expert=expert, ready=ready):
                pltpu.make_async_copy(given[place].at[expert], target.at[expert], ready).start()


def await_weights(kept, targets, expert, semaphores):
    for place, target in enumerate(targets):
        pltpu.make_async_copy(
            kept[place].at[expert], target.at[expert], semaphores.at[place, expert]
        ).wait()


def within(rows, head, end):
    index = lax.broadcasted_iota(jnp.int32, rows.shape, 0)
    return jnp.where((index >= head) & (index < end), rows, 0)


def block_copies(block, pairs, semaphores):
    for place, (source, targets) in enumerate(pairs):
        for b in range(4):

            @pl.when(block == b)
            def _(place=place, source=source, targets=targets, b=b):
                target = targets[b] if isinstance(targets, tuple) else targets.at[b]
                rows = source.at[b, : target.shape[0]]
                pltpu.make_async_copy(rows, target, semaphores.at[place, b]).start()


def await_blocks(pairs, semaphores):
    for place, (source, targets) in enumerate(pairs):
        for b in range(4):
            target = targets[b] if isinstance(targets, tuple) else targets.at[b]
            rows = source.at[b, : target.shape[0]]
            pltpu.make_async_copy(rows, target, semaphores.at[place, b]).wait()


def moe_steps(table, experts, inputs, weights, outputs, tails, visit, semaphores):
    block = pl.program_id(0)
    kept, given, held = weights
    arrived, left, ready = semaphores
    count = inputs[0][1][0].shape[0]

    @pl.when(block == 0)
    def _():
        for place, (target, sources) in enumerate(inputs):
            for b in range(4):
                source = sources[b] if isinstance(sources, tuple) else sources.at[b]
                rows = target.at[b, : source.shape[0]]
                pltpu.make_async_copy(source, rows, arrived.at[place, b]).start()
        fetch_weights(table[8 * experts], kept, given, held, ready)
        for ref in tails:
            ref[:, count:, :] = jnp.zeros((4, TILE, ref.shape[2]), ref.dtype)

    for place, (target, sources) in enumerate(inputs):
        source = sources[0] if isinstance(sources, tuple) else sources.at[0]
        rows = target.at[block, : source.shape[0]]
        pltpu.make_async_copy(source, rows, arrived.at[place, block]).wait()

    def expert_rows(expert, carry):
        @pl.when(block == 0)
        def _():
            await_weights(kept, held, expert, ready)

        each_tile(
            table, block, expert, experts,
            lambda place, head, end: visit(block, expert, place, head, end),
        )
        return carry

    lax.fori_loop(0, experts, expert_rows, 0)
    block_copies(block, outputs, left)

    @pl.when(block == 3)
    def _():
        await_blocks(outputs, left)


def moe_forward_kernel(
    table, x0, x1, x2, x3, own_up, own_down, new_up, new_down,
    y0, y1, y2, y3, hidden_out, slope_out,
    x_ref, y_ref, hidden_ref, slope_ref, up_ref, down_ref, *semaphores,
):
    width = up_ref.shape[2]

    def visit(block, expert, place, head, end):
        x = x_ref[block, place, :]
        total = None
        for part in range(0, width, CHUNK):
            chunk = slice(part, part + CHUNK)
            u = matmul(x, up_ref[expert, :, chunk])
            cube = 0.7978845608028654 * u * (1.0 + 0.044715 * u * u)
            bend = 1.0 + jnp.tanh(cube)
            half = 0.5 * bend
            hidden = (u * half).astype(jnp.bfloat16)
            slope = half + u * (half * (2.0 - bend)) * (
                0.7978845608028654 * (1.0 + 3.0 * 0.044715 * u * u)
            )
            put_rows(hidden_ref.at[:, :, chunk], block, place, hidden, head)
            put_rows(slope_ref.at[:, :, chunk], block, place, slope.astype(jnp.bfloat16), head)
            term = matmul(hidden, down_ref[expert, chunk, :])
            total = term if total is None else total + term
        put_rows(y_ref, block, place, total.astype(jnp.bfloat16), head)

    moe_steps(
        table, up_ref.shape[0], [(x_ref, (x0, x1, x2, x3))],
        ((own_up, own_down), (new_up, new_down), (up_ref, down_ref)),
        [(y_ref, (y0, y1, y2, y3)), (hidden_ref, hidden_out), (slope_ref, slope_out)],
        (x_ref, hidden_ref, slope_ref), visit, semaphores,
    )


def moe_backward_kernel(
    table, d0, d1, d2, d3, slope_in, own_up, own_down, new_up, new_down,
    y0, y1, y2, y3, grad_out,
    d_ref, slope_ref, y_ref, grad_ref, up_ref, down_ref, *semaphores,
):
    width = up_ref.shape[2]

    def visit(block, expert, place, head, end):
        upstream = within(d_ref[block, place, :], head, end)
        total = None
        for part in range(0, width, CHUNK):
            chunk = slice(part, part + CHUNK)
            slope = slope_ref[block, place, chunk].astype(jnp.float32)
            grad = matmul(upstream, down_ref[expert, chunk, :], ((1,), (1,))) * slope
            grad = grad.astype(jnp.bfloat16)
            put_rows(grad_ref.at[:, :, chunk], block, place, grad, head)
            term = matmul(grad, up_ref[expert, :, chunk], ((1,), (1,)))
            total = term if total is None else total + term
        put_rows(y_ref, block, place, total.astype(jnp.bfloat16), head)

    moe_steps(
        table, up_ref.shape[0], [(d_ref, (d0, d1, d2, d3)), (slope_ref, slope_in)],
        ((own_up, own_down), (new_up, new_down), (up_ref, down_ref)),
        [(y_ref, (y0, y1, y2, y3)), (grad_ref, grad_out)],
        (d_ref, grad_ref), visit, semaphores,
    )


def moe_weights_kernel(
    table, a0, a1, a2, a3, b_in, token_in, out_ref, token_ref, a_ref, b_ref, sum_ref, semaphores
):
    expert = pl.program_id(0)
    experts = pl.num_programs(0)
    count = a0.shape[0]

    @pl.when(expert == 0)
    def _():
        token_ref[...] = jnp.zeros_like(token_ref)
        a_ref[:, count:, :] = jnp.zeros((4, TILE, a_ref.shape[2]), jnp.bfloat16)
        copies(
            [(a, a_ref.at[b, :count]) for b, a in enumerate((a0, a1, a2, a3))] + [(b_in, b_ref)],
            semaphores,
        )

    sum_ref[...] = jnp.zeros_like(sum_ref)

    def of_block(block, carry):
        def visit(place, head, end):
            rows = within(a_ref[block, place, :], head, end)
            sum_ref[...] += matmul(rows, b_ref[block, place, :], ((0,), (0,)))

        each_tile(table, block, expert, experts, visit)
        return carry

    lax.fori_loop(0, 4, of_block, 0)
    out_ref[0] = sum_ref[...].astype(jnp.bfloat16)


def moe_call(kernel, name, table, arrays, grid, specs, outs, scratch, semaphores, cost):
    return pl.pallas_call(
        kernel,
        grid_spec=pltpu.PrefetchScalarGridSpec(
            num_scalar_prefetch=1,
            grid=(grid,),
            in_specs=[HBM] * len(arrays),
            out_specs=specs,
            scratch_shapes=[
                *[pltpu.VMEM(*shape) for shape in scratch],
                *[pltpu.SemaphoreType.DMA(shape) for shape in semaphores],
            ],
        ),
        out_shape=[jax.ShapeDtypeStruct(shape, jnp.bfloat16) for shape in outs],
        compiler_params=pltpu.CompilerParams(vmem_limit_bytes=58 << 20),
        cost_estimate=pl.CostEstimate(flops=cost, transcendentals=0, bytes_accessed=40 << 20),
        name=name,
    )(table, *arrays)


def moe_forward(table, x, own, new):
    count, width = x[0].shape
    experts, _, hidden = own[0].shape
    low = jnp.bfloat16
    wide, tall = ((4, count + TILE, width), low), ((4, count + TILE, hidden), low)
    *y, hid, slope = moe_call(
        moe_forward_kernel, "moe_forward", table, [*x, *own, *new], 4, [HBM] * 6,
        [(count, width)] * 4 + [tall[0], tall[0]],
        [wide, wide, tall, tall, (own[0].shape, low), (own[1].shape, low)],
        [(1, 4), (3, 4), (2, experts)], 20 * count * width * hidden,
    )
    return (y, hid, slope)


def moe_backward(table, d, slope, own, new):
    count, width = d[0].shape
    experts, _, hidden = own[0].shape
    low = jnp.bfloat16
    wide, tall = ((4, count + TILE, width), low), ((4, count + TILE, hidden), low)
    *y, grad = moe_call(
        moe_backward_kernel, "moe_backward", table, [*d, slope, *own, *new], 4, [HBM] * 5,
        [(count, width)] * 4 + [tall[0]],
        [wide, tall, wide, tall, (own[0].shape, low), (own[1].shape, low)],
        [(2, 4), (2, 4), (2, experts)], 20 * count * width * hidden,
    )
    return (y, grad)


def moe_weights(table, blocks, tall, token, experts):
    count, width = blocks[0].shape
    hidden = tall.shape[2]
    return moe_call(
        moe_weights_kernel, "moe_weights", table, [*blocks, tall, token], experts,
        [
            pl.BlockSpec((1, width, hidden), lambda e, t: (e, 0, 0)),
            pl.BlockSpec(TOKEN, lambda e, t: (0, 0)),
        ],
        [(experts, width, hidden), TOKEN],
        [((4, count + TILE, width), jnp.bfloat16), (tall.shape, jnp.bfloat16),
         ((width, hidden), jnp.float32)],
        [(5,)], 10 * count * width * hidden,
    )


def at_home():
    return lax.axis_index("c") == lax.axis_index("zh")


def swap_roles(value):
    moved = lax.ppermute(value, ("c", "zh"), [(1, 2), (2, 1)])
    return jnp.where(at_home(), value, moved)


def flip(value, axis):
    return lax.ppermute(value, axis, [(0, 1), (1, 0)])


def flip_some(value, home):
    moves = [(0, 1), (1, 0), (6, 7), (7, 6)] if home else [(2, 3), (3, 2), (4, 5), (5, 4)]
    return lax.ppermute(value, ("c", "zh", "zl"), moves)


def tie(*values):
    return lax.optimization_barrier(values)


def gather_blocks(rows):
    across = flip(rows, "zl")
    return [rows, flip(rows, "c"), across, flip(across, "c")]


def far_rows(blocks):
    return (
        flip(blocks[3], "c").astype(jnp.float32) + blocks[2].astype(jnp.float32)
    ).astype(blocks[2].dtype)


def near_rows(blocks):
    return blocks[0].astype(jnp.float32) + flip(blocks[1], "c").astype(jnp.float32)


def scatter_blocks(blocks):
    return near_rows(blocks) + flip(far_rows(blocks), "zl").astype(jnp.float32)


def send_half(value, axis, dimension):
    count = value.shape[dimension] // 2
    side = lax.axis_index(axis)
    kept = lax.dynamic_slice_in_dim(value, side * count, count, dimension)
    sent = lax.dynamic_slice_in_dim(value, (1 - side) * count, count, dimension)
    return [kept, flip(sent, axis)]


def halve(kept, came):
    return (kept.astype(jnp.float32) + came.astype(jnp.float32)).astype(kept.dtype)


def send_home(value, dimension):
    count = value.shape[dimension] // 2
    high = lax.axis_index("zh")
    straight = lax.dynamic_slice_in_dim(value, high * count, count, dimension)
    turned = lax.dynamic_slice_in_dim(value, (1 - high) * count, count, dimension)
    turned = lax.ppermute(turned, ("c", "zh"), [(0, 2), (1, 0), (2, 3), (3, 1)])
    return [straight, lax.ppermute(straight, ("c", "zh"), [(1, 2), (2, 1)]), turned]


def sum_home(straight, moved, turned):
    straight = jnp.where(at_home(), straight, moved)
    return straight.astype(jnp.float32) + turned.astype(jnp.float32)


def piece_of(weight, users):
    flat = weight.reshape(-1, weight.shape[-1])
    part = flat.shape[0] // lax.axis_size(users)
    return lax.dynamic_slice_in_dim(flat, lax.axis_index(users) * part, part, 0)


def share(piece, users, shape):
    return lax.all_gather(piece, users, axis=0, tiled=True).reshape(shape)


def share_small(piece, users, shape):
    for bit in reversed(users):
        given = flip(piece, bit)
        low = lax.axis_index(bit) == 0
        piece = jnp.concatenate([jnp.where(low, piece, given), jnp.where(low, given, piece)], axis=0)
    return piece.reshape(shape)


def body(
    high_bits,
    block_input,
    attention_gain,
    qkv_weight,
    proj_weight,
    moe_gain,
    centroids,
    expert_up,
    expert_down,
    out_grad,
    routes,
    priority,
    segments,
):
    row_count = block_input.shape[1]
    model_width = block_input.shape[2]
    experts = expert_up.shape[0]
    token_count = segments.shape[1]
    capacity = 9 * token_count // (8 * experts)
    users = (*high_bits, "c")
    core, near = lax.axis_index("c"), lax.axis_index("zl")
    ranks = jnp.stack(
        [2 * core + near, 2 * (1 - core) + near, 2 * core + 1 - near, 3 - 2 * core - near]
    )
    home = at_home()
    staying = block_input[0]
    coming = lax.ppermute(staying, ("c", "zh"), [(1, 2), (2, 1)])
    small = jnp.concatenate([qkv_weight, proj_weight.T[None]], axis=0)
    small_piece = flip(piece_of(small, users), "zh")

    def normed(rows):
        return (normalize_plain(rows.astype(jnp.float32))[0] * attention_gain).astype(jnp.bfloat16)

    normed_staying = normed(staying)
    home_across = flip_some(normed_staying, True)
    indices = jnp.stack([routes[0, :, 0], priority[0], segments[0]])
    indices = jnp.where(home, indices, flip(indices, "c"))
    segment = indices[2]
    ranges, start = key_ranges(segment, FORWARD_BLOCKS)
    coming, small_piece, home_across, ranges, start = tie(
        coming, small_piece, home_across, ranges, start
    )
    small_other = share(small_piece, users, small.shape)
    normed_coming = normed(coming)
    away_across = flip_some(normed_coming, False)
    across = jnp.where(home, home_across, away_across)
    across, up_piece, down_piece = tie(
        across, piece_of(expert_up, users), piece_of(expert_down, users)
    )
    up_piece, down_piece = flip(up_piece, "zh"), flip(down_piece, "zh")
    normed_one = jnp.where(home, normed_staying, normed_coming)
    normed_one = [normed_one, flip(normed_one, "c"), across, flip(across, "c")]
    inputs = jnp.where(home, staying, coming).astype(jnp.float32)
    unit_one, inverse_one = normalize_plain(inputs)
    small = jnp.where(home, small, small_other)
    *attended, qt, k, kt, v, ctx, lse = attention_forward(
        ranges, start, ranks, normed_one, small
    )
    saved = (qt, k, kt, v, ctx, lse)
    attended[3], up_piece, down_piece, indices = tie(
        attended[3], up_piece, down_piece, indices
    )
    new_experts = [share(piece, users, expert_up.shape) for piece in (up_piece, down_piece)]
    back_ranges = key_ranges(indices[2], BACKWARD_BLOCKS)[0]
    kept_rows, order, table, hot_rows = route_rows(
        indices[0], indices[1], experts, capacity, row_count, ranks
    )
    own_experts = (expert_up, expert_down)
    far, back_ranges, order, table, kept_rows, upstream = tie(
        flip(far_rows(attended), "zl"), back_ranges, order, table, kept_rows, out_grad[0]
    )
    away_upstream = lax.ppermute(upstream, ("c", "zh"), [(1, 2), (2, 1)])
    upstream = jnp.where(home, upstream, away_upstream).astype(jnp.float32)
    attended = near_rows(attended) + far.astype(jnp.float32)
    mixed_one = inputs + attended
    unit_two, inverse_two = normalize_plain(mixed_one)
    normed_two_rows = (unit_two * moe_gain).astype(jnp.bfloat16)
    centroid_rows = jnp.dot(
        hot_rows.astype(jnp.bfloat16), centroids, preferred_element_type=jnp.float32
    )
    normed_two_float = normed_two_rows.astype(jnp.float32)
    gate_prob = jax.nn.sigmoid(jnp.sum(normed_two_float * centroid_rows, axis=-1))
    gate_used = jnp.where(kept_rows, gate_prob, 0.0)
    grad_eo_rows = (gate_used[:, None] * upstream).astype(jnp.bfloat16)
    sorted_rows = sort_rows(order, normed_two_rows)
    beside, across = flip(sorted_rows, "c"), flip(sorted_rows, "zl")
    across, grad_sorted = tie(across, sort_rows(order, grad_eo_rows))
    grad_beside, grad_across = flip(grad_sorted, "c"), flip(grad_sorted, "zl")
    dispatched = [sorted_rows, beside, across, flip(across, "c")]
    returned, hidden, slope = moe_forward(table, dispatched, own_experts, new_experts)
    grad_across, *returned = tie(grad_across, *returned)
    returned_far, grad_corner = tie(far_rows(returned), flip(grad_across, "c"))
    grad_dispatched = [grad_sorted, grad_beside, grad_across, grad_corner]
    returned_far = flip(returned_far, "zl")
    returned_near = near_rows(returned)
    back_moe, grad_upward = moe_backward(table, grad_dispatched, slope, own_experts, new_experts)
    returned_far, back_moe[3] = tie(returned_far, back_moe[3])
    back_far, hidden = tie(far_rows(back_moe), hidden)
    back_far = flip(back_far, "zl")
    back_near = near_rows(back_moe)
    down_part, token = moe_weights(table, grad_dispatched, hidden, back_moe[3], experts)
    back_far, token = tie(back_far, token)
    expert_out = unsort_rows(order, returned_near + returned_far.astype(jnp.float32))
    mixed_two = (mixed_one + gate_used[:, None] * expert_out).astype(jnp.bfloat16)
    grad_gate = jnp.where(kept_rows, jnp.sum(upstream * expert_out, axis=-1), 0.0)
    grad_score = grad_gate * gate_prob * (1.0 - gate_prob)
    down_rest = lax.psum_scatter(down_part, high_bits, scatter_dimension=1, tiled=True)
    back_moe = back_near + back_far.astype(jnp.float32)
    grad_two = unsort_rows(order, back_moe) + grad_score[:, None] * centroid_rows
    centroid_part = jnp.einsum(
        "te,td->ed",
        hot_rows.astype(jnp.float32),
        grad_score[:, None] * normed_two_float,
        precision=highest,
    )
    moe_gain_part = jnp.sum(grad_two * unit_two, axis=0)
    grad_mixed = upstream + normalize_back(grad_two, unit_two, inverse_two, moe_gain)
    grad_mixed, grad_upward = tie(grad_mixed, grad_upward)
    up_part, _ = moe_weights(table, dispatched, grad_upward, token, experts)
    grad_att = gather_blocks(grad_mixed.astype(jnp.bfloat16))
    early = jnp.concatenate([moe_gain_part[None], centroid_part], axis=0)
    everyone = (*users, "zh", "zl")
    early = jnp.swapaxes(early.reshape(experts + 1, lax.axis_size(everyone), -1), 0, 1)
    early = jnp.sum(lax.all_to_all(early, everyone, 0, 0, tiled=True), axis=0)
    grad_att[2], early, up_part = tie(grad_att[2], early, up_part)
    grad_att[3] = flip(grad_att[2], "c")
    up_rest = lax.psum_scatter(up_part, high_bits, scatter_dimension=1, tiled=True)
    down_rest, mixed_two, grad_att[3] = tie(down_rest, mixed_two, grad_att[3])
    down_home = send_home(down_rest, 1)
    away_output = lax.ppermute(mixed_two, ("c", "zh"), [(1, 2), (2, 1)])
    *grad_one, weights_part = attention_backward(
        back_ranges, start, ranks, grad_att, normed_one, saved, small
    )
    grad_one[3], away_output, *down_home = tie(grad_one[3], away_output, *down_home)
    one_far = far_rows(grad_one)
    one_near = near_rows(grad_one)

    def finish(far):
        grad = normalize_back(
            one_near + far.astype(jnp.float32), unit_one, inverse_one, attention_gain
        )
        return (grad_mixed + grad).astype(jnp.bfloat16)

    going = flip_some(one_far, False)
    weights_part = lax.psum_scatter(weights_part, high_bits, scatter_dimension=1, tiled=True)
    up_home = send_home(up_rest, 1)
    going, one_far, weights_part, up_home[0], up_home[1] = tie(
        going, one_far, weights_part, up_home[0], up_home[1]
    )
    going, one_far, weights_part, away_output, *homes = tie(
        finish(going), one_far, weights_part, away_output, *down_home, *up_home
    )
    down_home, up_home = homes[:3], homes[3:]
    block_output = jnp.where(home, mixed_two, away_output)[None]
    going = lax.ppermute(going, ("c", "zh"), [(1, 2), (2, 1)])
    kept_far = flip_some(one_far, True)
    input_grad = jnp.where(home, finish(kept_far), going)[None]
    down_summed = jnp.swapaxes(sum_home(*down_home), 1, 2)
    up_summed = sum_home(*up_home)
    weights_part = sum_home(*send_home(weights_part, 1))
    qkv_summed, proj_summed = weights_part[:3], weights_part[3].T
    gain_two_sum, centroid_sum = early[0], early[1:]
    entries = gain_two_sum.shape[0]
    own_entries = lax.axis_index(everyone) * entries
    slice_rows = qkv_summed.shape[1]
    own_rows = lax.dynamic_slice_in_dim(
        qkv_weight, lax.axis_index(users) * slice_rows, slice_rows, 1
    )
    gain_one = jnp.sum(own_rows.astype(jnp.float32) * qkv_summed, axis=(0, 2))
    for bit in ("zh", "zl"):
        gain_one = halve(*send_half(gain_one, bit, 0))
    gain_one_sum = gain_one / lax.dynamic_slice_in_dim(attention_gain, own_entries, entries, 0)
    return (
        block_output,
        input_grad,
        gain_one_sum,
        gain_two_sum,
        centroid_sum,
        qkv_summed,
        proj_summed,
        up_summed,
        down_summed,
    )


def solution(mesh):
    shape = mesh.devices.shape
    high_bits = tuple(f"u{place}" for place in range((shape[0] // 2).bit_length() - 1))
    dp, tensor = (*high_bits, "c"), ("zh", "zl")
    mesh = Mesh(mesh.devices.reshape((2,) * len(dp + tensor)), dp + tensor)

    def program(*arguments):
        return body(high_bits, *arguments)

    return jax.shard_map(
        program,
        mesh=mesh,
        in_specs=(
            P(dp, tensor, None),
            P(),
            P(None, None, tensor),
            P(tensor, None),
            P(),
            P(),
            P(None, None, tensor),
            P(None, tensor, None),
            P(dp, tensor, None),
            P(dp, None, None),
            P(dp, None),
            P(dp, None),
        ),
        out_specs=(
            P(dp, tensor, None),
            P(dp, tensor, None),
            P(dp + tensor),
            P(dp + tensor),
            P(None, dp + tensor),
            P(None, dp, tensor),
            P(tensor, dp),
            P(None, dp, tensor),
            P(None, tensor, dp),
        ),
        check_vma=False,
    )
```

```python
import jax
import jax.numpy as jnp
from jax import lax
from jax.experimental import pallas as pl
from jax.experimental.pallas import tpu as pltpu
from jax.sharding import Mesh
from jax.sharding import PartitionSpec as P

HEAD_DIM = 64
FORWARD_BLOCKS = (512, 512)
BACKWARD_BLOCKS = (512, 256)
LOG2E = 1.4426950408889634
NEGATIVE = -1e30
TILE = 256
CHUNK = 256
TOKEN = (16, 128)
ALIGN = 16
CONTINUATIONS = 8
HBM = pl.BlockSpec(memory_space=pl.ANY)

epsilon = 1e-05
highest = lax.Precision.HIGHEST


def normalize_plain(values):
    centered = values - jnp.mean(values, axis=-1, keepdims=True)
    variance = jnp.mean(centered * centered, axis=-1, keepdims=True)
    inverse = lax.rsqrt(variance + epsilon)
    return (centered * inverse, inverse)


def normalize_back(upstream, unit_rows, inverse, gain_row):
    scaled = upstream * gain_row
    centered = scaled - jnp.mean(scaled, axis=-1, keepdims=True)
    return inverse * (centered - unit_rows * jnp.mean(scaled * unit_rows, axis=-1, keepdims=True))


def matmul(a, b, dims=((1,), (0,))):
    return lax.dot_general(a, b, (dims, ((), ())), preferred_element_type=jnp.float32)


def key_ranges(segment, blocks):
    block, fine = blocks
    token_count = segment.shape[0]
    numbers = jnp.arange(1, CONTINUATIONS + 1, dtype=jnp.int32)[:, None]
    earlier = jnp.sum((segment[None, :] < numbers).astype(jnp.int32), axis=1, keepdims=True)
    prompt = earlier[0, 0]
    start = jnp.sum(jnp.where(segment[None, :] == numbers, earlier, 0), axis=0)
    first = jnp.arange(token_count // block, dtype=jnp.int32) * block
    whole = jnp.minimum(prompt, first) // fine
    shared = (jnp.minimum(prompt, first + block) + fine - 1) // fine
    own = jnp.maximum(shared, start.reshape(-1, block)[:, 0] // fine)
    last = (first + block) // fine
    return (jnp.stack([whole, shared, own, last, jnp.full_like(whole, prompt)]), start[None, :])


def copies(pairs, semaphores):
    moved = [
        pltpu.make_async_copy(source, target, semaphores.at[place])
        for place, (source, target) in enumerate(pairs)
    ]
    for copy in moved:
        copy.start()
    for copy in moved:
        copy.wait()


def rank_rows(ref, rank, like):
    count = like.shape[0]
    return ref.at[pl.ds(pl.multiple_of(rank * count, count), count)]


def send_ranks(ref, targets, ranks, semaphores, edge, block, down):
    count = targets[0].shape[0]
    for rank in range(4):
        if down:
            first = rank * count
            due = (edge <= first) & (edge + block > first)
        else:
            last = (rank + 1) * count
            due = (edge >= last) & (edge - block < last)

        @pl.when(due)
        def _(rank=rank):
            for b, target in enumerate(targets):

                @pl.when(ranks[b] == rank)
                def _(b=b, target=target):
                    source = ref.at[rank * count : (rank + 1) * count]
                    pltpu.make_async_copy(source, target, semaphores.at[b]).start()


def take_ranks(ref, sources, ranks, semaphores, edge, block, first):
    count = sources[0].shape[0]

    @pl.when(first)
    def _():
        for b, source in enumerate(sources):
            target = rank_rows(ref, ranks[b], source)
            pltpu.make_async_copy(source, target, semaphores.at[b]).start()

    for b, source in enumerate(sources):
        begin = ranks[b] * count
        before = jnp.where(first, 0, edge)

        @pl.when((begin >= before) & (begin < edge + block))
        def _(b=b, source=source):
            target = rank_rows(ref, ranks[b], source)
            pltpu.make_async_copy(source, target, semaphores.at[b]).wait()


def await_ranks(ref, targets, ranks, semaphores):
    for b, target in enumerate(targets):
        pltpu.make_async_copy(rank_rows(ref, ranks[b], target), target, semaphores.at[b]).wait()


def forward_kernel(
    ranges, ranks, x0, x1, x2, x3, w_ref, start_ref,
    p0, p1, p2, p3, qt_ref, k_ref, kt_ref, v_ref, ctx_ref, lse_ref,
    x_ref, part_ref, vt_ref, score_ref, top_ref, sum_ref, arrived, left,
):
    step = pl.program_id(0)
    heads = qt_ref.shape[0]
    block = qt_ref.shape[2]
    fine = vt_ref.shape[3]
    step_keys = kt_ref.shape[3]
    rows = pl.ds(pl.multiple_of(step * block, block), block)

    take_ranks(x_ref, (x0, x1, x2, x3), ranks, arrived, step * block, block, step == 0)
    x = x_ref[rows, :]
    for kind in range(3):
        made = matmul(x, w_ref[kind]).astype(jnp.bfloat16)
        turned = made.T
        for head in range(heads):
            part = slice(head * HEAD_DIM, (head + 1) * HEAD_DIM)
            if kind == 0:
                qt_ref[head] = turned[part]
            if kind == 1:
                k_ref[head, rows, :] = made[:, part]
            if kind == 2:
                v_ref[head, rows, :] = made[:, part]
            for piece in range(block // step_keys if kind == 1 else 0):
                columns = slice(piece * step_keys, (piece + 1) * step_keys)
                kt_ref[piece, head] = turned[part, columns]
            for piece in range(block // fine if kind == 2 else 0):
                columns = slice(piece * fine, (piece + 1) * fine)
                at = step * (block // fine) + piece
                vt_ref[at, head, :HEAD_DIM] = turned[part, columns]
                vt_ref[at, head, HEAD_DIM:] = jnp.ones((16, fine), jnp.bfloat16)
    top_ref[...] = jnp.full_like(top_ref, NEGATIVE)
    sum_ref[...] = jnp.zeros_like(sum_ref)
    prompt = ranges[4, step]
    scale = LOG2E * HEAD_DIM ** (-0.5)

    def visit(key, masked):
        place = pl.ds(pl.multiple_of(key * fine, fine), fine)
        if masked:
            key_at = key * fine + lax.broadcasted_iota(jnp.int32, (fine, block), 0)
            query_at = step * block + lax.broadcasted_iota(jnp.int32, (fine, block), 1)
            seen = (key_at <= query_at) & ((key_at < prompt) | (key_at >= start_ref[...]))
        for head in range(heads):
            scores = matmul(k_ref[head, place, :], qt_ref[head])
            if masked:
                scores = jnp.where(seen, scores, NEGATIVE)
            score_ref[key, head] = scores
            top_ref[head] = jnp.maximum(
                top_ref[head], jnp.max(scores.reshape(fine // 8, 8, block), axis=0)
            )

    def plain(key, carry):
        visit(key, False)
        return carry

    def edge(key, carry):
        visit(key, True)
        return carry

    lax.fori_loop(0, ranges[0, step], plain, 0)
    lax.fori_loop(ranges[0, step], ranges[1, step], edge, 0)
    lax.fori_loop(ranges[2, step], ranges[3, step], edge, 0)
    for head in range(heads):
        top_ref[head, :1] = jnp.max(top_ref[head], axis=0, keepdims=True) * scale

    def add(key, carry):
        for head in range(heads):
            weights = jnp.exp2(score_ref[key, head] * scale - top_ref[head, :1])
            sum_ref[head] += matmul(vt_ref[key, head], weights.astype(jnp.bfloat16))
        return carry

    lax.fori_loop(0, ranges[1, step], add, 0)
    lax.fori_loop(ranges[2, step], ranges[3, step], add, 0)
    for head in range(heads):
        total = sum_ref[head, HEAD_DIM : HEAD_DIM + 1]
        context = sum_ref[head, :HEAD_DIM] / total
        ctx_ref[head * HEAD_DIM : (head + 1) * HEAD_DIM] = context.astype(jnp.bfloat16)
        lse_ref[head] = top_ref[head, :1] + jnp.log(total) * LOG2E
    part_ref[rows, :] = matmul(ctx_ref[...].T, w_ref[3], ((1,), (1,))).astype(jnp.bfloat16)
    send_ranks(part_ref, (p0, p1, p2, p3), ranks, left, (step + 1) * block, block, False)

    @pl.when(step == pl.num_programs(0) - 1)
    def _():
        await_ranks(part_ref, (p0, p1, p2, p3), ranks, left)


def attention_forward(ranges, start, ranks, x, w):
    tokens, width = start.shape[1], x[0].shape[1]
    local = w.shape[2]
    heads = local // HEAD_DIM
    block, fine = FORWARD_BLOCKS
    step_keys = BACKWARD_BLOCKS[1]
    count = tokens // block
    low = jnp.bfloat16
    head_rows = pl.BlockSpec((heads, tokens, HEAD_DIM), lambda i, r, n: (0, 0, 0))
    flops = 2 * tokens * width * local * 4 + tokens * tokens * local * 2
    return pl.pallas_call(
        forward_kernel,
        grid_spec=pltpu.PrefetchScalarGridSpec(
            num_scalar_prefetch=2,
            grid=(count,),
            in_specs=[
                *[HBM] * 4,
                pl.BlockSpec((4, width, local), lambda i, r, n: (0, 0, 0)),
                pl.BlockSpec((1, block), lambda i, r, n: (0, i)),
            ],
            out_specs=[
                *[HBM] * 4,
                pl.BlockSpec((heads, HEAD_DIM, block), lambda i, r, n: (0, 0, i)),
                head_rows,
                pl.BlockSpec(
                    (block // step_keys, heads, HEAD_DIM, step_keys), lambda i, r, n: (i, 0, 0, 0)
                ),
                head_rows,
                pl.BlockSpec((local, block), lambda i, r, n: (0, i)),
                pl.BlockSpec((heads, 1, block), lambda i, r, n: (0, 0, i)),
            ],
            scratch_shapes=[
                pltpu.VMEM((tokens, width), low),
                pltpu.VMEM((tokens, width), low),
                pltpu.VMEM((tokens // fine, heads, HEAD_DIM + 16, fine), low),
                pltpu.VMEM((tokens // fine, heads, fine, block), jnp.float32),
                pltpu.VMEM((heads, 8, block), jnp.float32),
                pltpu.VMEM((heads, HEAD_DIM + 16, block), jnp.float32),
                pltpu.SemaphoreType.DMA((4,)),
                pltpu.SemaphoreType.DMA((4,)),
            ],
        ),
        out_shape=[
            *[jax.ShapeDtypeStruct(x[0].shape, low)] * 4,
            jax.ShapeDtypeStruct((heads, HEAD_DIM, tokens), low),
            jax.ShapeDtypeStruct((heads, tokens, HEAD_DIM), low),
            jax.ShapeDtypeStruct((tokens // step_keys, heads, HEAD_DIM, step_keys), low),
            jax.ShapeDtypeStruct((heads, tokens, HEAD_DIM), low),
            jax.ShapeDtypeStruct((local, tokens), low),
            jax.ShapeDtypeStruct((heads, 1, tokens), jnp.float32),
        ],
        compiler_params=pltpu.CompilerParams(vmem_limit_bytes=56 << 20),
        cost_estimate=pl.CostEstimate(
            flops=4 * flops, transcendentals=tokens * tokens * heads // 2, bytes_accessed=40 << 20
        ),
        name="attention_forward",
    )(ranges, ranks, *x, w, start)


def backward_kernel(
    ranges, ranks, g0, g1, g2, g3, x0, x1, x2, x3,
    ctx_ref, lse_ref, qt_ref, start_ref, k_ref, kt_ref, v_ref, w_ref,
    p0, p1, p2, p3, weights_ref,
    g_ref, x_ref, part_ref, wgrad_ref, pgrad_ref,
    dk_ref, dv_ref, dq_ref, outer_ref, inner_ref, grad_ref, prob_ref, dscore_ref, arrived, left,
):
    number = pl.program_id(0)
    step = pl.num_programs(0) - 1 - number
    heads = qt_ref.shape[0]
    block = qt_ref.shape[2]
    fine = kt_ref.shape[3]
    local = heads * HEAD_DIM
    rows = pl.ds(pl.multiple_of(step * block, block), block)

    @pl.when(number == 0)
    def _():
        for place, (ref, sources) in enumerate(((g_ref, (g0, g1, g2, g3)), (x_ref, (x0, x1, x2, x3)))):
            for b, source in enumerate(sources):
                target = rank_rows(ref, ranks[b], source)
                pltpu.make_async_copy(source, target, arrived.at[place, b]).start()
        dk_ref[...] = jnp.zeros_like(dk_ref)
        dv_ref[...] = jnp.zeros_like(dv_ref)
        wgrad_ref[...] = jnp.zeros_like(wgrad_ref)
        pgrad_ref[...] = jnp.zeros_like(pgrad_ref)
        await_copies(g_ref, (g0, g1, g2, g3), ranks, arrived.at[0])

    upstream = g_ref[rows, :]
    outer = matmul(upstream, w_ref[3]).astype(jnp.bfloat16).T
    for head in range(heads):
        part = slice(head * HEAD_DIM, (head + 1) * HEAD_DIM)
        outer_ref[head] = outer[part]
        inner_ref[head] = jnp.sum(
            outer[part].astype(jnp.float32) * ctx_ref[part].astype(jnp.float32),
            axis=0,
            keepdims=True,
        )
    pgrad_ref[...] += matmul(ctx_ref[...], upstream)
    dq_ref[...] = jnp.zeros_like(dq_ref)
    prompt = ranges[4, step]
    scale = LOG2E * HEAD_DIM ** (-0.5)

    def add(key, head):
        prob, dscore = prob_ref[head], dscore_ref[head]
        dv_ref[key, head] += matmul(outer_ref[head], prob, ((1,), (1,)))
        dk_ref[key, head] += matmul(qt_ref[head], dscore, ((1,), (1,)))
        dq_ref[head] += matmul(kt_ref[key, head], dscore)

    def visit(number, before, masked):
        key = jnp.where(number < ranges[1, step], number, number - ranges[1, step] + ranges[2, step])
        place = pl.ds(pl.multiple_of(key * fine, fine), fine)
        if masked:
            key_at = key * fine + lax.broadcasted_iota(jnp.int32, (fine, block), 0)
            query_at = step * block + lax.broadcasted_iota(jnp.int32, (fine, block), 1)
            seen = (key_at <= query_at) & ((key_at < prompt) | (key_at >= start_ref[...]))
        for head in range(heads):
            scores = matmul(k_ref[head, place, :], qt_ref[head]) * scale
            dprob = matmul(v_ref[head, place, :], outer_ref[head])
            if before is not None:
                add(before, head)
            if masked:
                scores = jnp.where(seen, scores, NEGATIVE)
            prob = jnp.exp2(scores - lse_ref[head])
            prob_ref[head] = prob.astype(jnp.bfloat16)
            dscore_ref[head] = (prob * (dprob - inner_ref[head])).astype(jnp.bfloat16)
        return key

    visits = ranges[1, step] + ranges[3, step] - ranges[2, step]
    plain = jnp.maximum(ranges[0, step], 1)
    key = visit(0, None, True)
    key = lax.fori_loop(1, plain, lambda number, before: visit(number, before, False), key)
    key = lax.fori_loop(plain, visits, lambda number, before: visit(number, before, True), key)
    for head in range(heads):
        add(key, head)
    small = HEAD_DIM ** (-0.5)

    @pl.when(number == 0)
    def _():
        await_copies(x_ref, (x0, x1, x2, x3), ranks, arrived.at[1])

    for head in range(heads):
        part = slice(head * HEAD_DIM, (head + 1) * HEAD_DIM)
        grad_ref[0, part] = (dq_ref[head] * small).astype(jnp.bfloat16)
        for piece in range(block // fine):
            at = step * (block // fine) + piece
            columns = slice(piece * fine, (piece + 1) * fine)
            grad_ref[1, part, columns] = (dk_ref[at, head] * small).astype(jnp.bfloat16)
            grad_ref[2, part, columns] = dv_ref[at, head].astype(jnp.bfloat16)
    x = x_ref[rows, :]
    total = None
    for kind in range(3):
        wgrad_ref[kind] += matmul(grad_ref[kind], x)
        term = matmul(grad_ref[kind].T, w_ref[kind], ((1,), (1,)))
        total = term if total is None else total + term
    part_ref[rows, :] = total.astype(jnp.bfloat16)
    send_ranks(part_ref, (p0, p1, p2, p3), ranks, left, step * block, block, True)

    @pl.when(step == 0)
    def _():
        for kind in range(3):
            weights_ref[kind] = wgrad_ref[kind].T.astype(jnp.bfloat16)
        weights_ref[3] = pgrad_ref[...].T.astype(jnp.bfloat16)
        await_ranks(part_ref, (p0, p1, p2, p3), ranks, left)


def await_copies(ref, sources, ranks, semaphores):
    for b, source in enumerate(sources):
        target = rank_rows(ref, ranks[b], source)
        pltpu.make_async_copy(source, target, semaphores.at[b]).wait()


def attention_backward(ranges, start, ranks, upstream, x, saved, w):
    qt, k, kt, v, ctx, lse = saved
    tokens, width = start.shape[1], x[0].shape[1]
    local = w.shape[2]
    heads = local // HEAD_DIM
    block, fine = BACKWARD_BLOCKS
    count = tokens // block
    low = jnp.bfloat16

    def at(i):
        return count - 1 - i

    head_rows = pl.BlockSpec((heads, tokens, HEAD_DIM), lambda i, r, n: (0, 0, 0))
    flops = 2 * tokens * width * local * 8 + tokens * tokens * local * 5
    return pl.pallas_call(
        backward_kernel,
        grid_spec=pltpu.PrefetchScalarGridSpec(
            num_scalar_prefetch=2,
            grid=(count,),
            in_specs=[
                *[HBM] * 8,
                pl.BlockSpec((local, block), lambda i, r, n: (0, at(i))),
                pl.BlockSpec((heads, 1, block), lambda i, r, n: (0, 0, at(i))),
                pl.BlockSpec((heads, HEAD_DIM, block), lambda i, r, n: (0, 0, at(i))),
                pl.BlockSpec((1, block), lambda i, r, n: (0, at(i))),
                head_rows,
                pl.BlockSpec((tokens // fine, heads, HEAD_DIM, fine), lambda i, r, n: (0, 0, 0, 0)),
                head_rows,
                pl.BlockSpec((4, width, local), lambda i, r, n: (0, 0, 0)),
            ],
            out_specs=[
                *[HBM] * 4,
                pl.BlockSpec((4, width, local), lambda i, r, n: (0, 0, 0)),
            ],
            scratch_shapes=[
                pltpu.VMEM((tokens, width), low),
                pltpu.VMEM((tokens, width), low),
                pltpu.VMEM((tokens, width), low),
                pltpu.VMEM((3, local, width), jnp.float32),
                pltpu.VMEM((local, width), jnp.float32),
                pltpu.VMEM((tokens // fine, heads, HEAD_DIM, fine), jnp.float32),
                pltpu.VMEM((tokens // fine, heads, HEAD_DIM, fine), jnp.float32),
                pltpu.VMEM((heads, HEAD_DIM, block), jnp.float32),
                pltpu.VMEM((heads, HEAD_DIM, block), low),
                pltpu.VMEM((heads, 1, block), jnp.float32),
                pltpu.VMEM((3, local, block), low),
                pltpu.VMEM((heads, fine, block), low),
                pltpu.VMEM((heads, fine, block), low),
                pltpu.SemaphoreType.DMA((2, 4)),
                pltpu.SemaphoreType.DMA((4,)),
            ],
        ),
        out_shape=[
            *[jax.ShapeDtypeStruct(x[0].shape, low)] * 4,
            jax.ShapeDtypeStruct((4, width, local), low),
        ],
        compiler_params=pltpu.CompilerParams(vmem_limit_bytes=56 << 20),
        cost_estimate=pl.CostEstimate(
            flops=4 * flops, transcendentals=tokens * tokens * heads // 2, bytes_accessed=40 << 20
        ),
        name="attention_backward",
    )(ranges, ranks, *upstream, *x, ctx, lse, qt, start, k, kt, v, w)


def route_rows(route, priority, experts, capacity, row_count, ranks):
    own_start = ranks[0] * row_count
    own_route = lax.dynamic_slice_in_dim(route, own_start, row_count, 0)
    own_priority = lax.dynamic_slice_in_dim(priority, own_start, row_count, 0)
    ahead = (route[None, :] == own_route[:, None]) & (priority[None, :] < own_priority[:, None])
    kept = jnp.sum(ahead.astype(jnp.int32), axis=1) < capacity
    kinds = jnp.arange(experts, dtype=jnp.int32)
    block_hot = (route.reshape(-1, row_count)[:, :, None] == kinds).astype(jnp.int32)
    lengths = jnp.sum(block_hot, axis=1)
    starts = jnp.cumsum(lengths, axis=1) - lengths
    own_hot = (own_route[:, None] == kinds).astype(jnp.int32)
    index = jnp.arange(row_count, dtype=jnp.int32)
    before = (own_route[None, :] == own_route[:, None]) & (index[None, :] < index[:, None])
    own_starts = lax.dynamic_slice_in_dim(starts, ranks[0], 1, 0)
    place = jnp.sum(before.astype(jnp.int32), axis=1) + jnp.sum(own_hot * own_starts, axis=1)
    order = (index[:, None] == place[None, :]).astype(jnp.bfloat16)
    picked = [
        lax.dynamic_slice_in_dim(array, ranks[b], 1, 0)[0]
        for array in (starts, lengths)
        for b in range(4)
    ]
    home = at_home().astype(jnp.int32)[None]
    return (kept, order, jnp.concatenate([*picked, home]), own_hot)


def sort_rows(order, rows):
    return jnp.dot(order, rows, preferred_element_type=jnp.float32).astype(jnp.bfloat16)


def unsort_rows(order, rows):
    return matmul(order, rows.astype(jnp.bfloat16), ((0,), (0,)))


def each_tile(table, block, expert, experts, visit):
    start = table[block * experts + expert]
    end = start + table[(4 + block) * experts + expert]
    first = start // ALIGN * ALIGN

    def tile(number, carry):
        at = first + number * TILE
        visit(pl.ds(pl.multiple_of(at, ALIGN), TILE), start - at, end - at)
        return carry

    lax.fori_loop(0, jnp.where(end > start, (end - first + TILE - 1) // TILE, 0), tile, 0)


def put_rows(ref, block, place, rows, head):
    top = pl.ds(place.start, ALIGN)
    old = ref[block, top, :]
    index = lax.broadcasted_iota(jnp.int32, old.shape, 0)
    ref[block, place, :] = rows
    ref[block, top, :] = jnp.where(index < head, old, rows[:ALIGN])


def fetch_weights(choice, kept, given, targets, semaphores):
    for place, target in enumerate(targets):
        for expert in range(target.shape[0]):
            ready = semaphores.at[place, expert]

            @pl.when(choice == 1)
            def _(place=place, target=target, expert=expert, ready=ready):
                pltpu.make_async_copy(kept[place].at[expert], target.at[expert], ready).start()

            @pl.when(choice == 0)
            def _(place=place, target=target, expert=expert, ready=ready):
                pltpu.make_async_copy(given[place].at[expert], target.at[expert], ready).start()


def await_weights(kept, targets, expert, semaphores):
    for place, target in enumerate(targets):
        pltpu.make_async_copy(
            kept[place].at[expert], target.at[expert], semaphores.at[place, expert]
        ).wait()


def within(rows, head, end):
    index = lax.broadcasted_iota(jnp.int32, rows.shape, 0)
    return jnp.where((index >= head) & (index < end), rows, 0)


def block_copies(block, pairs, semaphores):
    for place, (source, targets) in enumerate(pairs):
        for b in range(4):

            @pl.when(block == b)
            def _(place=place, source=source, targets=targets, b=b):
                target = targets[b] if isinstance(targets, tuple) else targets.at[b]
                rows = source.at[b, : target.shape[0]]
                pltpu.make_async_copy(rows, target, semaphores.at[place, b]).start()


def await_blocks(pairs, semaphores):
    for place, (source, targets) in enumerate(pairs):
        for b in range(4):
            target = targets[b] if isinstance(targets, tuple) else targets.at[b]
            rows = source.at[b, : target.shape[0]]
            pltpu.make_async_copy(rows, target, semaphores.at[place, b]).wait()


def moe_steps(table, experts, inputs, weights, outputs, tails, visit, semaphores):
    block = pl.program_id(0)
    kept, given, held = weights
    arrived, left, ready = semaphores
    count = inputs[0][1][0].shape[0]

    @pl.when(block == 0)
    def _():
        for place, (target, sources) in enumerate(inputs):
            for b in range(4):
                source = sources[b] if isinstance(sources, tuple) else sources.at[b]
                rows = target.at[b, : source.shape[0]]
                pltpu.make_async_copy(source, rows, arrived.at[place, b]).start()
        fetch_weights(table[8 * experts], kept, given, held, ready)
        for ref in tails:
            ref[:, count:, :] = jnp.zeros((4, TILE, ref.shape[2]), ref.dtype)

    for place, (target, sources) in enumerate(inputs):
        source = sources[0] if isinstance(sources, tuple) else sources.at[0]
        rows = target.at[block, : source.shape[0]]
        pltpu.make_async_copy(source, rows, arrived.at[place, block]).wait()

    def expert_rows(expert, carry):
        @pl.when(block == 0)
        def _():
            await_weights(kept, held, expert, ready)

        each_tile(
            table, block, expert, experts,
            lambda place, head, end: visit(block, expert, place, head, end),
        )
        return carry

    lax.fori_loop(0, experts, expert_rows, 0)
    block_copies(block, outputs, left)

    @pl.when(block == 3)
    def _():
        await_blocks(outputs, left)


def moe_forward_kernel(
    table, x0, x1, x2, x3, own_up, own_down, new_up, new_down,
    y0, y1, y2, y3, hidden_out, slope_out,
    x_ref, y_ref, hidden_ref, slope_ref, up_ref, down_ref, *semaphores,
):
    width = up_ref.shape[2]

    def visit(block, expert, place, head, end):
        x = x_ref[block, place, :]
        total = None
        for part in range(0, width, CHUNK):
            chunk = slice(part, part + CHUNK)
            u = matmul(x, up_ref[expert, :, chunk])
            cube = 0.7978845608028654 * u * (1.0 + 0.044715 * u * u)
            bend = 1.0 + jnp.tanh(cube)
            half = 0.5 * bend
            hidden = (u * half).astype(jnp.bfloat16)
            slope = half + u * (half * (2.0 - bend)) * (
                0.7978845608028654 * (1.0 + 3.0 * 0.044715 * u * u)
            )
            put_rows(hidden_ref.at[:, :, chunk], block, place, hidden, head)
            put_rows(slope_ref.at[:, :, chunk], block, place, slope.astype(jnp.bfloat16), head)
            term = matmul(hidden, down_ref[expert, chunk, :])
            total = term if total is None else total + term
        put_rows(y_ref, block, place, total.astype(jnp.bfloat16), head)

    moe_steps(
        table, up_ref.shape[0], [(x_ref, (x0, x1, x2, x3))],
        ((own_up, own_down), (new_up, new_down), (up_ref, down_ref)),
        [(y_ref, (y0, y1, y2, y3)), (hidden_ref, hidden_out), (slope_ref, slope_out)],
        (x_ref, hidden_ref, slope_ref), visit, semaphores,
    )


def moe_backward_kernel(
    table, d0, d1, d2, d3, slope_in, own_up, own_down, new_up, new_down,
    y0, y1, y2, y3, grad_out,
    d_ref, slope_ref, y_ref, grad_ref, up_ref, down_ref, *semaphores,
):
    width = up_ref.shape[2]

    def visit(block, expert, place, head, end):
        upstream = within(d_ref[block, place, :], head, end)
        total = None
        for part in range(0, width, CHUNK):
            chunk = slice(part, part + CHUNK)
            slope = slope_ref[block, place, chunk].astype(jnp.float32)
            grad = matmul(upstream, down_ref[expert, chunk, :], ((1,), (1,))) * slope
            grad = grad.astype(jnp.bfloat16)
            put_rows(grad_ref.at[:, :, chunk], block, place, grad, head)
            term = matmul(grad, up_ref[expert, :, chunk], ((1,), (1,)))
            total = term if total is None else total + term
        put_rows(y_ref, block, place, total.astype(jnp.bfloat16), head)

    moe_steps(
        table, up_ref.shape[0], [(d_ref, (d0, d1, d2, d3)), (slope_ref, slope_in)],
        ((own_up, own_down), (new_up, new_down), (up_ref, down_ref)),
        [(y_ref, (y0, y1, y2, y3)), (grad_ref, grad_out)],
        (d_ref, grad_ref), visit, semaphores,
    )


def moe_weights_kernel(
    table, a0, a1, a2, a3, b_in, token_in, out_ref, token_ref, a_ref, b_ref, sum_ref, semaphores
):
    expert = pl.program_id(0)
    experts = pl.num_programs(0)
    count = a0.shape[0]

    @pl.when(expert == 0)
    def _():
        token_ref[...] = jnp.zeros_like(token_ref)
        a_ref[:, count:, :] = jnp.zeros((4, TILE, a_ref.shape[2]), jnp.bfloat16)
        copies(
            [(a, a_ref.at[b, :count]) for b, a in enumerate((a0, a1, a2, a3))] + [(b_in, b_ref)],
            semaphores,
        )

    sum_ref[...] = jnp.zeros_like(sum_ref)

    def of_block(block, carry):
        def visit(place, head, end):
            rows = within(a_ref[block, place, :], head, end)
            sum_ref[...] += matmul(rows, b_ref[block, place, :], ((0,), (0,)))

        each_tile(table, block, expert, experts, visit)
        return carry

    lax.fori_loop(0, 4, of_block, 0)
    out_ref[0] = sum_ref[...].astype(jnp.bfloat16)


def moe_call(kernel, name, table, arrays, grid, specs, outs, scratch, semaphores, cost):
    return pl.pallas_call(
        kernel,
        grid_spec=pltpu.PrefetchScalarGridSpec(
            num_scalar_prefetch=1,
            grid=(grid,),
            in_specs=[HBM] * len(arrays),
            out_specs=specs,
            scratch_shapes=[
                *[pltpu.VMEM(*shape) for shape in scratch],
                *[pltpu.SemaphoreType.DMA(shape) for shape in semaphores],
            ],
        ),
        out_shape=[jax.ShapeDtypeStruct(shape, jnp.bfloat16) for shape in outs],
        compiler_params=pltpu.CompilerParams(vmem_limit_bytes=58 << 20),
        cost_estimate=pl.CostEstimate(flops=cost, transcendentals=0, bytes_accessed=40 << 20),
        name=name,
    )(table, *arrays)


def moe_forward(table, x, own, new):
    count, width = x[0].shape
    experts, _, hidden = own[0].shape
    low = jnp.bfloat16
    wide, tall = ((4, count + TILE, width), low), ((4, count + TILE, hidden), low)
    *y, hid, slope = moe_call(
        moe_forward_kernel, "moe_forward", table, [*x, *own, *new], 4, [HBM] * 6,
        [(count, width)] * 4 + [tall[0], tall[0]],
        [wide, wide, tall, tall, (own[0].shape, low), (own[1].shape, low)],
        [(1, 4), (3, 4), (2, experts)], 20 * count * width * hidden,
    )
    return (y, hid, slope)


def moe_backward(table, d, slope, own, new):
    count, width = d[0].shape
    experts, _, hidden = own[0].shape
    low = jnp.bfloat16
    wide, tall = ((4, count + TILE, width), low), ((4, count + TILE, hidden), low)
    *y, grad = moe_call(
        moe_backward_kernel, "moe_backward", table, [*d, slope, *own, *new], 4, [HBM] * 5,
        [(count, width)] * 4 + [tall[0]],
        [wide, tall, wide, tall, (own[0].shape, low), (own[1].shape, low)],
        [(2, 4), (2, 4), (2, experts)], 20 * count * width * hidden,
    )
    return (y, grad)


def moe_weights(table, blocks, tall, token, experts):
    count, width = blocks[0].shape
    hidden = tall.shape[2]
    return moe_call(
        moe_weights_kernel, "moe_weights", table, [*blocks, tall, token], experts,
        [
            pl.BlockSpec((1, width, hidden), lambda e, t: (e, 0, 0)),
            pl.BlockSpec(TOKEN, lambda e, t: (0, 0)),
        ],
        [(experts, width, hidden), TOKEN],
        [((4, count + TILE, width), jnp.bfloat16), (tall.shape, jnp.bfloat16),
         ((width, hidden), jnp.float32)],
        [(5,)], 10 * count * width * hidden,
    )


def at_home():
    return lax.axis_index("c") == lax.axis_index("zh")


def swap_roles(value):
    moved = lax.ppermute(value, ("c", "zh"), [(1, 2), (2, 1)])
    return jnp.where(at_home(), value, moved)


def flip(value, axis):
    return lax.ppermute(value, axis, [(0, 1), (1, 0)])


def flip_some(value, home):
    moves = [(0, 1), (1, 0), (6, 7), (7, 6)] if home else [(2, 3), (3, 2), (4, 5), (5, 4)]
    return lax.ppermute(value, ("c", "zh", "zl"), moves)


def tie(*values):
    return lax.optimization_barrier(values)


def gather_blocks(rows):
    across = flip(rows, "zl")
    return [rows, flip(rows, "c"), across, flip(across, "c")]


def far_rows(blocks):
    return (
        flip(blocks[3], "c").astype(jnp.float32) + blocks[2].astype(jnp.float32)
    ).astype(blocks[2].dtype)


def near_rows(blocks):
    return blocks[0].astype(jnp.float32) + flip(blocks[1], "c").astype(jnp.float32)


def scatter_blocks(blocks):
    return near_rows(blocks) + flip(far_rows(blocks), "zl").astype(jnp.float32)


def send_half(value, axis, dimension):
    count = value.shape[dimension] // 2
    side = lax.axis_index(axis)
    kept = lax.dynamic_slice_in_dim(value, side * count, count, dimension)
    sent = lax.dynamic_slice_in_dim(value, (1 - side) * count, count, dimension)
    return [kept, flip(sent, axis)]


def halve(kept, came):
    return (kept.astype(jnp.float32) + came.astype(jnp.float32)).astype(kept.dtype)


def send_home(value, dimension):
    count = value.shape[dimension] // 2
    high = lax.axis_index("zh")
    straight = lax.dynamic_slice_in_dim(value, high * count, count, dimension)
    turned = lax.dynamic_slice_in_dim(value, (1 - high) * count, count, dimension)
    turned = lax.ppermute(turned, ("c", "zh"), [(0, 2), (1, 0), (2, 3), (3, 1)])
    return [straight, lax.ppermute(straight, ("c", "zh"), [(1, 2), (2, 1)]), turned]


def sum_home(straight, moved, turned):
    straight = jnp.where(at_home(), straight, moved)
    return straight.astype(jnp.float32) + turned.astype(jnp.float32)


def piece_of(weight, users):
    flat = weight.reshape(-1, weight.shape[-1])
    part = flat.shape[0] // lax.axis_size(users)
    return lax.dynamic_slice_in_dim(flat, lax.axis_index(users) * part, part, 0)


def share(piece, users, shape):
    return lax.all_gather(piece, users, axis=0, tiled=True).reshape(shape)


def share_small(piece, users, shape):
    for bit in reversed(users):
        given = flip(piece, bit)
        low = lax.axis_index(bit) == 0
        piece = jnp.concatenate([jnp.where(low, piece, given), jnp.where(low, given, piece)], axis=0)
    return piece.reshape(shape)


def body(
    high_bits,
    block_input,
    attention_gain,
    qkv_weight,
    proj_weight,
    moe_gain,
    centroids,
    expert_up,
    expert_down,
    out_grad,
    routes,
    priority,
    segments,
):
    row_count = block_input.shape[1]
    model_width = block_input.shape[2]
    experts = expert_up.shape[0]
    token_count = segments.shape[1]
    capacity = 9 * token_count // (8 * experts)
    users = (*high_bits, "c")
    core, near = lax.axis_index("c"), lax.axis_index("zl")
    ranks = jnp.stack(
        [2 * core + near, 2 * (1 - core) + near, 2 * core + 1 - near, 3 - 2 * core - near]
    )
    home = at_home()
    staying = block_input[0]
    coming = lax.ppermute(staying, ("c", "zh"), [(1, 2), (2, 1)])
    small = jnp.concatenate([qkv_weight, proj_weight.T[None]], axis=0)
    small_piece = flip(piece_of(small, users), "zh")

    def normed(rows):
        return (normalize_plain(rows.astype(jnp.float32))[0] * attention_gain).astype(jnp.bfloat16)

    normed_staying = normed(staying)
    home_across = flip_some(normed_staying, True)
    indices = jnp.stack([routes[0, :, 0], priority[0], segments[0]])
    indices = jnp.where(home, indices, flip(indices, "c"))
    segment = indices[2]
    ranges, start = key_ranges(segment, FORWARD_BLOCKS)
    coming, small_piece, home_across, ranges, start = tie(
        coming, small_piece, home_across, ranges, start
    )
    small_other = share(small_piece, users, small.shape)
    normed_coming = normed(coming)
    away_across = flip_some(normed_coming, False)
    across = jnp.where(home, home_across, away_across)
    across, up_piece, down_piece = tie(
        across, piece_of(expert_up, users), piece_of(expert_down, users)
    )
    up_piece, down_piece = flip(up_piece, "zh"), flip(down_piece, "zh")
    normed_one = jnp.where(home, normed_staying, normed_coming)
    normed_one = [normed_one, flip(normed_one, "c"), across, flip(across, "c")]
    inputs = jnp.where(home, staying, coming).astype(jnp.float32)
    unit_one, inverse_one = normalize_plain(inputs)
    small = jnp.where(home, small, small_other)
    *attended, qt, k, kt, v, ctx, lse = attention_forward(
        ranges, start, ranks, normed_one, small
    )
    saved = (qt, k, kt, v, ctx, lse)
    attended[3], up_piece, down_piece, indices = tie(
        attended[3], up_piece, down_piece, indices
    )
    new_experts = [share(piece, users, expert_up.shape) for piece in (up_piece, down_piece)]
    back_ranges = key_ranges(indices[2], BACKWARD_BLOCKS)[0]
    kept_rows, order, table, hot_rows = route_rows(
        indices[0], indices[1], experts, capacity, row_count, ranks
    )
    own_experts = (expert_up, expert_down)
    far, back_ranges, order, table, kept_rows, upstream = tie(
        flip(far_rows(attended), "zl"), back_ranges, order, table, kept_rows, out_grad[0]
    )
    away_upstream = lax.ppermute(upstream, ("c", "zh"), [(1, 2), (2, 1)])
    upstream = jnp.where(home, upstream, away_upstream).astype(jnp.float32)
    attended = near_rows(attended) + far.astype(jnp.float32)
    mixed_one = inputs + attended
    unit_two, inverse_two = normalize_plain(mixed_one)
    normed_two_rows = (unit_two * moe_gain).astype(jnp.bfloat16)
    centroid_rows = jnp.dot(
        hot_rows.astype(jnp.bfloat16), centroids, preferred_element_type=jnp.float32
    )
    normed_two_float = normed_two_rows.astype(jnp.float32)
    gate_prob = jax.nn.sigmoid(jnp.sum(normed_two_float * centroid_rows, axis=-1))
    gate_used = jnp.where(kept_rows, gate_prob, 0.0)
    grad_eo_rows = (gate_used[:, None] * upstream).astype(jnp.bfloat16)
    sorted_rows = sort_rows(order, normed_two_rows)
    beside, across = flip(sorted_rows, "c"), flip(sorted_rows, "zl")
    across, grad_sorted = tie(across, sort_rows(order, grad_eo_rows))
    grad_beside, grad_across = flip(grad_sorted, "c"), flip(grad_sorted, "zl")
    dispatched = [sorted_rows, beside, across, flip(across, "c")]
    returned, hidden, slope = moe_forward(table, dispatched, own_experts, new_experts)
    grad_across, *returned = tie(grad_across, *returned)
    returned_far, grad_corner = tie(far_rows(returned), flip(grad_across, "c"))
    grad_dispatched = [grad_sorted, grad_beside, grad_across, grad_corner]
    returned_far = flip(returned_far, "zl")
    returned_near = near_rows(returned)
    back_moe, grad_upward = moe_backward(table, grad_dispatched, slope, own_experts, new_experts)
    returned_far, back_moe[3] = tie(returned_far, back_moe[3])
    back_far, hidden = tie(far_rows(back_moe), hidden)
    back_far = flip(back_far, "zl")
    back_near = near_rows(back_moe)
    down_part, token = moe_weights(table, grad_dispatched, hidden, back_moe[3], experts)
    back_far, token = tie(back_far, token)
    expert_out = unsort_rows(order, returned_near + returned_far.astype(jnp.float32))
    mixed_two = (mixed_one + gate_used[:, None] * expert_out).astype(jnp.bfloat16)
    grad_gate = jnp.where(kept_rows, jnp.sum(upstream * expert_out, axis=-1), 0.0)
    grad_score = grad_gate * gate_prob * (1.0 - gate_prob)
    down_rest = lax.psum_scatter(down_part, high_bits, scatter_dimension=1, tiled=True)
    back_moe = back_near + back_far.astype(jnp.float32)
    grad_two = unsort_rows(order, back_moe) + grad_score[:, None] * centroid_rows
    centroid_part = jnp.einsum(
        "te,td->ed",
        hot_rows.astype(jnp.float32),
        grad_score[:, None] * normed_two_float,
        precision=highest,
    )
    moe_gain_part = jnp.sum(grad_two * unit_two, axis=0)
    grad_mixed = upstream + normalize_back(grad_two, unit_two, inverse_two, moe_gain)
    grad_mixed, grad_upward = tie(grad_mixed, grad_upward)
    up_part, _ = moe_weights(table, dispatched, grad_upward, token, experts)
    grad_att = gather_blocks(grad_mixed.astype(jnp.bfloat16))
    early = jnp.concatenate([moe_gain_part[None], centroid_part], axis=0)
    everyone = (*users, "zh", "zl")
    early = jnp.swapaxes(early.reshape(experts + 1, lax.axis_size(everyone), -1), 0, 1)
    early = jnp.sum(lax.all_to_all(early, everyone, 0, 0, tiled=True), axis=0)
    grad_att[2], early, up_part = tie(grad_att[2], early, up_part)
    grad_att[3] = flip(grad_att[2], "c")
    up_rest = lax.psum_scatter(up_part, high_bits, scatter_dimension=1, tiled=True)
    down_rest, mixed_two, grad_att[3] = tie(down_rest, mixed_two, grad_att[3])
    down_home = send_home(down_rest, 1)
    away_output = lax.ppermute(mixed_two, ("c", "zh"), [(1, 2), (2, 1)])
    *grad_one, weights_part = attention_backward(
        back_ranges, start, ranks, grad_att, normed_one, saved, small
    )
    grad_one[3], away_output, *down_home = tie(grad_one[3], away_output, *down_home)
    one_far = far_rows(grad_one)
    one_near = near_rows(grad_one)

    def finish(far):
        grad = normalize_back(
            one_near + far.astype(jnp.float32), unit_one, inverse_one, attention_gain
        )
        return (grad_mixed + grad).astype(jnp.bfloat16)

    going = flip_some(one_far, False)
    weights_part = lax.psum_scatter(weights_part, high_bits, scatter_dimension=1, tiled=True)
    up_home = send_home(up_rest, 1)
    going, one_far, weights_part, up_home[0], up_home[1] = tie(
        going, one_far, weights_part, up_home[0], up_home[1]
    )
    going, one_far, weights_part, away_output, *homes = tie(
        finish(going), one_far, weights_part, away_output, *down_home, *up_home
    )
    down_home, up_home = homes[:3], homes[3:]
    block_output = jnp.where(home, mixed_two, away_output)[None]
    going = lax.ppermute(going, ("c", "zh"), [(1, 2), (2, 1)])
    kept_far = flip_some(one_far, True)
    down_summed = jnp.swapaxes(sum_home(*down_home), 1, 2)
    up_summed = sum_home(*up_home)
    weights_part = sum_home(*send_home(weights_part, 1))
    qkv_summed, proj_summed = weights_part[:3], weights_part[3].T
    gain_two_sum, centroid_sum = early[0], early[1:]
    entries = gain_two_sum.shape[0]
    own_entries = lax.axis_index(everyone) * entries
    slice_rows = qkv_summed.shape[1]
    own_rows = lax.dynamic_slice_in_dim(
        qkv_weight, lax.axis_index(users) * slice_rows, slice_rows, 1
    )
    gain_one = jnp.sum(own_rows.astype(jnp.float32) * qkv_summed, axis=(0, 2))
    gain_one, kept_rows = tie(gain_one, finish(kept_far))
    input_grad = jnp.where(home, kept_rows, going)[None]
    for bit in ("zh", "zl"):
        gain_one = halve(*send_half(gain_one, bit, 0))
    gain_one_sum = gain_one / lax.dynamic_slice_in_dim(attention_gain, own_entries, entries, 0)
    return (
        block_output,
        input_grad,
        gain_one_sum,
        gain_two_sum,
        centroid_sum,
        qkv_summed,
        proj_summed,
        up_summed,
        down_summed,
    )


def solution(mesh):
    shape = mesh.devices.shape
    high_bits = tuple(f"u{place}" for place in range((shape[0] // 2).bit_length() - 1))
    dp, tensor = (*high_bits, "c"), ("zh", "zl")
    mesh = Mesh(mesh.devices.reshape((2,) * len(dp + tensor)), dp + tensor)

    def program(*arguments):
        return body(high_bits, *arguments)

    return jax.shard_map(
        program,
        mesh=mesh,
        in_specs=(
            P(dp, tensor, None),
            P(),
            P(None, None, tensor),
            P(tensor, None),
            P(),
            P(),
            P(None, None, tensor),
            P(None, tensor, None),
            P(dp, tensor, None),
            P(dp, None, None),
            P(dp, None),
            P(dp, None),
        ),
        out_specs=(
            P(dp, tensor, None),
            P(dp, tensor, None),
            P(dp + tensor),
            P(dp + tensor),
            P(None, dp + tensor),
            P(None, dp, tensor),
            P(tensor, dp),
            P(None, dp, tensor),
            P(None, tensor, dp),
        ),
        check_vma=False,
    )
```
